32 devices in a mesh: dom: 8 (over y, x, core), spec: 4 (over z).
Axes of the slice: x: 2, y: 2, z: 4, core: 2. Of those that a mesh axis runs over, the one named last changes fastest.
Arguments:
- spectrum: float32 [1296, 8192], P('spec', 'dom'), may hold values from 0.2 to 2
- normals: float32 [2, 3, 16384], P(None, None, 'dom'), may hold values from -3 to 3, as said below
- conn: int32 [3, 16384], P(None, 'dom'), may hold values from 0 to 1535, as said below
- send_nodes: int32 [8, 4, 128], P('dom'), may hold values from 0 to 1023, as said below
- step_weight: float32 [8192], P('dom'), may hold values from 0.02 to 0.06
- group_speed: float32 [36], replicated, may hold values from 0.25 to 1
- dia_plus: int32 [1296], replicated, may hold values from 0 to 1295, as said below
- dia_minus: int32 [1296], replicated, may hold values from 0 to 1295, as said below
- dia_coeff: float32 [1296], replicated, may hold values from 0.01 to 0.04
Outputs:
- spectrum_out: float32 [1296, 8192], P(None, ('dom', 'spec'))
The draws below stay inside these ranges and needn't reach their ends.
Inputs may be any that keep to these rules, and one draw needn't show every extreme that they name: `conn`: for partition i, an entry below 1024 names an owned node; an entry 1024 + m * 128 + s names slot s of ghost block m, from partition i + g (g as in the reference program); only blocks of partitions that exist are named, and each block only in a leading run of its slots. `send_nodes`: each row lists distinct owned nodes of the sending partition. `dia_plus`: for bin f * 36 + d the partner has frequency min(f + 1 or f + 2, 35) and a direction 1 to 3 steps higher, modulo 36. `dia_minus`: for bin f * 36 + d the partner has frequency max(f - 1 or f - 2, 0) and a direction 1 to 3 steps lower, modulo 36. `normals`: for each triangle the three vectors sum to zero and no two are parallel.
All inputs are finite; a program needn't handle non-finite values.
Results may differ from the reference program's by a relative error of at most 0.00002.
Values sent between devices are 32-bit elements; how exact they have to be, the bound alone decides.
No kernel may reach another device: no remote copies, remote signals or barrier semaphores. Data moves between devices by JAX's collectives and lax.ppermute only.
A program may use at most 64 MiB of HBM per device.

```python
import math
import jax
import jax.numpy as jnp
from jax import lax

NDIR = 36
NFREQ = 36
NODE_DEV = 1024
SLOT = 128
REACH = 2
STEPS = 2
BINS = 1296
ELEM_DEV = 2048
PARTITIONS = 8
NODES = 8192
ELEMENTS = 16384
N_DOM = 8


def draw_conn(key, part):
    blocks = 2 * REACH
    local_total = NODE_DEV + blocks * SLOT
    first_key, second_key = jax.random.split(jax.random.fold_in(key, 11))
    counts = jax.random.randint(first_key, (PARTITIONS, blocks), SLOT // 2, SLOT + 1)
    counts = counts.at[1, blocks - 1].set(SLOT)
    raw_index = jax.random.randint(second_key, (3, PARTITIONS, ELEM_DEV), 0, local_total)
    ghost_index = raw_index - NODE_DEV
    block_index = jnp.clip(ghost_index // SLOT, 0, blocks - 1)
    slot_index = ghost_index % SLOT
    offset = jnp.where(block_index < REACH, block_index - REACH, block_index - REACH + 1)
    part_of = jnp.arange(PARTITIONS, dtype=jnp.int32)[None, :, None]
    sender = part_of + offset
    limit = counts[jnp.broadcast_to(part_of, block_index.shape), block_index]
    usable = (sender >= 0) & (sender < PARTITIONS) & (slot_index < limit)
    local_index = jnp.where(ghost_index < 0, raw_index, jnp.where(usable, raw_index, raw_index % NODE_DEV))
    local_index = local_index.at[0, 0, 0].set(0)
    local_index = local_index.at[0, 1, 0].set(local_total - 1)
    return local_index.reshape(3, PARTITIONS * ELEM_DEV).astype(jnp.int32)


def draw_send_nodes(key, part):
    blocks = 2 * REACH
    keys = jax.random.split(jax.random.fold_in(key, 12), PARTITIONS * blocks)
    chosen = jax.vmap(lambda one_key: jax.random.permutation(one_key, NODE_DEV)[:SLOT])(keys)
    return chosen.reshape(PARTITIONS, blocks, SLOT).astype(jnp.int32)


def partner_bins(key, salt, upward):
    bins = jnp.arange(BINS, dtype=jnp.int32)
    freq = bins // NDIR
    direc = bins % NDIR
    freq_key, dir_key = jax.random.split(jax.random.fold_in(key, salt))
    freq_step = jax.random.randint(freq_key, (BINS,), 1, 3)
    dir_step = jax.random.randint(dir_key, (BINS,), 1, 4)
    if upward:
        new_freq = jnp.minimum(freq + freq_step, NFREQ - 1)
        new_dir = (direc + dir_step) % NDIR
    else:
        new_freq = jnp.maximum(freq - freq_step, 0)
        new_dir = (direc - dir_step) % NDIR
    return (new_freq * NDIR + new_dir).astype(jnp.int32)


def draw_dia_plus(key, part):
    return partner_bins(key, 13, True)


def draw_dia_minus(key, part):
    return partner_bins(key, 14, False)


def draw_normals(key, part):
    keys = jax.random.split(jax.random.fold_in(key, 15), 3)
    rotation = jax.random.uniform(keys[0], (ELEMENTS,), jnp.float32, -math.pi, math.pi)
    uniform_draw = jax.random.uniform(keys[1], (ELEMENTS,), jnp.float32)
    length = jnp.exp(math.log(0.5) + (math.log(2.0) - math.log(0.5)) * uniform_draw)
    jitter = jax.random.uniform(keys[2], (2, 2, ELEMENTS), jnp.float32, -0.1, 0.1)
    angles = rotation[None, :] + 2.0 * math.pi / 3.0 * jnp.arange(2, dtype=jnp.float32)[:, None]
    first_two = jnp.stack([jnp.cos(angles), jnp.sin(angles)]) + jitter
    third = -(first_two[:, 0] + first_two[:, 1])
    whole = jnp.concatenate([first_two, third[:, None, :]], axis=1)
    return (whole * length[None, None, :]).astype(jnp.float32)


def levels(stream_key, dims, shards, least, high):
    gain, own = 1.0, jax.random.fold_in(stream_key, 6)
    for position, parts in shards:
        heights = jnp.exp(jax.random.uniform(jax.random.fold_in(own, position), (parts,), jnp.float32, least / len(shards), high / len(shards)))
        gain = gain * jnp.repeat(heights, dims[position] // parts).reshape([-1 if axis == position else 1 for axis in range(len(dims))])
    return gain


def setup_inputs(seed: int = 0) -> dict:
    key_list = jax.random.split(jax.random.key(seed), 10)
    spectrum = jnp.clip(jnp.exp(math.log(2.0) - 2.3025851 * jax.random.uniform(key_list[0], (BINS, NODES), jnp.float32) ** levels(key_list[0], (BINS, NODES), ((0, 4), (1, 8)), -0.2, 0.2)), 0.2, 2.0)
    normals = draw_normals(jax.random.fold_in(key_list[9], 71), 0)
    conn = draw_conn(jax.random.fold_in(key_list[9], 71), 0)
    send_nodes = draw_send_nodes(jax.random.fold_in(key_list[9], 71), 0)
    step_weight = jnp.clip(0.02 + 0.04 * jax.random.uniform(key_list[4], (NODES,), jnp.float32) ** levels(key_list[4], (NODES,), ((0, 8),), -0.2, 0.2), 0.02, 0.06)
    group_speed = jnp.clip(jnp.exp(jax.random.uniform(key_list[5], (NFREQ,), jnp.float32, math.log(0.25), math.log(1.0))), 0.25, 1.0)
    dia_plus = draw_dia_plus(jax.random.fold_in(key_list[9], 71), 0)
    dia_minus = draw_dia_minus(jax.random.fold_in(key_list[9], 71), 0)
    dia_coeff = jnp.clip(jnp.exp(jax.random.uniform(key_list[8], (BINS,), jnp.float32, math.log(0.01), math.log(0.04))), 0.01, 0.04)
    return {"spectrum": spectrum, "normals": normals, "conn": conn, "send_nodes": send_nodes, "step_weight": step_weight, "group_speed": group_speed, "dia_plus": dia_plus, "dia_minus": dia_minus, "dia_coeff": dia_coeff}


weight_plus = 1.25 ** -4
weight_minus = 0.75 ** -4
weight_both = 0.9375 ** -4


def global_corners(conn, send_nodes):
    part_of = (jnp.arange(ELEMENTS, dtype=jnp.int32) // ELEM_DEV)[None, :]
    ghost_index = conn - NODE_DEV
    block_index = jnp.clip(ghost_index // SLOT, 0, 2 * REACH - 1)
    slot_index = ghost_index % SLOT
    offset = jnp.where(block_index < REACH, block_index - REACH, block_index - REACH + 1)
    sender = jnp.clip(part_of + offset, 0, N_DOM - 1)
    row_index = 2 * REACH - 1 - block_index
    remote = sender * NODE_DEV + send_nodes[sender, row_index, slot_index]
    return jnp.where(ghost_index < 0, part_of * NODE_DEV + conn, remote).astype(jnp.int32)


def residual_of(energy, corners, normals, speed_east, speed_north, node_count):
    coeffs = [speed_east[:, None] * normals[0, vertex][None, :] + speed_north[:, None] * normals[1, vertex][None, :] for vertex in range(3)]
    outward = [jnp.maximum(item, 0.0) for item in coeffs]
    inward = [jnp.minimum(item, 0.0) for item in coeffs]
    denom = inward[0] + inward[1] + inward[2]
    values = [jnp.take(energy, corners[vertex], axis=1) for vertex in range(3)]
    inflow = (inward[0] * values[0] + inward[1] * values[1] + inward[2] * values[2]) / denom
    totals = jnp.zeros((energy.shape[0], node_count), jnp.float32)
    for vertex in range(3):
        totals = totals.at[:, corners[vertex]].add(outward[vertex] * (values[vertex] - inflow))
    return totals


def interact(energy, dia_plus, dia_minus, dia_coeff):
    upper = jnp.take(energy, dia_plus, axis=0)
    lower = jnp.take(energy, dia_minus, axis=0)
    term = dia_coeff[:, None] * (energy * energy * (weight_plus * upper + weight_minus * lower) - 2.0 * weight_both * energy * upper * lower)
    change = (-2.0 * term).at[dia_plus].add(term).at[dia_minus].add(term)
    return energy + change


def reference(spectrum, normals, conn, send_nodes, step_weight, group_speed, dia_plus, dia_minus, dia_coeff):
    corners = global_corners(conn, send_nodes)
    directions = jnp.arange(NDIR, dtype=jnp.int32).astype(jnp.float32) * (2.0 * math.pi / NDIR)

    def one_frequency(inputs):
        freq_index, freq_block = inputs
        speed = group_speed[freq_index]
        speed_east = speed * jnp.cos(directions)
        speed_north = speed * jnp.sin(directions)
        energy = freq_block
        for sweep_index in range(STEPS):
            energy = energy - step_weight[None, :] * residual_of(energy, corners, normals, speed_east, speed_north, NODES)
        return energy

    propagated = lax.map(one_frequency, (jnp.arange(NFREQ, dtype=jnp.int32), spectrum.reshape(NFREQ, NDIR, NODES)))
    by_part = jnp.transpose(propagated.reshape(BINS, N_DOM, NODE_DEV), (1, 0, 2))
    mixed = lax.map(lambda slab: interact(slab, dia_plus, dia_minus, dia_coeff), by_part)
    return jnp.transpose(mixed, (1, 0, 2)).reshape(BINS, NODES)
```

```python
import functools
import math

import jax
import jax.numpy as jnp
from jax import lax
from jax.experimental import pallas as pl
from jax.experimental.pallas import tpu as pltpu
from jax.sharding import PartitionSpec as P

NDIR = 36
REACH = 2
STEPS = 2
BLOCKS = 2 * REACH
LANES = 128
GROUPS = 2

weight_plus = 1.25 ** (-4)
weight_minus = 0.75 ** (-4)
weight_both = 0.9375 ** (-4)

VM = pl.BlockSpec(memory_space=pltpu.VMEM)
SM = pl.BlockSpec(memory_space=pltpu.SMEM)


def offset_of(position):
    return position - REACH if position < REACH else position - REACH + 1


def passed_along(value, axis, steps):
    count = lax.axis_size(axis)
    leading, last = (max(0, -steps), min(count, count - steps))
    return lax.ppermute(value, axis, [(source, source + steps) for source in range(leading, last)])


def chunked(total, limit):
    return max(size for size in range(1, limit + 1) if total % size == 0)


def pack_rows(sub, slots, send, energy, outs):
    unroll = chunked(slots, 16)
    for position in range(BLOCKS):

        @pl.loop(0, slots // unroll)
        def _(k):
            first = k * unroll
            for u in range(unroll):
                row = send[(BLOCKS - 1 - position) * slots + first + u]
                outs[position][pl.ds((first + u) * sub, sub), :] = energy[pl.ds(row, sub), :]


def enter_kernel(sub, lanes, slots, send, spectrum, energy, *outs):
    owned = spectrum.shape[2]

    @pl.loop(0, owned // LANES)
    def _(k):
        for part in range(sub):
            block = spectrum[part, :, pl.ds(pl.multiple_of(k * LANES, LANES), LANES)]
            energy[pl.ds(k * LANES * sub + part, LANES, stride=sub), :] = block.T

    pack_rows(sub, slots, send, energy, outs)


def sweep_kernel(sub, shared, slots, conn, energy, coef, weight, *rest):
    ghosts, rest = rest[:BLOCKS], rest[BLOCKS:]
    partial, returned, rest = rest[0], rest[1 : 1 + BLOCKS], rest[1 + BLOCKS :]
    full, sums = rest[0], rest[1:]
    own_rows = energy.shape[0]
    ghost_rows = slots * sub
    rows = full.shape[0]
    elements = conn.shape[0] // 3
    step = chunked(rows, 64)
    zero = jnp.zeros((step, LANES), jnp.float32)

    @pl.loop(0, rows // step)
    def _(k):
        for item in sums:
            item[pl.ds(pl.multiple_of(k * step, step), step), :] = zero

    full[:own_rows, :] = energy[...]
    for position in range(BLOCKS):
        first = own_rows + position * ghost_rows
        full[first : first + ghost_rows, :] = ghosts[position][...]

    share = elements // GROUPS
    unroll = chunked(share, 16)

    def coef_rows(which, element):
        if shared:
            return coef[pl.ds(which * elements + element, sub, stride=0), :]
        return coef[pl.ds((which * elements + element) * sub, sub), :]

    @pl.loop(0, share // unroll)
    def _(k):
        for u in range(unroll):
            for group in range(GROUPS):
                element = group * share + k * unroll + u
                index = [conn[corner * elements + element] for corner in range(3)]
                value = [full[pl.ds(row, sub), :] for row in index]
                inflow = coef_rows(3, element) * value[0]
                inflow = inflow + coef_rows(4, element) * value[1]
                inflow = inflow + coef_rows(5, element) * value[2]
                for corner in range(3):
                    part = coef_rows(corner, element) * (value[corner] - inflow)
                    item = sums[group * 3 + corner]
                    item[pl.ds(index[corner], sub), :] = item[pl.ds(index[corner], sub), :] + part

    def total(at):
        result = sums[0][at, :]
        for item in sums[1:]:
            result = result + item[at, :]
        return result

    own_step = chunked(own_rows, 64)

    @pl.loop(0, own_rows // own_step)
    def _(k):
        at = pl.ds(pl.multiple_of(k * own_step, own_step), own_step)
        partial[at, :] = energy[at, :] - weight[at, :] * total(at)

    ghost_step = chunked(ghost_rows, 64)
    for position in range(BLOCKS):

        @pl.loop(0, ghost_rows // ghost_step)
        def _(k):
            at = pl.multiple_of(k * ghost_step, ghost_step)
            source = pl.ds(own_rows + position * ghost_rows + at, ghost_step)
            returned[position][pl.ds(at, ghost_step), :] = total(source)


def add_returned(sub, slots, send, weight, incoming, energy):
    unroll = chunked(slots, 16)
    for position in range(BLOCKS):

        @pl.loop(0, slots // unroll)
        def _(k):
            first = k * unroll
            rows = [send[(BLOCKS - 1 - position) * slots + first + u] for u in range(unroll)]
            fresh = [
                energy[pl.ds(row, sub), :]
                - weight[pl.ds(row, sub), :] * incoming[position][pl.ds((first + u) * sub, sub), :]
                for u, row in enumerate(rows)
            ]
            for row, item in zip(rows, fresh):
                energy[pl.ds(row, sub), :] = item


def between_kernel(sub, slots, send, partial, weight, *rest):
    incoming, energy, outs = rest[:BLOCKS], rest[BLOCKS], rest[BLOCKS + 1 :]
    energy[...] = partial[...]
    add_returned(sub, slots, send, weight, incoming, energy)
    pack_rows(sub, slots, send, energy, outs)


def leave_kernel(sub, lanes, slots, halves, send, partial, weight, *rest):
    incoming, out, energy = rest[:BLOCKS], rest[BLOCKS], rest[BLOCKS + 1]
    energy[...] = partial[...]
    add_returned(sub, slots, send, weight, incoming, energy)
    owned = energy.shape[0] // sub
    per_target = sub * lanes * halves
    for block in range(owned // LANES):
        target, half = divmod(block, halves)
        for part in range(sub):
            tile = energy[pl.ds(block * LANES * sub + part, LANES, stride=sub), :].T
            first = target * per_target + part * lanes * halves + half
            out[pl.ds(first, lanes, stride=halves), :] = tile[:lanes]


def interact_kernel(halves, plus, minus, rate, energy, out, *sums):
    bins = plus.shape[0]
    rows = energy.shape[0]
    step = chunked(rows, 64)
    zero = jnp.zeros((step, LANES), jnp.float32)

    @pl.loop(0, rows // step)
    def _(k):
        for item in sums[1:]:
            item[pl.ds(pl.multiple_of(k * step, step), step), :] = zero

    share = bins // GROUPS
    unroll = chunked(share, 12)

    @pl.loop(0, share // unroll)
    def _(k):
        for u in range(unroll):
            for group in range(GROUPS):
                index = group * share + k * unroll + u
                up, down = plus[index], minus[index]
                own = energy[pl.ds(index * halves, halves), :]
                upper = energy[pl.ds(up, halves), :]
                lower = energy[pl.ds(down, halves), :]
                term = rate[index] * (
                    own * own * (weight_plus * upper + weight_minus * lower)
                    - 2.0 * weight_both * own * upper * lower
                )
                sums[0][pl.ds(index * halves, halves), :] = own - 2.0 * term
                high, low = sums[1 + 2 * group], sums[2 + 2 * group]
                high[pl.ds(up, halves), :] = high[pl.ds(up, halves), :] + term
                low[pl.ds(down, halves), :] = low[pl.ds(down, halves), :] + term

    step = chunked(bins, 48)

    @pl.loop(0, bins // step)
    def _(k):
        for half in range(halves):
            at = pl.ds(k * step * halves + half, step, stride=halves)
            result = sums[0][at, :]
            for item in sums[1:]:
                result = result + item[at, :]
            out[pl.ds(pl.multiple_of(k * step, step), step), half * LANES : (half + 1) * LANES] = result


def shape_of(*dims):
    return jax.ShapeDtypeStruct(dims, jnp.float32)


def cost(flops, moved):
    return pl.CostEstimate(flops=flops, bytes_accessed=moved, transcendentals=0)


def on_device(
    spectrum, normals, conn, send_nodes, step_weight, group_speed, dia_plus, dia_minus, dia_coeff
):
    row_count, owned = spectrum.shape
    slots = send_nodes.shape[2]
    elements = conn.shape[1]
    bins = dia_plus.shape[0]
    spec_count = lax.axis_size("spec")
    sub = -(-row_count // LANES)
    while row_count % sub:
        sub += 1
    lanes = row_count // sub
    shared = lanes % NDIR == 0
    own_rows = owned * sub
    ghost_rows = slots * sub
    rows = own_rows + BLOCKS * ghost_rows
    halves = owned // (spec_count * LANES)

    send = (send_nodes[0] * sub).reshape(-1)
    nodes = (conn * sub).reshape(-1)

    bin_of = (
        lax.axis_index("spec") * row_count
        + jnp.arange(sub, dtype=jnp.int32)[:, None] * lanes
        + jnp.arange(LANES, dtype=jnp.int32)[None, :]
    )
    angle = (bin_of % NDIR).astype(jnp.float32) * (2.0 * math.pi / NDIR)
    east, north = jnp.cos(angle), jnp.sin(angle)
    select = ((bin_of // NDIR)[:, :, None] == jnp.arange(group_speed.shape[0], dtype=jnp.int32)).astype(jnp.float32)
    speed = jnp.sum(select * group_speed, axis=2)
    if shared:
        east, north = east[:1], north[:1]
    slope = normals[0][:, :, None, None] * east + normals[1][:, :, None, None] * north
    inward = jnp.minimum(slope, 0.0)
    share = inward / jnp.sum(inward, axis=0)
    coef = jnp.concatenate([jnp.maximum(slope, 0.0), share]).reshape(-1, LANES)
    weight = (step_weight[:, None, None] * speed).reshape(own_rows, LANES)

    padded = jnp.pad(spectrum.reshape(sub, lanes, owned), ((0, 0), (0, LANES - lanes), (0, 0)))
    block_shapes = [shape_of(ghost_rows, LANES)] * BLOCKS
    energy, *outs = pl.pallas_call(
        functools.partial(enter_kernel, sub, lanes, slots),
        out_shape=[shape_of(own_rows, LANES)] + block_shapes,
        in_specs=[SM, VM],
        out_specs=[VM] * (1 + BLOCKS),
        cost_estimate=cost(0, 8 * own_rows * LANES),
        name="enter",
    )(send, padded)

    for sweep_index in range(STEPS):
        ghosts = [passed_along(outs[p], "dom", -offset_of(p)) for p in range(BLOCKS)]
        partial, *returned = pl.pallas_call(
            functools.partial(sweep_kernel, sub, shared, slots),
            out_shape=[shape_of(own_rows, LANES)] + block_shapes,
            in_specs=[SM] + [VM] * (3 + BLOCKS),
            out_specs=[VM] * (1 + BLOCKS),
            scratch_shapes=[pltpu.VMEM((rows, LANES), jnp.float32)] * (1 + 3 * GROUPS),
            cost_estimate=cost(elements * 24 * row_count, 4 * LANES * (8 * elements + 4 * rows)),
            name="sweep",
        )(nodes, energy, coef, weight, *ghosts)
        incoming = [passed_along(returned[p], "dom", offset_of(p)) for p in range(BLOCKS)]
        if sweep_index < STEPS - 1:
            energy, *outs = pl.pallas_call(
                functools.partial(between_kernel, sub, slots),
                out_shape=[shape_of(own_rows, LANES)] + block_shapes,
                in_specs=[SM] + [VM] * (2 + BLOCKS),
                out_specs=[VM] * (1 + BLOCKS),
                cost_estimate=cost(2 * owned * row_count, 16 * own_rows * LANES),
                name="between",
            )(send, partial, weight, *incoming)

    leaving = pl.pallas_call(
        functools.partial(leave_kernel, sub, lanes, slots, halves),
        out_shape=shape_of(spec_count * row_count * halves, LANES),
        in_specs=[SM] + [VM] * (2 + BLOCKS),
        out_specs=VM,
        scratch_shapes=[pltpu.VMEM((own_rows, LANES), jnp.float32)],
        cost_estimate=cost(2 * owned * row_count, 16 * own_rows * LANES),
        name="leave",
    )(send, partial, weight, *incoming)
    arrived = lax.all_to_all(
        leaving.reshape(spec_count, row_count * halves, LANES), "spec", split_axis=0, concat_axis=0
    )
    return pl.pallas_call(
        functools.partial(interact_kernel, halves),
        out_shape=shape_of(bins, halves * LANES),
        in_specs=[SM] * 3 + [VM],
        out_specs=VM,
        scratch_shapes=[pltpu.VMEM((bins * halves, LANES), jnp.float32)] * (1 + 2 * GROUPS),
        cost_estimate=cost(16 * bins * halves * LANES, 8 * bins * halves * LANES),
        name="interact",
    )(dia_plus * halves, dia_minus * halves, dia_coeff, arrived.reshape(bins * halves, LANES))


def solution(mesh):
    in_specs = (
        P("spec", "dom"),
        P(None, None, "dom"),
        P(None, "dom"),
        P("dom", None, None),
        P("dom"),
        P(),
        P(),
        P(),
        P(),
    )
    out_specs = P(None, ("dom", "spec"))
    return jax.shard_map(
        on_device, mesh=mesh, in_specs=in_specs, out_specs=out_specs, check_vma=False
    )
```

```python
import functools
import math

import jax
import jax.numpy as jnp
from jax import lax
from jax.experimental import pallas as pl
from jax.experimental.pallas import tpu as pltpu
from jax.sharding import PartitionSpec as P

NDIR = 36
REACH = 2
STEPS = 2
BLOCKS = 2 * REACH
LANES = 128
GROUPS = 2

weight_plus = 1.25 ** (-4)
weight_minus = 0.75 ** (-4)
weight_both = 0.9375 ** (-4)

VM = pl.BlockSpec(memory_space=pltpu.VMEM)
SM = pl.BlockSpec(memory_space=pltpu.SMEM)


def offset_of(position):
    return position - REACH if position < REACH else position - REACH + 1


def passed_along(value, axis, steps):
    count = lax.axis_size(axis)
    leading, last = (max(0, -steps), min(count, count - steps))
    return lax.ppermute(value, axis, [(source, source + steps) for source in range(leading, last)])


def chunked(total, limit):
    return max(size for size in range(1, limit + 1) if total % size == 0)


def pack_rows(sub, slots, send, energy, outs):
    unroll = chunked(slots, 16)
    for position in range(BLOCKS):

        @pl.loop(0, slots // unroll)
        def _(k):
            first = k * unroll
            listed = send.at[pl.ds((BLOCKS - 1 - position) * slots + first, unroll)]
            for u in range(unroll):
                outs[position][pl.ds((first + u) * sub, sub), :] = energy[pl.ds(listed[u], sub), :]


def enter_kernel(sub, lanes, slots, send, spectrum, energy, *rest):
    outs, square = rest[:BLOCKS], rest[BLOCKS]
    owned = spectrum.shape[1]
    square[...] = jnp.zeros_like(square)
    for block in range(owned // LANES):
        for part in range(sub):
            slot = square.at[(block * sub + part) % square.shape[0]]
            slot[:lanes, :] = spectrum[part * lanes : (part + 1) * lanes, block * LANES : (block + 1) * LANES]
            energy[pl.ds(block * LANES * sub + part, LANES, stride=sub), :] = slot[...].T
    pack_rows(sub, slots, send, energy, outs)


def slope_kernel(sub, shared, normals, step_weight, wave, coef, weight, lines):
    elements = normals.shape[2]
    parts = 1 if shared else sub
    pitch = coef.shape[0] // elements
    lines[...] = jnp.zeros_like(lines)
    for component in range(2):
        for corner in range(2):
            row = component * 2 + corner
            lines[row : row + 1, :] = normals[component, corner : corner + 1, :]

    def spread(column):
        return jnp.broadcast_to(column, (8, LANES))

    @pl.loop(0, elements // LANES)
    def _(k):
        turned = lines[:, pl.ds(pl.multiple_of(k * LANES, LANES), LANES)].T
        for group in range(LANES // 8):
            at = slice(group * 8, group * 8 + 8)
            x0, x1, y0, y1 = (spread(turned[at, j : j + 1]) for j in range(4))
            base = (k * LANES + group * 8) * pitch
            for part in range(parts):
                east, north = wave[part : part + 1, :], wave[sub + part : sub + part + 1, :]
                first = x0 * east + y0 * north
                second = x1 * east + y1 * north
                inward = jnp.minimum(first, 0.0) + jnp.minimum(second, 0.0) - jnp.maximum(first + second, 0.0)
                for which, value in enumerate((first, second, 1.0 / inward)):
                    coef[pl.ds(base + which * parts + part, 8, stride=pitch), :] = value

    nodes = step_weight.shape[1]
    for block in range(nodes // LANES):
        turned = jnp.broadcast_to(step_weight[0:1, block * LANES : (block + 1) * LANES], (8, LANES)).T
        for group in range(LANES // 8):
            value = spread(turned[group * 8 : group * 8 + 8, 0:1])
            for part in range(sub):
                at = pl.ds((block * LANES + group * 8) * sub + part, 8, stride=sub)
                weight[at, :] = value * wave[2 * sub + part : 2 * sub + part + 1, :]


def sweep_kernel(sub, shared, slots, conn, energy, coef, weight, *rest):
    ghosts, rest = rest[:BLOCKS], rest[BLOCKS:]
    partial, returned, rest = rest[0], rest[1 : 1 + BLOCKS], rest[1 + BLOCKS :]
    full, sums = rest[0], rest[1:]
    own_rows = energy.shape[0]
    ghost_rows = slots * sub
    rows = full.shape[0]
    elements = conn.shape[0] // 3
    parts = 1 if shared else sub
    pitch = coef.shape[0] // elements
    step = chunked(rows, 64)
    zero = jnp.zeros((step, LANES), jnp.float32)

    @pl.loop(0, rows // step)
    def _(k):
        for item in sums:
            item[pl.ds(pl.multiple_of(k * step, step), step), :] = zero

    full[:own_rows, :] = energy[...]
    for position in range(BLOCKS):
        first = own_rows + position * ghost_rows
        full[first : first + ghost_rows, :] = ghosts[position][...]

    share = elements // GROUPS
    unroll = chunked(share, 16)

    @pl.loop(0, share // unroll)
    def _(k):
        listed = [
            [conn.at[pl.ds(corner * elements + group * share + k * unroll, unroll)] for corner in range(3)]
            for group in range(GROUPS)
        ]
        for u in range(unroll):
            for group in range(GROUPS):
                element = group * share + k * unroll + u
                index = [item[u] for item in listed[group]]
                value = [full[pl.ds(row, sub), :] for row in index]
                tile = coef[pl.ds(element * pitch, pitch), :]
                first, second, inverse = (
                    jnp.broadcast_to(tile[j * parts : (j + 1) * parts], (sub, LANES)) for j in range(3)
                )
                both = first + second
                inflow = jnp.minimum(first, 0.0) * value[0] + jnp.minimum(second, 0.0) * value[1]
                inflow = (inflow - jnp.maximum(both, 0.0) * value[2]) * inverse
                residual = (
                    jnp.maximum(first, 0.0) * (value[0] - inflow),
                    jnp.maximum(second, 0.0) * (value[1] - inflow),
                    jnp.minimum(both, 0.0) * (inflow - value[2]),
                )
                for corner in range(3):
                    item = sums[group * 3 + corner]
                    at = pl.ds(index[corner], sub)
                    item[at, :] = item[at, :] + residual[corner]

    def total(at):
        result = sums[0][at, :]
        for item in sums[1:]:
            result = result + item[at, :]
        return result

    own_step = chunked(own_rows, 64)

    @pl.loop(0, own_rows // own_step)
    def _(k):
        at = pl.ds(pl.multiple_of(k * own_step, own_step), own_step)
        partial[at, :] = energy[at, :] - weight[at, :] * total(at)

    ghost_step = chunked(ghost_rows, 64)
    for position in range(BLOCKS):

        @pl.loop(0, ghost_rows // ghost_step)
        def _(k):
            at = pl.multiple_of(k * ghost_step, ghost_step)
            source = pl.ds(own_rows + position * ghost_rows + at, ghost_step)
            returned[position][pl.ds(at, ghost_step), :] = total(source)


def add_returned(sub, slots, send, weight, incoming, energy):
    unroll = chunked(slots, 16)
    for position in range(BLOCKS):

        @pl.loop(0, slots // unroll)
        def _(k):
            first = k * unroll
            listed = send.at[pl.ds((BLOCKS - 1 - position) * slots + first, unroll)]
            rows = [listed[u] for u in range(unroll)]
            fresh = [
                energy[pl.ds(row, sub), :]
                - weight[pl.ds(row, sub), :] * incoming[position][pl.ds((first + u) * sub, sub), :]
                for u, row in enumerate(rows)
            ]
            for row, item in zip(rows, fresh):
                energy[pl.ds(row, sub), :] = item


def between_kernel(sub, slots, send, partial, weight, *rest):
    incoming, energy, outs = rest[:BLOCKS], rest[BLOCKS], rest[BLOCKS + 1 :]
    energy[...] = partial[...]
    add_returned(sub, slots, send, weight, incoming, energy)
    pack_rows(sub, slots, send, energy, outs)


def leave_kernel(sub, lanes, slots, halves, send, partial, weight, *rest):
    incoming, out, energy = rest[:BLOCKS], rest[BLOCKS], rest[BLOCKS + 1]
    energy[...] = partial[...]
    add_returned(sub, slots, send, weight, incoming, energy)
    owned = energy.shape[0] // sub
    per_target = sub * lanes * halves
    for block in range(owned // LANES):
        target, half = divmod(block, halves)
        for part in range(sub):
            tile = energy[pl.ds(block * LANES * sub + part, LANES, stride=sub), :].T
            first = target * per_target + part * lanes * halves + half
            out[pl.ds(first, lanes, stride=halves), :] = tile[:lanes]


def interact_kernel(halves, plus, minus, rate, energy, out, *sums):
    bins = plus.shape[0]
    rows = energy.shape[0]
    step = chunked(rows, 64)
    zero = jnp.zeros((step, LANES), jnp.float32)

    @pl.loop(0, rows // step)
    def _(k):
        for item in sums[1:]:
            item[pl.ds(pl.multiple_of(k * step, step), step), :] = zero

    share = bins // GROUPS
    unroll = chunked(share, 12)

    @pl.loop(0, share // unroll)
    def _(k):
        for u in range(unroll):
            for group in range(GROUPS):
                index = group * share + k * unroll + u
                up, down = plus[index], minus[index]
                own = energy[pl.ds(index * halves, halves), :]
                upper = energy[pl.ds(up, halves), :]
                lower = energy[pl.ds(down, halves), :]
                term = rate[index] * (
                    own * own * (weight_plus * upper + weight_minus * lower)
                    - 2.0 * weight_both * own * upper * lower
                )
                sums[0][pl.ds(index * halves, halves), :] = own - 2.0 * term
                high, low = sums[1 + 2 * group], sums[2 + 2 * group]
                high[pl.ds(up, halves), :] = high[pl.ds(up, halves), :] + term
                low[pl.ds(down, halves), :] = low[pl.ds(down, halves), :] + term

    step = chunked(bins, 48)

    @pl.loop(0, bins // step)
    def _(k):
        for half in range(halves):
            at = pl.ds(k * step * halves + half, step, stride=halves)
            result = sums[0][at, :]
            for item in sums[1:]:
                result = result + item[at, :]
            out[pl.ds(pl.multiple_of(k * step, step), step), half * LANES : (half + 1) * LANES] = result


def shape_of(*dims):
    return jax.ShapeDtypeStruct(dims, jnp.float32)


def cost(flops, moved):
    return pl.CostEstimate(flops=flops, bytes_accessed=moved, transcendentals=0)


def limit(mebibytes):
    return pltpu.CompilerParams(vmem_limit_bytes=mebibytes << 20)


def on_device(
    spectrum, normals, conn, send_nodes, step_weight, group_speed, dia_plus, dia_minus, dia_coeff
):
    row_count, owned = spectrum.shape
    slots = send_nodes.shape[2]
    elements = conn.shape[1]
    bins = dia_plus.shape[0]
    spec_count = lax.axis_size("spec")
    sub = -(-row_count // LANES)
    while row_count % sub:
        sub += 1
    lanes = row_count // sub
    shared = lanes % NDIR == 0
    own_rows = owned * sub
    ghost_rows = slots * sub
    rows = own_rows + BLOCKS * ghost_rows
    halves = owned // (spec_count * LANES)

    send = (send_nodes[0] * sub).reshape(-1)
    nodes = (conn * sub).reshape(-1)

    bin_of = (
        lax.axis_index("spec") * row_count
        + jnp.arange(sub, dtype=jnp.int32)[:, None] * lanes
        + jnp.arange(LANES, dtype=jnp.int32)[None, :]
    )
    angle = (bin_of % NDIR).astype(jnp.float32) * (2.0 * math.pi / NDIR)
    east, north = jnp.cos(angle), jnp.sin(angle)
    select = ((bin_of // NDIR)[:, :, None] == jnp.arange(group_speed.shape[0], dtype=jnp.int32)).astype(jnp.float32)
    speed = jnp.sum(select * group_speed, axis=2)
    wave = jnp.concatenate([east, north, speed])

    block_shapes = [shape_of(ghost_rows, LANES)] * BLOCKS
    energy, *outs = pl.pallas_call(
        functools.partial(enter_kernel, sub, lanes, slots),
        out_shape=[shape_of(own_rows, LANES)] + block_shapes,
        in_specs=[SM, VM],
        out_specs=[VM] * (1 + BLOCKS),
        scratch_shapes=[pltpu.VMEM((4, LANES, LANES), jnp.float32)],
        cost_estimate=cost(0, 8 * own_rows * LANES),
        compiler_params=limit(8),
        name="enter",
    )(send, spectrum)
    pitch = 3 if shared else 3 * sub
    coef, weight = pl.pallas_call(
        functools.partial(slope_kernel, sub, shared),
        out_shape=[shape_of(elements * pitch, LANES), shape_of(own_rows, LANES)],
        in_specs=[VM] * 3,
        out_specs=[VM] * 2,
        scratch_shapes=[pltpu.VMEM((LANES, elements), jnp.float32)],
        cost_estimate=cost(20 * elements * LANES, 4 * LANES * (elements * pitch + own_rows)),
        compiler_params=limit(12),
        name="slopes",
    )(normals, step_weight.reshape(1, owned), wave)

    for sweep_index in range(STEPS):
        ghosts = [passed_along(outs[p], "dom", -offset_of(p)) for p in range(BLOCKS)]
        partial, *returned = pl.pallas_call(
            functools.partial(sweep_kernel, sub, shared, slots),
            out_shape=[shape_of(own_rows, LANES)] + block_shapes,
            in_specs=[SM] + [VM] * (3 + BLOCKS),
            out_specs=[VM] * (1 + BLOCKS),
            scratch_shapes=[pltpu.VMEM((rows, LANES), jnp.float32)] * (1 + 3 * GROUPS),
            cost_estimate=cost(elements * 24 * row_count, 4 * LANES * (3 * elements + 4 * rows)),
            compiler_params=limit(32),
            name="sweep",
        )(nodes, energy, coef, weight, *ghosts)
        incoming = [passed_along(returned[p], "dom", offset_of(p)) for p in range(BLOCKS)]
        if sweep_index < STEPS - 1:
            energy, *outs = pl.pallas_call(
                functools.partial(between_kernel, sub, slots),
                out_shape=[shape_of(own_rows, LANES)] + block_shapes,
                in_specs=[SM] + [VM] * (2 + BLOCKS),
                out_specs=[VM] * (1 + BLOCKS),
                cost_estimate=cost(2 * owned * row_count, 16 * own_rows * LANES),
                compiler_params=limit(8),
                name="between",
            )(send, partial, weight, *incoming)

    leaving = pl.pallas_call(
        functools.partial(leave_kernel, sub, lanes, slots, halves),
        out_shape=shape_of(spec_count * row_count * halves, LANES),
        in_specs=[SM] + [VM] * (2 + BLOCKS),
        out_specs=VM,
        scratch_shapes=[pltpu.VMEM((own_rows, LANES), jnp.float32)],
        cost_estimate=cost(2 * owned * row_count, 16 * own_rows * LANES),
        compiler_params=limit(8),
        name="leave",
    )(send, partial, weight, *incoming)
    arrived = lax.all_to_all(
        leaving.reshape(spec_count, row_count * halves, LANES), "spec", split_axis=0, concat_axis=0
    )
    return pl.pallas_call(
        functools.partial(interact_kernel, halves),
        out_shape=shape_of(bins, halves * LANES),
        in_specs=[SM] * 3 + [VM],
        out_specs=VM,
        scratch_shapes=[pltpu.VMEM((bins * halves, LANES), jnp.float32)] * (1 + 2 * GROUPS),
        cost_estimate=cost(16 * bins * halves * LANES, 8 * bins * halves * LANES),
        compiler_params=limit(12),
        name="interact",
    )(dia_plus * halves, dia_minus * halves, dia_coeff, arrived.reshape(bins * halves, LANES))


def solution(mesh):
    in_specs = (
        P("spec", "dom"),
        P(None, None, "dom"),
        P(None, "dom"),
        P("dom", None, None),
        P("dom"),
        P(),
        P(),
        P(),
        P(),
    )
    out_specs = P(None, ("dom", "spec"))
    return jax.shard_map(
        on_device, mesh=mesh, in_specs=in_specs, out_specs=out_specs, check_vma=False
    )
```

```python
import functools
import math

import jax
import jax.numpy as jnp
from jax import lax
from jax.experimental import pallas as pl
from jax.experimental.pallas import tpu as pltpu
from jax.sharding import PartitionSpec as P

NDIR = 36
REACH = 2
STEPS = 2
BLOCKS = 2 * REACH
LANES = 128
GROUPS = 2

weight_plus = 1.25 ** (-4)
weight_minus = 0.75 ** (-4)
weight_both = 0.9375 ** (-4)

VM = pl.BlockSpec(memory_space=pltpu.VMEM)
SM = pl.BlockSpec(memory_space=pltpu.SMEM)


def offset_of(position):
    return position - REACH if position < REACH else position - REACH + 1


def passed_along(value, axis, steps):
    count = lax.axis_size(axis)
    return lax.ppermute(value, axis, [(source, (source + steps) % count) for source in range(count)])


def chunked(total, limit):
    return max(size for size in range(1, limit + 1) if total % size == 0)


def rows_to_block(sub, lanes, stage, block):
    for column in range(block.shape[1] // LANES):
        for part in range(sub):
            tile = stage[pl.ds(column * LANES * sub + part, LANES, stride=sub), :].T
            block[part * lanes : (part + 1) * lanes, column * LANES : (column + 1) * LANES] = tile[:lanes]


def block_to_rows(sub, lanes, block, square, rows, first):
    for column in range(block.shape[1] // LANES):
        for part in range(sub):
            slot = square.at[(column * sub + part) % square.shape[0]]
            slot[:lanes, :] = block[part * lanes : (part + 1) * lanes, column * LANES : (column + 1) * LANES]
            rows[pl.ds(first + column * LANES * sub + part, LANES, stride=sub), :] = slot[...].T


def pack_rows(sub, lanes, send, energy, stages, outs):
    slots = outs[0].shape[1]
    unroll = chunked(slots, 32)
    for position in range(BLOCKS):
        stage = stages.at[position]

        @pl.loop(0, slots // unroll)
        def _(k):
            first = k * unroll
            listed = send.at[pl.ds((BLOCKS - 1 - position) * slots + first, unroll)]
            for u in range(unroll):
                stage[pl.ds((first + u) * sub, sub), :] = energy[pl.ds(listed[u], sub), :]

        rows_to_block(sub, lanes, stage, outs[position])


def enter_kernel(sub, lanes, send, spectrum, full, *rest):
    outs, square, stages = rest[:BLOCKS], rest[BLOCKS], rest[BLOCKS + 1]
    square[...] = jnp.zeros_like(square)
    block_to_rows(sub, lanes, spectrum, square, full, 0)
    pack_rows(sub, lanes, send, full, stages, outs)


def clear(items):
    rows = items[0].shape[0]
    step = chunked(rows, 64)
    zero = jnp.zeros((step, LANES), jnp.float32)

    @pl.loop(0, rows // step)
    def _(k):
        for item in items:
            item[pl.ds(pl.multiple_of(k * step, step), step), :] = zero


def slope_kernel(sub, shared, normals, step_weight, wave, coef, weight, lines):
    elements = normals.shape[2]
    parts = 1 if shared else sub
    pitch = coef.shape[0] // elements
    lines[...] = jnp.zeros_like(lines)
    for component in range(2):
        for corner in range(2):
            row = component * 2 + corner
            lines[row : row + 1, :] = normals[component, corner : corner + 1, :]

    def spread(column):
        return jnp.broadcast_to(column, (8, LANES))

    @pl.loop(0, elements // LANES)
    def _(k):
        turned = lines[:, pl.ds(pl.multiple_of(k * LANES, LANES), LANES)].T
        for group in range(LANES // 8):
            at = slice(group * 8, group * 8 + 8)
            x0, x1, y0, y1 = (spread(turned[at, j : j + 1]) for j in range(4))
            base = (k * LANES + group * 8) * pitch
            for part in range(parts):
                east, north = wave[part : part + 1, :], wave[sub + part : sub + part + 1, :]
                first = x0 * east + y0 * north
                second = x1 * east + y1 * north
                inward = jnp.minimum(first, 0.0) + jnp.minimum(second, 0.0) - jnp.maximum(first + second, 0.0)
                for which, value in enumerate((first, second, 1.0 / inward)):
                    coef[pl.ds(base + which * parts + part, 8, stride=pitch), :] = value

    nodes = step_weight.shape[1]
    for block in range(nodes // LANES):
        turned = jnp.broadcast_to(step_weight[0:1, block * LANES : (block + 1) * LANES], (8, LANES)).T
        for group in range(LANES // 8):
            value = spread(turned[group * 8 : group * 8 + 8, 0:1])
            for part in range(sub):
                at = pl.ds((block * LANES + group * 8) * sub + part, 8, stride=sub)
                weight[at, :] = value * wave[2 * sub + part : 2 * sub + part + 1, :]


def total(sums, at):
    result = sums[0][at, :]
    for item in sums[1:]:
        result = result + item[at, :]
    return result


def sweep_kernel(sub, lanes, shared, own_rows, conn, coef, weight, *rest):
    ghosts, full, rest = rest[:BLOCKS], rest[BLOCKS + 1], rest[BLOCKS + 2 :]
    returned, square, stages, sums = rest[:BLOCKS], rest[BLOCKS], rest[BLOCKS + 1], rest[BLOCKS + 2 :]
    clear(sums)
    ghost_rows = (full.shape[0] - own_rows) // BLOCKS
    elements = conn.shape[0] // 3
    parts = 1 if shared else sub
    pitch = coef.shape[0] // elements
    square[...] = jnp.zeros_like(square)
    for position in range(BLOCKS):
        block_to_rows(sub, lanes, ghosts[position], square, full, own_rows + position * ghost_rows)

    share = elements // GROUPS
    unroll = chunked(share, 16)

    @pl.loop(0, share // unroll)
    def _(k):
        listed = [
            [conn.at[pl.ds(corner * elements + group * share + k * unroll, unroll)] for corner in range(3)]
            for group in range(GROUPS)
        ]
        for u in range(unroll):
            for group in range(GROUPS):
                element = group * share + k * unroll + u
                index = [item[u] for item in listed[group]]
                value = [full[pl.ds(row, sub), :] for row in index]
                tile = coef[pl.ds(element * pitch, pitch), :]
                first, second, inverse = (
                    jnp.broadcast_to(tile[j * parts : (j + 1) * parts], (sub, LANES)) for j in range(3)
                )
                both = first + second
                inflow = jnp.minimum(first, 0.0) * value[0] + jnp.minimum(second, 0.0) * value[1]
                inflow = (inflow - jnp.maximum(both, 0.0) * value[2]) * inverse
                residual = (
                    jnp.maximum(first, 0.0) * (value[0] - inflow),
                    jnp.maximum(second, 0.0) * (value[1] - inflow),
                    jnp.minimum(both, 0.0) * (inflow - value[2]),
                )
                for corner in range(3):
                    item = sums[group * 3 + corner]
                    at = pl.ds(index[corner], sub)
                    item[at, :] = item[at, :] + residual[corner]

    step = chunked(ghost_rows, 64)
    for position in range(BLOCKS):
        stage = stages.at[position]

        @pl.loop(0, ghost_rows // step)
        def _(k):
            at = pl.multiple_of(k * step, step)
            stage[pl.ds(at, step), :] = total(sums, pl.ds(own_rows + position * ghost_rows + at, step))

        rows_to_block(sub, lanes, stage, returned[position])

    own_step = chunked(own_rows, 64)

    @pl.loop(0, own_rows // own_step)
    def _(k):
        at = pl.ds(pl.multiple_of(k * own_step, own_step), own_step)
        full[at, :] = full[at, :] - weight[at, :] * total(sums, at)


def add_returned(sub, lanes, send, weight, incoming, square, stages, full):
    slots = incoming[0].shape[1]
    square[...] = jnp.zeros_like(square)
    unroll = chunked(slots, 16)
    for position in range(BLOCKS):
        block_to_rows(sub, lanes, incoming[position], square, stages.at[position], 0)
    for position in range(BLOCKS):
        stage = stages.at[position]

        @pl.loop(0, slots // unroll)
        def _(k):
            first = k * unroll
            listed = send.at[pl.ds((BLOCKS - 1 - position) * slots + first, unroll)]
            rows = [listed[u] for u in range(unroll)]
            fresh = [
                full[pl.ds(row, sub), :] - weight[pl.ds(row, sub), :] * stage[pl.ds((first + u) * sub, sub), :]
                for u, row in enumerate(rows)
            ]
            for row, item in zip(rows, fresh):
                full[pl.ds(row, sub), :] = item


def between_kernel(sub, lanes, send, weight, *rest):
    incoming, rest = rest[:BLOCKS], rest[BLOCKS + 1 :]
    full, outs, square, stages = rest[0], rest[1 : 1 + BLOCKS], rest[1 + BLOCKS], rest[2 + BLOCKS]
    add_returned(sub, lanes, send, weight, incoming, square, stages, full)
    pack_rows(sub, lanes, send, full, stages, outs)


def leave_kernel(sub, lanes, halves, owned, send, weight, *rest):
    incoming, rest = rest[:BLOCKS], rest[BLOCKS + 1 :]
    full, out, square, stages = rest
    add_returned(sub, lanes, send, weight, incoming, square, stages, full)
    per_target = sub * lanes * halves
    for block in range(owned // LANES):
        target, half = divmod(block, halves)
        for part in range(sub):
            tile = full[pl.ds(block * LANES * sub + part, LANES, stride=sub), :].T
            first = target * per_target + part * lanes * halves + half
            out[pl.ds(first, lanes, stride=halves), :] = tile[:lanes]


def interact_kernel(halves, plus, minus, rate, energy, *rest):
    out, kept, added = rest[0], rest[1], rest[2:]
    clear(added)
    bins = plus.shape[0]
    share = bins // GROUPS
    unroll = chunked(share, 12)

    @pl.loop(0, share // unroll)
    def _(k):
        for u in range(unroll):
            for group in range(GROUPS):
                index = group * share + k * unroll + u
                up, down = plus[index], minus[index]
                here = pl.ds(index * halves, halves)
                own = energy[here, :]
                upper = energy[pl.ds(up, halves), :]
                lower = energy[pl.ds(down, halves), :]
                term = rate[index] * (
                    own * own * (weight_plus * upper + weight_minus * lower)
                    - 2.0 * weight_both * own * upper * lower
                )
                kept[here, :] = own - 2.0 * term
                for item, row in zip(added[2 * group :], (up, down)):
                    item[pl.ds(row, halves), :] = item[pl.ds(row, halves), :] + term

    step = chunked(bins, 48)

    @pl.loop(0, bins // step)
    def _(k):
        for half in range(halves):
            at = pl.ds(k * step * halves + half, step, stride=halves)
            result = kept[at, :] + total(added, at)
            out[pl.ds(pl.multiple_of(k * step, step), step), half * LANES : (half + 1) * LANES] = result


def shape_of(*dims):
    return jax.ShapeDtypeStruct(dims, jnp.float32)


def cost(flops, moved):
    return pl.CostEstimate(flops=flops, bytes_accessed=moved, transcendentals=0)


def limit(mebibytes):
    return pltpu.CompilerParams(vmem_limit_bytes=mebibytes << 20)


def on_device(
    spectrum, normals, conn, send_nodes, step_weight, group_speed, dia_plus, dia_minus, dia_coeff
):
    row_count, owned = spectrum.shape
    slots = send_nodes.shape[2]
    elements = conn.shape[1]
    bins = dia_plus.shape[0]
    spec_count = lax.axis_size("spec")
    sub = -(-row_count // LANES)
    while row_count % sub:
        sub += 1
    lanes = row_count // sub
    shared = lanes % NDIR == 0
    own_rows = owned * sub
    ghost_rows = slots * sub
    rows = own_rows + BLOCKS * ghost_rows
    halves = owned // (spec_count * LANES)

    send = (send_nodes[0] * sub).reshape(-1)
    nodes = (conn * sub).reshape(-1)

    bin_of = (
        lax.axis_index("spec") * row_count
        + jnp.arange(sub, dtype=jnp.int32)[:, None] * lanes
        + jnp.arange(LANES, dtype=jnp.int32)[None, :]
    )
    angle = (bin_of % NDIR).astype(jnp.float32) * (2.0 * math.pi / NDIR)
    east, north = jnp.cos(angle), jnp.sin(angle)
    select = ((bin_of // NDIR)[:, :, None] == jnp.arange(group_speed.shape[0], dtype=jnp.int32)).astype(jnp.float32)
    speed = jnp.sum(select * group_speed, axis=2)
    wave = jnp.concatenate([east, north, speed])

    block_shapes = [shape_of(row_count, slots)] * BLOCKS
    full_shape = shape_of(rows, LANES)
    sums = [pltpu.VMEM((rows, LANES), jnp.float32)] * (3 * GROUPS)
    squares = pltpu.VMEM((4, LANES, LANES), jnp.float32)
    stages = pltpu.VMEM((BLOCKS, ghost_rows, LANES), jnp.float32)
    moved = 4 * LANES * own_rows

    full, *outs = pl.pallas_call(
        functools.partial(enter_kernel, sub, lanes),
        out_shape=[full_shape] + block_shapes,
        in_specs=[SM, VM],
        out_specs=[VM] * (1 + BLOCKS),
        scratch_shapes=[squares, stages],
        cost_estimate=cost(0, 2 * moved),
        compiler_params=limit(4),
        name="enter",
    )(send, spectrum)
    pitch = 3 if shared else 3 * sub
    coef, weight = pl.pallas_call(
        functools.partial(slope_kernel, sub, shared),
        out_shape=[shape_of(elements * pitch, LANES), shape_of(own_rows, LANES)],
        in_specs=[VM] * 3,
        out_specs=[VM] * 2,
        scratch_shapes=[pltpu.VMEM((LANES, elements), jnp.float32)],
        cost_estimate=cost(20 * elements * LANES, 4 * LANES * (elements * pitch + own_rows)),
        compiler_params=limit(4),
        name="slopes",
    )(normals, step_weight.reshape(1, owned), wave)

    for sweep_index in range(STEPS):
        again = sweep_index < STEPS - 1
        ghosts = [passed_along(outs[p], "dom", -offset_of(p)) for p in range(BLOCKS)]
        full, *returned = pl.pallas_call(
            functools.partial(sweep_kernel, sub, lanes, shared, own_rows),
            out_shape=[full_shape] + block_shapes,
            in_specs=[SM] + [VM] * (3 + BLOCKS),
            out_specs=[VM] * (1 + BLOCKS),
            input_output_aliases={3 + BLOCKS: 0},
            scratch_shapes=[squares, stages] + sums,
            cost_estimate=cost(elements * 24 * row_count, 4 * LANES * (3 * elements + 4 * rows)),
            compiler_params=limit(20),
            name="sweep",
        )(nodes, coef, weight, *ghosts, full)
        incoming = [passed_along(returned[p], "dom", offset_of(p)) for p in range(BLOCKS)]
        if again:
            full, *outs = pl.pallas_call(
                functools.partial(between_kernel, sub, lanes),
                out_shape=[full_shape] + block_shapes,
                in_specs=[SM] + [VM] * (2 + BLOCKS),
                out_specs=[VM] * (1 + BLOCKS),
                input_output_aliases={2 + BLOCKS: 0},
                scratch_shapes=[squares, stages],
                cost_estimate=cost(2 * owned * row_count, 4 * moved),
                compiler_params=limit(4),
                name="between",
            )(send, weight, *incoming, full)

    full, leaving = pl.pallas_call(
        functools.partial(leave_kernel, sub, lanes, halves, owned),
        out_shape=[full_shape, shape_of(spec_count * row_count * halves, LANES)],
        in_specs=[SM] + [VM] * (2 + BLOCKS),
        out_specs=[VM] * 2,
        input_output_aliases={2 + BLOCKS: 0},
        scratch_shapes=[squares, stages],
        cost_estimate=cost(2 * owned * row_count, 4 * moved),
        compiler_params=limit(4),
        name="leave",
    )(send, weight, *incoming, full)
    arrived = lax.all_to_all(
        leaving.reshape(spec_count, row_count * halves, LANES), "spec", split_axis=0, concat_axis=0
    )
    return pl.pallas_call(
        functools.partial(interact_kernel, halves),
        out_shape=shape_of(bins, halves * LANES),
        in_specs=[SM] * 3 + [VM],
        out_specs=VM,
        scratch_shapes=[pltpu.VMEM((bins * halves, LANES), jnp.float32)] * (1 + 2 * GROUPS),
        cost_estimate=cost(16 * bins * halves * LANES, 8 * bins * halves * LANES),
        compiler_params=limit(10),
        name="interact",
    )(dia_plus * halves, dia_minus * halves, dia_coeff, arrived.reshape(bins * halves, LANES))


def solution(mesh):
    in_specs = (
        P("spec", "dom"),
        P(None, None, "dom"),
        P(None, "dom"),
        P("dom", None, None),
        P("dom"),
        P(),
        P(),
        P(),
        P(),
    )
    out_specs = P(None, ("dom", "spec"))
    return jax.shard_map(
        on_device, mesh=mesh, in_specs=in_specs, out_specs=out_specs, check_vma=False
    )
```

```python
import functools
import math

import jax
import jax.numpy as jnp
from jax import lax
from jax.experimental import pallas as pl
from jax.experimental.pallas import tpu as pltpu
from jax.sharding import PartitionSpec as P

NDIR = 36
REACH = 2
STEPS = 2
BLOCKS = 2 * REACH
LANES = 128
GROUPS = 2


weight_plus = 1.25 ** (-4)
weight_minus = 0.75 ** (-4)
weight_both = 0.9375 ** (-4)

VM = pl.BlockSpec(memory_space=pltpu.VMEM)
SM = pl.BlockSpec(memory_space=pltpu.SMEM)


def offset_of(position):
    return position - REACH if position < REACH else position - REACH + 1


def passed_along(value, axis, steps):
    count = lax.axis_size(axis)
    return lax.ppermute(value, axis, [(source, (source + steps) % count) for source in range(count)])


def chunked(total, limit):
    return max(size for size in range(1, limit + 1) if total % size == 0)


def rows_to_block(lanes, stage, block):
    for column in range(block.shape[1] // LANES):
        at = slice(column * LANES, (column + 1) * LANES)
        block[:, at] = stage[at, :].T[:lanes]


def block_to_rows(lanes, block, square, rows, first, chunk=0):
    for column in range(block.shape[1] // LANES):
        slot = square.at[column % square.shape[0]]
        slot[:lanes, :] = block[chunk * lanes : (chunk + 1) * lanes, column * LANES : (column + 1) * LANES]
        rows[first + column * LANES : first + (column + 1) * LANES, :] = slot[...].T


def pack_rows(lanes, send, full, stages, outs):
    slots = outs[0].shape[1]
    unroll = chunked(slots, 32)
    for position in range(BLOCKS):
        stage = stages.at[position]

        @pl.loop(0, slots // unroll)
        def _(k):
            first = k * unroll
            listed = send.at[pl.ds((BLOCKS - 1 - position) * slots + first, unroll)]
            for u in range(unroll):
                stage[pl.ds(first + u, 1), :] = full[pl.ds(listed[u], 1), :]

    for position in range(BLOCKS):
        rows_to_block(lanes, stages.at[position], outs[position])


def enter_kernel(chunk, lanes, send, spectrum, full, *rest):
    outs, square, stages = rest[:BLOCKS], rest[BLOCKS], rest[BLOCKS + 1]
    square[...] = jnp.zeros_like(square)
    block_to_rows(lanes, spectrum, square, full, 0, chunk)
    pack_rows(lanes, send, full, stages, outs)


def clear(items):
    rows = items[0].shape[0]
    step = chunked(rows, 64)
    zero = jnp.zeros((step, LANES), jnp.float32)

    @pl.loop(0, rows // step)
    def _(k):
        for item in items:
            item[pl.ds(pl.multiple_of(k * step, step), step), :] = zero


def slope_kernel(chunks, normals, step_weight, wave, *rest):
    weights, coefs, lines = rest[:chunks], rest[chunks:-1], rest[-1]
    elements = normals.shape[2]
    lines[...] = jnp.zeros_like(lines)
    for component in range(2):
        for corner in range(2):
            row = component * 2 + corner
            lines[row : row + 1, :] = normals[component, corner : corner + 1, :]

    def spread(column):
        return jnp.broadcast_to(column, (8, LANES))

    @pl.loop(0, elements // LANES)
    def _(k):
        turned = lines[:, pl.ds(pl.multiple_of(k * LANES, LANES), LANES)].T
        for group in range(LANES // 8):
            at = slice(group * 8, group * 8 + 8)
            x0, x1, y0, y1 = (spread(turned[at, j : j + 1]) for j in range(4))
            base = (k * LANES + group * 8) * 3
            for chunk, coef in enumerate(coefs):
                east, north = wave[chunk : chunk + 1, :], wave[chunks + chunk : chunks + chunk + 1, :]
                first = x0 * east + y0 * north
                second = x1 * east + y1 * north
                inward = jnp.minimum(first, 0.0) + jnp.minimum(second, 0.0) - jnp.maximum(first + second, 0.0)
                for which, value in enumerate((first, second, 1.0 / inward)):
                    coef[pl.ds(base + which, 8, stride=3), :] = value

    nodes = step_weight.shape[1]
    for block in range(nodes // LANES):
        turned = jnp.broadcast_to(step_weight[0:1, block * LANES : (block + 1) * LANES], (8, LANES)).T
        for group in range(LANES // 8):
            value = spread(turned[group * 8 : group * 8 + 8, 0:1])
            at = slice(block * LANES + group * 8, block * LANES + group * 8 + 8)
            for chunk, weight in enumerate(weights):
                weight[at, :] = value * wave[2 * chunks + chunk : 2 * chunks + chunk + 1, :]


def total(sums, at):
    result = sums[0][at, :]
    for item in sums[1:]:
        result = result + item[at, :]
    return result


def sweep_kernel(lanes, owned, conn, coef, weight, *rest):
    ghosts, full, rest = rest[:BLOCKS], rest[BLOCKS + 1], rest[BLOCKS + 2 :]
    returned, square, stages, sums = rest[:BLOCKS], rest[BLOCKS], rest[BLOCKS + 1], rest[BLOCKS + 2 :]
    clear(sums)
    slots = ghosts[0].shape[1]
    elements = conn.shape[0] // 3
    square[...] = jnp.zeros_like(square)
    for position in range(BLOCKS):
        block_to_rows(lanes, ghosts[position], square, full, owned + position * slots)

    share = elements // GROUPS
    unroll = chunked(share, 16)

    @pl.loop(0, share // unroll)
    def _(k):
        listed = [
            [conn.at[pl.ds(corner * elements + group * share + k * unroll, unroll)] for corner in range(3)]
            for group in range(GROUPS)
        ]
        for u in range(unroll):
            for group in range(GROUPS):
                element = group * share + k * unroll + u
                at = [pl.ds(item[u], 1) for item in listed[group]]
                value = [full[row, :] for row in at]
                tile = coef[pl.ds(element * 3, 3), :]
                first, second, inverse = (tile[j : j + 1] for j in range(3))
                both = first + second
                inflow = jnp.minimum(first, 0.0) * value[0] + jnp.minimum(second, 0.0) * value[1]
                inflow = (inflow - jnp.maximum(both, 0.0) * value[2]) * inverse
                residual = (
                    jnp.maximum(first, 0.0) * (value[0] - inflow),
                    jnp.maximum(second, 0.0) * (value[1] - inflow),
                    jnp.minimum(both, 0.0) * (inflow - value[2]),
                )
                for corner in range(3):
                    item = sums[group * 3 + corner]
                    item[at[corner], :] = item[at[corner], :] + residual[corner]

    for position in range(BLOCKS):
        first = owned + position * slots
        stages[position] = total(sums, slice(first, first + slots))
        rows_to_block(lanes, stages.at[position], returned[position])

    step = chunked(owned, 64)

    @pl.loop(0, owned // step)
    def _(k):
        at = pl.ds(pl.multiple_of(k * step, step), step)
        full[at, :] = full[at, :] - weight[at, :] * total(sums, at)


def add_returned(lanes, send, weight, incoming, square, stages, full):
    slots = incoming[0].shape[1]
    square[...] = jnp.zeros_like(square)
    unroll = chunked(slots, 16)
    for position in range(BLOCKS):
        block_to_rows(lanes, incoming[position], square, stages.at[position], 0)
    for position in range(BLOCKS):
        stage = stages.at[position]

        @pl.loop(0, slots // unroll)
        def _(k):
            first = k * unroll
            listed = send.at[pl.ds((BLOCKS - 1 - position) * slots + first, unroll)]
            rows = [pl.ds(listed[u], 1) for u in range(unroll)]
            fresh = [full[row, :] - weight[row, :] * stage[pl.ds(first + u, 1), :] for u, row in enumerate(rows)]
            for row, item in zip(rows, fresh):
                full[row, :] = item


def between_kernel(lanes, send, weight, *rest):
    incoming, rest = rest[:BLOCKS], rest[BLOCKS + 1 :]
    full, outs, square, stages = rest[0], rest[1 : 1 + BLOCKS], rest[1 + BLOCKS], rest[2 + BLOCKS]
    add_returned(lanes, send, weight, incoming, square, stages, full)
    pack_rows(lanes, send, full, stages, outs)


def leave_kernel(lanes, halves, count, place, send, weight, *rest):
    incoming, rest = rest[:BLOCKS], rest[BLOCKS + 1 :]
    full, outs, square, stages = rest[0], rest[1 : 1 + count], rest[1 + count], rest[2 + count]
    add_returned(lanes, send, weight, incoming, square, stages, full)
    for distance in range(count):
        target = lax.rem(place[0] + distance, count)
        for half in range(halves):
            first = pl.multiple_of((target * halves + half) * LANES, LANES)
            outs[distance][pl.ds(half, lanes, stride=halves), :] = full[pl.ds(first, LANES), :].T[:lanes]


def interact_kernel(lanes, halves, count, chunks, place, plus, minus, rate, *rest):
    pieces, rest = rest[: count * chunks], rest[count * chunks :]
    out, energy, kept, added = rest[0], rest[1], rest[2], rest[3:]
    clear(added)
    rows = lanes * halves
    for distance in range(count):
        source = lax.rem(place[0] + count - distance, count)
        for chunk in range(chunks):
            first = (source * chunks + chunk) * rows
            if rows % 8 == 0:
                first = pl.multiple_of(first, 8)
            energy[pl.ds(first, rows), :] = pieces[distance * chunks + chunk][...]

    bins = plus.shape[0]
    share = bins // GROUPS
    unroll = chunked(share, 12)

    @pl.loop(0, share // unroll)
    def _(k):
        for u in range(unroll):
            for group in range(GROUPS):
                index = group * share + k * unroll + u
                up, down = plus[index], minus[index]
                here = pl.ds(index * halves, halves)
                own = energy[here, :]
                upper = energy[pl.ds(up, halves), :]
                lower = energy[pl.ds(down, halves), :]
                term = rate[index] * (
                    own * own * (weight_plus * upper + weight_minus * lower)
                    - 2.0 * weight_both * own * upper * lower
                )
                kept[here, :] = own - 2.0 * term
                for item, row in zip(added[2 * group :], (up, down)):
                    item[pl.ds(row, halves), :] = item[pl.ds(row, halves), :] + term

    step = chunked(bins, 48)

    @pl.loop(0, bins // step)
    def _(k):
        for half in range(halves):
            at = pl.ds(k * step * halves + half, step, stride=halves)
            result = kept[at, :] + total(added, at)
            out[pl.ds(pl.multiple_of(k * step, step), step), half * LANES : (half + 1) * LANES] = result


def shape_of(*dims):
    return jax.ShapeDtypeStruct(dims, jnp.float32)


def cost(flops, moved):
    return pl.CostEstimate(flops=flops, bytes_accessed=moved, transcendentals=0)


def limit(mebibytes):
    return pltpu.CompilerParams(vmem_limit_bytes=mebibytes << 20)


def on_device(
    spectrum, normals, conn, send_nodes, step_weight, group_speed, dia_plus, dia_minus, dia_coeff
):
    row_count, owned = spectrum.shape
    slots = send_nodes.shape[2]
    elements = conn.shape[1]
    bins = dia_plus.shape[0]
    count = lax.axis_size("spec")
    chunks = -(-row_count // LANES)
    while row_count % chunks:
        chunks += 1
    lanes = row_count // chunks
    shared = lanes % NDIR == 0
    rows = owned + BLOCKS * slots
    halves = owned // (count * LANES)

    send = send_nodes.reshape(-1)
    nodes = conn.reshape(-1)
    place = lax.axis_index("spec").reshape(1)

    bin_of = (
        lax.axis_index("spec") * row_count
        + jnp.arange(chunks, dtype=jnp.int32)[:, None] * lanes
        + jnp.arange(LANES, dtype=jnp.int32)[None, :]
    )
    angle = (bin_of % NDIR).astype(jnp.float32) * (2.0 * math.pi / NDIR)
    east, north = jnp.cos(angle), jnp.sin(angle)
    select = ((bin_of // NDIR)[:, :, None] == jnp.arange(group_speed.shape[0], dtype=jnp.int32)).astype(jnp.float32)
    speed = jnp.sum(select * group_speed, axis=2)
    wave = jnp.concatenate([east, north, speed])

    block_shapes = [shape_of(lanes, slots)] * BLOCKS
    full_shape = shape_of(rows, LANES)
    sums = [pltpu.VMEM((rows, LANES), jnp.float32)] * (3 * GROUPS)
    squares = pltpu.VMEM((4, LANES, LANES), jnp.float32)
    stages = pltpu.VMEM((BLOCKS, slots, LANES), jnp.float32)
    moved = 4 * LANES * owned
    every = range(chunks)

    entered = [
        pl.pallas_call(
            functools.partial(enter_kernel, chunk, lanes),
            out_shape=[full_shape] + block_shapes,
            in_specs=[SM, VM],
            out_specs=[VM] * (1 + BLOCKS),
            scratch_shapes=[squares, stages],
            cost_estimate=cost(0, 2 * moved),
            compiler_params=limit(2),
            name=f"enter{chunk}",
        )(send, spectrum)
        for chunk in every
    ]
    full, outs = [item[0] for item in entered], [item[1:] for item in entered]
    tables = 1 if shared else chunks
    made = pl.pallas_call(
        functools.partial(slope_kernel, chunks),
        out_shape=[shape_of(owned, LANES)] * chunks + [shape_of(elements * 3, LANES)] * tables,
        in_specs=[VM] * 3,
        out_specs=[VM] * (chunks + tables),
        scratch_shapes=[pltpu.VMEM((LANES, elements), jnp.float32)],
        cost_estimate=cost(20 * elements * LANES, 4 * LANES * (elements * 3 * tables + owned * chunks)),
        compiler_params=limit(3),
        name="slopes",
    )(normals, step_weight.reshape(1, owned), wave)
    weight, coef = made[:chunks], (made[chunks:] * chunks)[:chunks]

    incoming = [None] * chunks
    for sweep_index in range(STEPS):
        for chunk in every:
            ghosts = [passed_along(outs[chunk][p], "dom", -offset_of(p)) for p in range(BLOCKS)]
            full[chunk], *returned = pl.pallas_call(
                functools.partial(sweep_kernel, lanes, owned),
                out_shape=[full_shape] + block_shapes,
                in_specs=[SM] + [VM] * (3 + BLOCKS),
                out_specs=[VM] * (1 + BLOCKS),
                input_output_aliases={3 + BLOCKS: 0},
                scratch_shapes=[squares, stages] + sums,
                cost_estimate=cost(elements * 24 * row_count, 4 * LANES * 8 * elements),
                compiler_params=limit(7),
                name=f"sweep{chunk}",
            )(nodes, coef[chunk], weight[chunk], *ghosts, full[chunk])
            incoming[chunk] = [passed_along(returned[p], "dom", offset_of(p)) for p in range(BLOCKS)]
        if sweep_index < STEPS - 1:
            for chunk in every:
                full[chunk], *outs[chunk] = pl.pallas_call(
                    functools.partial(between_kernel, lanes),
                    out_shape=[full_shape] + block_shapes,
                    in_specs=[SM] + [VM] * (2 + BLOCKS),
                    out_specs=[VM] * (1 + BLOCKS),
                    input_output_aliases={2 + BLOCKS: 0},
                    scratch_shapes=[squares, stages],
                    cost_estimate=cost(2 * owned * LANES, 3 * moved),
                    compiler_params=limit(2),
                    name=f"between{chunk}",
                )(send, weight[chunk], *incoming[chunk], full[chunk])

    arrived = [[None] * chunks for _ in range(count)]
    for chunk in every:
        _, *blocks = pl.pallas_call(
            functools.partial(leave_kernel, lanes, halves, count),
            out_shape=[full_shape] + [shape_of(lanes * halves, LANES)] * count,
            in_specs=[SM] * 2 + [VM] * (2 + BLOCKS),
            out_specs=[VM] * (1 + count),
            input_output_aliases={3 + BLOCKS: 0},
            scratch_shapes=[squares, stages],
            cost_estimate=cost(2 * owned * LANES, 3 * moved),
            compiler_params=limit(2),
            name=f"leave{chunk}",
        )(place, send, weight[chunk], *incoming[chunk], full[chunk])
        for distance in range(count):
            arrived[distance][chunk] = passed_along(blocks[distance], "spec", distance) if distance else blocks[0]
    return pl.pallas_call(
        functools.partial(interact_kernel, lanes, halves, count, chunks),
        out_shape=shape_of(bins, halves * LANES),
        in_specs=[SM] * 4 + [VM] * (count * chunks),
        out_specs=VM,
        scratch_shapes=[pltpu.VMEM((bins * halves, LANES), jnp.float32)] * (2 + 2 * GROUPS),
        cost_estimate=cost(16 * bins * halves * LANES, 8 * bins * halves * LANES),
        compiler_params=limit(12),
        name="interact",
    )(place, dia_plus * halves, dia_minus * halves, dia_coeff, *(piece for row in arrived for piece in row))


def solution(mesh):
    in_specs = (
        P("spec", "dom"),
        P(None, None, "dom"),
        P(None, "dom"),
        P("dom", None, None),
        P("dom"),
        P(),
        P(),
        P(),
        P(),
    )
    out_specs = P(None, ("dom", "spec"))
    return jax.shard_map(
        on_device, mesh=mesh, in_specs=in_specs, out_specs=out_specs, check_vma=False
    )
```

```python
import functools
import math

import jax
import jax.numpy as jnp
from jax import lax
from jax.experimental import pallas as pl
from jax.experimental.pallas import tpu as pltpu
from jax.sharding import PartitionSpec as P

NDIR = 36
REACH = 2
STEPS = 2
BLOCKS = 2 * REACH
LANES = 128
GROUPS = 2

weight_plus = 1.25 ** (-4)
weight_minus = 0.75 ** (-4)
weight_both = 0.9375 ** (-4)

VM = pl.BlockSpec(memory_space=pltpu.VMEM)
SM = pl.BlockSpec(memory_space=pltpu.SMEM)


def offset_of(position):
    return position - REACH if position < REACH else position - REACH + 1


def passed_along(value, axis, steps):
    count = lax.axis_size(axis)
    return lax.ppermute(value, axis, [(source, (source + steps) % count) for source in range(count)])


def chunked(total, limit):
    return max(size for size in range(1, limit + 1) if total % size == 0)


def rows_to_block(sub, lanes, stage, block):
    for column in range(block.shape[1] // LANES):
        for part in range(sub):
            tile = stage[pl.ds(column * LANES * sub + part, LANES, stride=sub), :].T
            block[part * lanes : (part + 1) * lanes, column * LANES : (column + 1) * LANES] = tile[:lanes]


def block_to_rows(sub, lanes, block, square, rows, first):
    for column in range(block.shape[1] // LANES):
        for part in range(sub):
            slot = square.at[(column * sub + part) % square.shape[0]]
            slot[:lanes, :] = block[part * lanes : (part + 1) * lanes, column * LANES : (column + 1) * LANES]
            rows[pl.ds(first + column * LANES * sub + part, LANES, stride=sub), :] = slot[...].T


def pack_rows(sub, lanes, send, energy, stages, outs):
    slots = outs[0].shape[1]
    unroll = chunked(slots, 32)
    for position in range(BLOCKS):
        stage = stages.at[position]

        @pl.loop(0, slots // unroll)
        def _(k):
            first = k * unroll
            listed = send.at[pl.ds((BLOCKS - 1 - position) * slots + first, unroll)]
            for u in range(unroll):
                stage[pl.ds((first + u) * sub, sub), :] = energy[pl.ds(listed[u], sub), :]

        rows_to_block(sub, lanes, stage, outs[position])


def enter_kernel(sub, lanes, send, spectrum, full, *rest):
    outs, square, stages = rest[:BLOCKS], rest[BLOCKS], rest[BLOCKS + 1]
    square[...] = jnp.zeros_like(square)
    block_to_rows(sub, lanes, spectrum, square, full, 0)
    pack_rows(sub, lanes, send, full, stages, outs)


def clear(items):
    rows = items[0].shape[0]
    step = chunked(rows, 64)
    zero = jnp.zeros((step, LANES), jnp.float32)

    @pl.loop(0, rows // step)
    def _(k):
        for item in items:
            item[pl.ds(pl.multiple_of(k * step, step), step), :] = zero


def slope_kernel(sub, shared, normals, step_weight, wave, coef, weight, lines):
    elements = normals.shape[2]
    parts = 1 if shared else sub
    pitch = coef.shape[0] // elements
    lines[...] = jnp.zeros_like(lines)
    for component in range(2):
        for corner in range(2):
            row = component * 2 + corner
            lines[row : row + 1, :] = normals[component, corner : corner + 1, :]

    def spread(column):
        return jnp.broadcast_to(column, (8, LANES))

    @pl.loop(0, elements // LANES)
    def _(k):
        turned = lines[:, pl.ds(pl.multiple_of(k * LANES, LANES), LANES)].T
        for group in range(LANES // 8):
            at = slice(group * 8, group * 8 + 8)
            x0, x1, y0, y1 = (spread(turned[at, j : j + 1]) for j in range(4))
            base = (k * LANES + group * 8) * pitch
            for part in range(parts):
                east, north = wave[part : part + 1, :], wave[sub + part : sub + part + 1, :]
                first = x0 * east + y0 * north
                second = x1 * east + y1 * north
                inward = jnp.minimum(first, 0.0) + jnp.minimum(second, 0.0) - jnp.maximum(first + second, 0.0)
                for which, value in enumerate((first, second, 1.0 / inward)):
                    coef[pl.ds(base + which * parts + part, 8, stride=pitch), :] = value

    nodes = step_weight.shape[1]
    for block in range(nodes // LANES):
        turned = jnp.broadcast_to(step_weight[0:1, block * LANES : (block + 1) * LANES], (8, LANES)).T
        for group in range(LANES // 8):
            value = spread(turned[group * 8 : group * 8 + 8, 0:1])
            for part in range(sub):
                at = pl.ds((block * LANES + group * 8) * sub + part, 8, stride=sub)
                weight[at, :] = value * wave[2 * sub + part : 2 * sub + part + 1, :]


def total(sums, at):
    result = sums[0][at, :]
    for item in sums[1:]:
        result = result + item[at, :]
    return result


def sweep_kernel(sub, lanes, shared, own_rows, conn, coef, weight, *rest):
    ghosts, full, rest = rest[:BLOCKS], rest[BLOCKS + 1], rest[BLOCKS + 2 :]
    returned, square, stages, sums = rest[:BLOCKS], rest[BLOCKS], rest[BLOCKS + 1], rest[BLOCKS + 2 :]
    clear(sums)
    ghost_rows = (full.shape[0] - own_rows) // BLOCKS
    elements = conn.shape[0] // 3
    parts = 1 if shared else sub
    pitch = coef.shape[0] // elements
    square[...] = jnp.zeros_like(square)
    for position in range(BLOCKS):
        block_to_rows(sub, lanes, ghosts[position], square, full, own_rows + position * ghost_rows)

    share = elements // GROUPS
    unroll = chunked(share, 16)

    @pl.loop(0, share // unroll)
    def _(k):
        listed = [
            [conn.at[pl.ds(corner * elements + group * share + k * unroll, unroll)] for corner in range(3)]
            for group in range(GROUPS)
        ]
        for u in range(unroll):
            for group in range(GROUPS):
                element = group * share + k * unroll + u
                index = [item[u] for item in listed[group]]
                value = [full[pl.ds(row, sub), :] for row in index]
                tile = coef[pl.ds(element * pitch, pitch), :]
                first, second, inverse = (
                    jnp.broadcast_to(tile[j * parts : (j + 1) * parts], (sub, LANES)) for j in range(3)
                )
                both = first + second
                inflow = jnp.minimum(first, 0.0) * value[0] + jnp.minimum(second, 0.0) * value[1]
                inflow = (inflow - jnp.maximum(both, 0.0) * value[2]) * inverse
                residual = (
                    jnp.maximum(first, 0.0) * (value[0] - inflow),
                    jnp.maximum(second, 0.0) * (value[1] - inflow),
                    jnp.minimum(both, 0.0) * (inflow - value[2]),
                )
                for corner in range(3):
                    item = sums[group * 3 + corner]
                    at = pl.ds(index[corner], sub)
                    item[at, :] = item[at, :] + residual[corner]

    step = chunked(ghost_rows, 64)
    for position in range(BLOCKS):
        stage = stages.at[position]

        @pl.loop(0, ghost_rows // step)
        def _(k):
            at = pl.multiple_of(k * step, step)
            stage[pl.ds(at, step), :] = total(sums, pl.ds(own_rows + position * ghost_rows + at, step))

        rows_to_block(sub, lanes, stage, returned[position])

    own_step = chunked(own_rows, 64)

    @pl.loop(0, own_rows // own_step)
    def _(k):
        at = pl.ds(pl.multiple_of(k * own_step, own_step), own_step)
        full[at, :] = full[at, :] - weight[at, :] * total(sums, at)


def add_returned(sub, lanes, send, weight, incoming, square, stages, full):
    slots = incoming[0].shape[1]
    square[...] = jnp.zeros_like(square)
    unroll = chunked(slots, 16)
    for position in range(BLOCKS):
        block_to_rows(sub, lanes, incoming[position], square, stages.at[position], 0)
    for position in range(BLOCKS):
        stage = stages.at[position]

        @pl.loop(0, slots // unroll)
        def _(k):
            first = k * unroll
            listed = send.at[pl.ds((BLOCKS - 1 - position) * slots + first, unroll)]
            rows = [listed[u] for u in range(unroll)]
            fresh = [
                full[pl.ds(row, sub), :] - weight[pl.ds(row, sub), :] * stage[pl.ds((first + u) * sub, sub), :]
                for u, row in enumerate(rows)
            ]
            for row, item in zip(rows, fresh):
                full[pl.ds(row, sub), :] = item


def between_kernel(sub, lanes, send, weight, *rest):
    incoming, rest = rest[:BLOCKS], rest[BLOCKS + 1 :]
    full, outs, square, stages = rest[0], rest[1 : 1 + BLOCKS], rest[1 + BLOCKS], rest[2 + BLOCKS]
    add_returned(sub, lanes, send, weight, incoming, square, stages, full)
    pack_rows(sub, lanes, send, full, stages, outs)


def leave_kernel(sub, lanes, halves, count, place, send, weight, *rest):
    incoming, rest = rest[:BLOCKS], rest[BLOCKS + 1 :]
    full, outs, square, stages = rest[0], rest[1 : 1 + count], rest[1 + count], rest[2 + count]
    add_returned(sub, lanes, send, weight, incoming, square, stages, full)
    for distance in range(count):
        target = lax.rem(place[0] + distance, count)
        for half in range(halves):
            first = (target * halves + half) * LANES * sub
            for part in range(sub):
                tile = full[pl.ds(first + part, LANES, stride=sub), :].T
                outs[distance][pl.ds(part * lanes * halves + half, lanes, stride=halves), :] = tile[:lanes]


def interact_kernel(halves, count, place, plus, minus, rate, *rest):
    pieces, rest = rest[:count], rest[count:]
    out, energy, kept, added = rest[0], rest[1], rest[2], rest[3:]
    clear(added)
    rows = pieces[0].shape[0]
    for distance in range(count):
        first = lax.rem(place[0] + count - distance, count) * rows
        if rows % 8 == 0:
            first = pl.multiple_of(first, 8)
        energy[pl.ds(first, rows), :] = pieces[distance][...]
    bins = plus.shape[0]
    share = bins // GROUPS
    unroll = chunked(share, 12)

    @pl.loop(0, share // unroll)
    def _(k):
        for u in range(unroll):
            for group in range(GROUPS):
                index = group * share + k * unroll + u
                up, down = plus[index], minus[index]
                here = pl.ds(index * halves, halves)
                own = energy[here, :]
                upper = energy[pl.ds(up, halves), :]
                lower = energy[pl.ds(down, halves), :]
                term = rate[index] * (
                    own * own * (weight_plus * upper + weight_minus * lower)
                    - 2.0 * weight_both * own * upper * lower
                )
                kept[here, :] = own - 2.0 * term
                for item, row in zip(added[2 * group :], (up, down)):
                    item[pl.ds(row, halves), :] = item[pl.ds(row, halves), :] + term

    step = chunked(bins, 48)

    @pl.loop(0, bins // step)
    def _(k):
        for half in range(halves):
            at = pl.ds(k * step * halves + half, step, stride=halves)
            result = kept[at, :] + total(added, at)
            out[pl.ds(pl.multiple_of(k * step, step), step), half * LANES : (half + 1) * LANES] = result


def shape_of(*dims):
    return jax.ShapeDtypeStruct(dims, jnp.float32)


def cost(flops, moved):
    return pl.CostEstimate(flops=flops, bytes_accessed=moved, transcendentals=0)


def limit(mebibytes):
    return pltpu.CompilerParams(vmem_limit_bytes=mebibytes << 20)


def on_device(
    spectrum, normals, conn, send_nodes, step_weight, group_speed, dia_plus, dia_minus, dia_coeff
):
    row_count, owned = spectrum.shape
    slots = send_nodes.shape[2]
    elements = conn.shape[1]
    bins = dia_plus.shape[0]
    spec_count = lax.axis_size("spec")
    sub = -(-row_count // LANES)
    while row_count % sub:
        sub += 1
    lanes = row_count // sub
    shared = lanes % NDIR == 0
    own_rows = owned * sub
    ghost_rows = slots * sub
    rows = own_rows + BLOCKS * ghost_rows
    halves = owned // (spec_count * LANES)

    send = (send_nodes[0] * sub).reshape(-1)
    nodes = (conn * sub).reshape(-1)
    place = lax.axis_index("spec").reshape(1)

    bin_of = (
        lax.axis_index("spec") * row_count
        + jnp.arange(sub, dtype=jnp.int32)[:, None] * lanes
        + jnp.arange(LANES, dtype=jnp.int32)[None, :]
    )
    angle = (bin_of % NDIR).astype(jnp.float32) * (2.0 * math.pi / NDIR)
    east, north = jnp.cos(angle), jnp.sin(angle)
    select = ((bin_of // NDIR)[:, :, None] == jnp.arange(group_speed.shape[0], dtype=jnp.int32)).astype(jnp.float32)
    speed = jnp.sum(select * group_speed, axis=2)
    wave = jnp.concatenate([east, north, speed])

    block_shapes = [shape_of(row_count, slots)] * BLOCKS
    full_shape = shape_of(rows, LANES)
    sums = [pltpu.VMEM((rows, LANES), jnp.float32)] * (3 * GROUPS)
    squares = pltpu.VMEM((4, LANES, LANES), jnp.float32)
    stages = pltpu.VMEM((BLOCKS, ghost_rows, LANES), jnp.float32)
    moved = 4 * LANES * own_rows

    full, *outs = pl.pallas_call(
        functools.partial(enter_kernel, sub, lanes),
        out_shape=[full_shape] + block_shapes,
        in_specs=[SM, VM],
        out_specs=[VM] * (1 + BLOCKS),
        scratch_shapes=[squares, stages],
        cost_estimate=cost(0, 2 * moved),
        compiler_params=limit(4),
        name="enter",
    )(send, spectrum)
    pitch = 3 if shared else 3 * sub
    coef, weight = pl.pallas_call(
        functools.partial(slope_kernel, sub, shared),
        out_shape=[shape_of(elements * pitch, LANES), shape_of(own_rows, LANES)],
        in_specs=[VM] * 3,
        out_specs=[VM] * 2,
        scratch_shapes=[pltpu.VMEM((LANES, elements), jnp.float32)],
        cost_estimate=cost(20 * elements * LANES, 4 * LANES * (elements * pitch + own_rows)),
        compiler_params=limit(4),
        name="slopes",
    )(normals, step_weight.reshape(1, owned), wave)

    for sweep_index in range(STEPS):
        again = sweep_index < STEPS - 1
        ghosts = [passed_along(outs[p], "dom", -offset_of(p)) for p in range(BLOCKS)]
        full, *returned = pl.pallas_call(
            functools.partial(sweep_kernel, sub, lanes, shared, own_rows),
            out_shape=[full_shape] + block_shapes,
            in_specs=[SM] + [VM] * (3 + BLOCKS),
            out_specs=[VM] * (1 + BLOCKS),
            input_output_aliases={3 + BLOCKS: 0},
            scratch_shapes=[squares, stages] + sums,
            cost_estimate=cost(elements * 24 * row_count, 4 * LANES * (3 * elements + 4 * rows)),
            compiler_params=limit(20),
            name="sweep",
        )(nodes, coef, weight, *ghosts, full)
        incoming = [passed_along(returned[p], "dom", offset_of(p)) for p in range(BLOCKS)]
        if again:
            full, *outs = pl.pallas_call(
                functools.partial(between_kernel, sub, lanes),
                out_shape=[full_shape] + block_shapes,
                in_specs=[SM] + [VM] * (2 + BLOCKS),
                out_specs=[VM] * (1 + BLOCKS),
                input_output_aliases={2 + BLOCKS: 0},
                scratch_shapes=[squares, stages],
                cost_estimate=cost(2 * owned * row_count, 4 * moved),
                compiler_params=limit(4),
                name="between",
            )(send, weight, *incoming, full)

    _, *blocks = pl.pallas_call(
        functools.partial(leave_kernel, sub, lanes, halves, spec_count),
        out_shape=[full_shape] + [shape_of(row_count * halves, LANES)] * spec_count,
        in_specs=[SM] * 2 + [VM] * (2 + BLOCKS),
        out_specs=[VM] * (1 + spec_count),
        input_output_aliases={3 + BLOCKS: 0},
        scratch_shapes=[squares, stages],
        cost_estimate=cost(2 * owned * row_count, 4 * moved),
        compiler_params=limit(4),
        name="leave",
    )(place, send, weight, *incoming, full)
    pieces = [blocks[0]] + [passed_along(blocks[d], "spec", d) for d in range(1, spec_count)]
    return pl.pallas_call(
        functools.partial(interact_kernel, halves, spec_count),
        out_shape=shape_of(bins, halves * LANES),
        in_specs=[SM] * 4 + [VM] * spec_count,
        out_specs=VM,
        scratch_shapes=[pltpu.VMEM((bins * halves, LANES), jnp.float32)] * (2 + 2 * GROUPS),
        cost_estimate=cost(16 * bins * halves * LANES, 8 * bins * halves * LANES),
        compiler_params=limit(12),
        name="interact",
    )(place, dia_plus * halves, dia_minus * halves, dia_coeff, *pieces)


def solution(mesh):
    in_specs = (
        P("spec", "dom"),
        P(None, None, "dom"),
        P(None, "dom"),
        P("dom", None, None),
        P("dom"),
        P(),
        P(),
        P(),
        P(),
    )
    out_specs = P(None, ("dom", "spec"))
    return jax.shard_map(
        on_device, mesh=mesh, in_specs=in_specs, out_specs=out_specs, check_vma=False
    )
```

```python
import functools
import math

import jax
import jax.numpy as jnp
from jax import lax
from jax.experimental import pallas as pl
from jax.experimental.pallas import tpu as pltpu
from jax.sharding import PartitionSpec as P


NDIR = 36
REACH = 2
STEPS = 2
BLOCKS = 2 * REACH
LANES = 128
GROUPS = 2


weight_plus = 1.25 ** (-4)
weight_minus = 0.75 ** (-4)
weight_both = 0.9375 ** (-4)

VM = pl.BlockSpec(memory_space=pltpu.VMEM)
SM = pl.BlockSpec(memory_space=pltpu.SMEM)


def offset_of(position):
    return position - REACH if position < REACH else position - REACH + 1


def passed_along(value, axis, steps):
    count = lax.axis_size(axis)
    return lax.ppermute(value, axis, [(source, (source + steps) % count) for source in range(count)])


def chunked(total, limit):
    return max(size for size in range(1, limit + 1) if total % size == 0)


def rows_to_block(sub, lanes, stage, block, start=0):
    for column in range(block.shape[1] // LANES):
        for part in range(block.shape[0] // lanes):
            tile = stage[pl.ds(column * LANES * sub + start + part, LANES, stride=sub), :].T
            block[part * lanes : (part + 1) * lanes, column * LANES : (column + 1) * LANES] = tile[:lanes]


def block_to_rows(sub, lanes, block, square, rows, first):
    for column in range(block.shape[1] // LANES):
        for part in range(sub):
            slot = square.at[(column * sub + part) % square.shape[0]]
            slot[:lanes, :] = block[part * lanes : (part + 1) * lanes, column * LANES : (column + 1) * LANES]
            rows[pl.ds(first + column * LANES * sub + part, LANES, stride=sub), :] = slot[...].T


def pack_rows(sub, lanes, send, energy, stages, outs):
    slots = outs[0].shape[1]
    unroll = chunked(slots, 32)
    for position in range(BLOCKS):
        stage = stages.at[position]

        @pl.loop(0, slots // unroll)
        def _(k):
            first = k * unroll
            listed = send.at[pl.ds((BLOCKS - 1 - position) * slots + first, unroll)]
            for u in range(unroll):
                stage[pl.ds((first + u) * sub, sub), :] = energy[pl.ds(listed[u], sub), :]

        rows_to_block(sub, lanes, stage, outs[position])


def enter_kernel(sub, lanes, send, spectrum, full, *rest):
    outs, square, stages = rest[:BLOCKS], rest[BLOCKS], rest[BLOCKS + 1]
    square[...] = jnp.zeros_like(square)
    block_to_rows(sub, lanes, spectrum, square, full, 0)
    pack_rows(sub, lanes, send, full, stages, outs)


def clear(items):
    rows = items[0].shape[0]
    step = chunked(rows, 64)
    zero = jnp.zeros((step, LANES), jnp.float32)

    @pl.loop(0, rows // step)
    def _(k):
        for item in items:
            item[pl.ds(pl.multiple_of(k * step, step), step), :] = zero


def slope_kernel(sub, shared, normals, step_weight, wave, coef, weight, lines):
    elements = normals.shape[2]
    parts = 1 if shared else sub
    plane = elements * parts
    lines[...] = jnp.zeros_like(lines)
    for component in range(2):
        for corner in range(2):
            row = component * 2 + corner
            lines[row : row + 1, :] = normals[component, corner : corner + 1, :]

    def spread(column):
        return jnp.broadcast_to(column, (8, LANES))

    @pl.loop(0, elements // LANES)
    def _(k):
        turned = lines[:, pl.ds(pl.multiple_of(k * LANES, LANES), LANES)].T
        for group in range(LANES // 8):
            at = slice(group * 8, group * 8 + 8)
            x0, x1, y0, y1 = (spread(turned[at, j : j + 1]) for j in range(4))
            base = (k * LANES + group * 8) * parts
            for part in range(parts):
                east, north = wave[part : part + 1, :], wave[sub + part : sub + part + 1, :]
                first = x0 * east + y0 * north
                second = x1 * east + y1 * north
                inward = jnp.minimum(first, 0.0) + jnp.minimum(second, 0.0) - jnp.maximum(first + second, 0.0)
                for which, value in enumerate((first, second, 1.0 / inward)):
                    first_row = which * plane + base
                    if parts == 1:
                        coef[pl.ds(pl.multiple_of(first_row, 8), 8), :] = value
                    else:
                        coef[pl.ds(first_row + part, 8, stride=parts), :] = value

    nodes = step_weight.shape[1]
    for block in range(nodes // LANES):
        turned = jnp.broadcast_to(step_weight[0:1, block * LANES : (block + 1) * LANES], (8, LANES)).T
        for group in range(LANES // 8):
            value = spread(turned[group * 8 : group * 8 + 8, 0:1])
            for part in range(sub):
                at = pl.ds((block * LANES + group * 8) * sub + part, 8, stride=sub)
                weight[at, :] = value * wave[2 * sub + part : 2 * sub + part + 1, :]


def total(sums, at):
    result = sums[0][at, :]
    for item in sums[1:]:
        result = result + item[at, :]
    return result


def sweep_kernel(sub, groups, lanes, shared, own_rows, conn, coef, weight, *rest):
    ghosts, full, rest = rest[:BLOCKS], rest[BLOCKS + 1], rest[BLOCKS + 2 :]
    returned, rest = rest[: BLOCKS * len(groups)], rest[BLOCKS * len(groups) :]
    square, stages, sums = rest[0], rest[1], rest[2:]
    clear(sums)
    ghost_rows = (full.shape[0] - own_rows) // BLOCKS
    elements = conn.shape[0] // 3
    parts = 1 if shared else sub
    square[...] = jnp.zeros_like(square)
    for position in range(BLOCKS):
        block_to_rows(sub, lanes, ghosts[position], square, full, own_rows + position * ghost_rows)

    share = elements // GROUPS
    unroll = chunked(share, 16)

    @pl.loop(0, share // unroll)
    def _(k):
        listed = [
            [conn.at[pl.ds(corner * elements + group * share + k * unroll, unroll)] for corner in range(3)]
            for group in range(GROUPS)
        ]
        for u in range(unroll):
            for group in range(GROUPS):
                element = group * share + k * unroll + u
                index = [item[u] for item in listed[group]]
                value = [full[pl.ds(row, sub), :] for row in index]
                first, second, inverse = (
                    jnp.broadcast_to(coef[pl.ds((j * elements + element) * parts, parts), :], (sub, LANES))
                    for j in range(3)
                )
                both = first + second
                inflow = jnp.minimum(first, 0.0) * value[0] + jnp.minimum(second, 0.0) * value[1]
                inflow = (inflow - jnp.maximum(both, 0.0) * value[2]) * inverse
                residual = (
                    jnp.maximum(first, 0.0) * (value[0] - inflow),
                    jnp.maximum(second, 0.0) * (value[1] - inflow),
                    jnp.minimum(both, 0.0) * (inflow - value[2]),
                )
                for corner in range(3):
                    item = sums[group * 3 + corner]
                    at = pl.ds(index[corner], sub)
                    item[at, :] = item[at, :] + residual[corner]

    step = chunked(ghost_rows, 64)
    for position in range(BLOCKS):
        stage = stages.at[position]

        @pl.loop(0, ghost_rows // step)
        def _(k):
            at = pl.multiple_of(k * step, step)
            stage[pl.ds(at, step), :] = total(sums, pl.ds(own_rows + position * ghost_rows + at, step))

    for which, (start, _) in enumerate(groups):
        for position in range(BLOCKS):
            rows_to_block(sub, lanes, stages.at[position], returned[which * BLOCKS + position], start)

    own_step = chunked(own_rows, 64)

    @pl.loop(0, own_rows // own_step)
    def _(k):
        at = pl.ds(pl.multiple_of(k * own_step, own_step), own_step)
        full[at, :] = full[at, :] - weight[at, :] * total(sums, at)


def add_returned(parts, lanes, send, weight, incoming, square, stages, full):
    start, size = parts
    slots = incoming[0].shape[1]
    square[...] = jnp.zeros_like(square)
    unroll = chunked(slots, 16)
    for position in range(BLOCKS):
        block_to_rows(size, lanes, incoming[position], square, stages.at[position], 0)
    for position in range(BLOCKS):
        stage = stages.at[position]

        @pl.loop(0, slots // unroll)
        def _(k):
            first = k * unroll
            listed = send.at[pl.ds((BLOCKS - 1 - position) * slots + first, unroll)]
            rows = [pl.ds(listed[u] + start, size) for u in range(unroll)]
            fresh = [
                full[row, :] - weight[row, :] * stage[pl.ds((first + u) * size, size), :]
                for u, row in enumerate(rows)
            ]
            for row, item in zip(rows, fresh):
                full[row, :] = item


def between_kernel(sub, lanes, send, weight, *rest):
    incoming, rest = rest[:BLOCKS], rest[BLOCKS + 1 :]
    full, outs, square, stages = rest[0], rest[1 : 1 + BLOCKS], rest[1 + BLOCKS], rest[2 + BLOCKS]
    add_returned((0, sub), lanes, send, weight, incoming, square, stages, full)
    pack_rows(sub, lanes, send, full, stages, outs)


def leave_kernel(sub, parts, lanes, halves, count, place, send, weight, *rest):
    incoming, rest = rest[:BLOCKS], rest[BLOCKS + 1 :]
    full, outs, square, stages = rest[0], rest[1 : 1 + count], rest[1 + count], rest[2 + count]
    add_returned(parts, lanes, send, weight, incoming, square, stages, full)
    start, size = parts
    for distance in range(count):
        target = lax.rem(place[0] + distance, count)
        for half in range(halves):
            first = (target * halves + half) * LANES * sub + start
            for part in range(size):
                tile = full[pl.ds(first + part, LANES, stride=sub), :].T
                outs[distance][pl.ds(part * lanes * halves + half, lanes, stride=halves), :] = tile[:lanes]


def interact_kernel(per_source, halves, count, starts, place, plus, minus, rate, *rest):
    pieces, rest = rest[: count * len(starts)], rest[count * len(starts) :]
    target, energy, kept, added, out, done = rest[0], rest[1], rest[2], rest[3:-2], rest[-2], rest[-1]
    clear(added)
    for which, start in enumerate(starts):
        for distance in range(count):
            piece = pieces[which * count + distance]
            first = lax.rem(place[0] + count - distance, count) * per_source + start
            if per_source % 8 == 0 and start % 8 == 0:
                first = pl.multiple_of(first, 8)
            energy[pl.ds(first, piece.shape[0]), :] = piece[...]
    bins = plus.shape[0]
    share = bins // GROUPS
    unroll = chunked(share, 12)

    @pl.loop(0, share // unroll)
    def _(k):
        for u in range(unroll):
            for group in range(GROUPS):
                index = group * share + k * unroll + u
                up, down = plus[index], minus[index]
                here = pl.ds(index * halves, halves)
                own = energy[here, :]
                upper = energy[pl.ds(up, halves), :]
                lower = energy[pl.ds(down, halves), :]
                term = rate[index] * (
                    own * own * (weight_plus * upper + weight_minus * lower)
                    - 2.0 * weight_both * own * upper * lower
                )
                kept[here, :] = own - 2.0 * term
                for item, row in zip(added[2 * group :], (up, down)):
                    item[pl.ds(row, halves), :] = item[pl.ds(row, halves), :] + term

    copies = done.shape[0]
    share = bins // copies
    step = chunked(share, 48)
    for which in range(copies):

        @pl.loop(which * share // step, (which + 1) * share // step)
        def _(k):
            for half in range(halves):
                at = pl.ds(k * step * halves + half, step, stride=halves)
                result = kept[at, :] + total(added, at)
                out[pl.ds(pl.multiple_of(k * step, step), step), half * LANES : (half + 1) * LANES] = result

        at = pl.ds(which * share, share)
        pltpu.make_async_copy(out.at[at], target.at[at], done.at[which]).start()
    for which in range(copies):
        at = pl.ds(which * share, share)
        pltpu.make_async_copy(out.at[at], target.at[at], done.at[which]).wait()


def shape_of(*dims):
    return jax.ShapeDtypeStruct(dims, jnp.float32)


def cost(flops, moved):
    return pl.CostEstimate(flops=flops, bytes_accessed=moved, transcendentals=0)


def limit(mebibytes):
    return pltpu.CompilerParams(vmem_limit_bytes=mebibytes << 20)


def on_device(
    spectrum, normals, conn, send_nodes, step_weight, group_speed, dia_plus, dia_minus, dia_coeff
):
    row_count, owned = spectrum.shape
    slots = send_nodes.shape[2]
    elements = conn.shape[1]
    bins = dia_plus.shape[0]
    spec_count = lax.axis_size("spec")
    sub = -(-row_count // LANES)
    while row_count % sub:
        sub += 1
    lanes = row_count // sub
    shared = lanes % NDIR == 0
    own_rows = owned * sub
    ghost_rows = slots * sub
    rows = own_rows + BLOCKS * ghost_rows
    halves = owned // (spec_count * LANES)

    send = (send_nodes[0] * sub).reshape(-1)
    nodes = (conn * sub).reshape(-1)
    place = lax.axis_index("spec").reshape(1)

    bin_of = (
        lax.axis_index("spec") * row_count
        + jnp.arange(sub, dtype=jnp.int32)[:, None] * lanes
        + jnp.arange(LANES, dtype=jnp.int32)[None, :]
    )
    angle = (bin_of % NDIR).astype(jnp.float32) * (2.0 * math.pi / NDIR)
    east, north = jnp.cos(angle), jnp.sin(angle)
    select = ((bin_of // NDIR)[:, :, None] == jnp.arange(group_speed.shape[0], dtype=jnp.int32)).astype(jnp.float32)
    speed = jnp.sum(select * group_speed, axis=2)
    wave = jnp.concatenate([east, north, speed])

    def blocks_of(groups):
        return [shape_of(size * lanes, slots) for _, size in groups for _ in range(BLOCKS)]

    whole = ((0, sub),)
    block_shapes = blocks_of(whole)
    full_shape = shape_of(rows, LANES)
    sums = [pltpu.VMEM((rows, LANES), jnp.float32)] * (3 * GROUPS)
    squares = pltpu.VMEM((4, LANES, LANES), jnp.float32)
    stages = pltpu.VMEM((BLOCKS, ghost_rows, LANES), jnp.float32)
    moved = 4 * LANES * own_rows

    full, *outs = pl.pallas_call(
        functools.partial(enter_kernel, sub, lanes),
        out_shape=[full_shape] + block_shapes,
        in_specs=[SM, VM],
        out_specs=[VM] * (1 + BLOCKS),
        scratch_shapes=[squares, stages],
        cost_estimate=cost(0, 2 * moved),
        compiler_params=limit(4),
        name="enter",
    )(send, spectrum)
    pitch = 3 if shared else 3 * sub
    coef, weight = pl.pallas_call(
        functools.partial(slope_kernel, sub, shared),
        out_shape=[shape_of(elements * pitch, LANES), shape_of(own_rows, LANES)],
        in_specs=[VM] * 3,
        out_specs=[VM] * 2,
        scratch_shapes=[pltpu.VMEM((LANES, elements), jnp.float32)],
        cost_estimate=cost(20 * elements * LANES, 4 * LANES * (elements * pitch + own_rows)),
        compiler_params=limit(4),
        name="slopes",
    )(normals, step_weight.reshape(1, owned), wave)

    for sweep_index in range(STEPS):
        again = sweep_index < STEPS - 1
        groups = whole if again or sub == 1 else ((0, 1), (1, sub - 1))
        ghosts = [passed_along(outs[p], "dom", -offset_of(p)) for p in range(BLOCKS)]
        full, *returned = pl.pallas_call(
            functools.partial(sweep_kernel, sub, groups, lanes, shared, own_rows),
            out_shape=[full_shape] + blocks_of(groups),
            in_specs=[SM] + [VM] * (3 + BLOCKS),
            out_specs=[VM] * (1 + BLOCKS * len(groups)),
            input_output_aliases={3 + BLOCKS: 0},
            scratch_shapes=[squares, stages] + sums,
            cost_estimate=cost(elements * 24 * row_count, 4 * LANES * (3 * elements + 4 * rows)),
            compiler_params=limit(20),
            name="sweep",
        )(nodes, coef, weight, *ghosts, full)
        incoming = []
        for p, item in enumerate(returned):
            incoming.append(passed_along(item, "dom", offset_of(p % BLOCKS)))
        if again:
            full, *outs = pl.pallas_call(
                functools.partial(between_kernel, sub, lanes),
                out_shape=[full_shape] + block_shapes,
                in_specs=[SM] + [VM] * (2 + BLOCKS),
                out_specs=[VM] * (1 + BLOCKS),
                input_output_aliases={2 + BLOCKS: 0},
                scratch_shapes=[squares, stages],
                cost_estimate=cost(2 * owned * row_count, 4 * moved),
                compiler_params=limit(4),
                name="between",
            )(send, weight, *incoming, full)

    pieces = []
    for which, (start, size) in enumerate(groups):
        full, *blocks = pl.pallas_call(
            functools.partial(leave_kernel, sub, (start, size), lanes, halves, spec_count),
            out_shape=[full_shape] + [shape_of(size * lanes * halves, LANES)] * spec_count,
            in_specs=[SM] * 2 + [VM] * (2 + BLOCKS),
            out_specs=[VM] * (1 + spec_count),
            input_output_aliases={3 + BLOCKS: 0},
            scratch_shapes=[squares, stages],
            cost_estimate=cost(2 * owned * size * LANES, 3 * moved * size // sub),
            compiler_params=limit(4),
        )(place, send, weight, *incoming[which * BLOCKS : (which + 1) * BLOCKS], full)
        pieces += [blocks[0]] + [passed_along(blocks[d], "spec", d) for d in range(1, spec_count)]
    return pl.pallas_call(
        functools.partial(interact_kernel, row_count * halves, halves, spec_count, [s * lanes * halves for s, _ in groups]),
        out_shape=shape_of(bins, halves * LANES),
        in_specs=[SM] * 4 + [VM] * len(pieces),
        out_specs=pl.BlockSpec(memory_space=pl.ANY),
        scratch_shapes=[pltpu.VMEM((bins * halves, LANES), jnp.float32)] * (2 + 2 * GROUPS)
        + [pltpu.VMEM((bins, halves * LANES), jnp.float32), pltpu.SemaphoreType.DMA((chunked(bins // 48, 4),))],
        cost_estimate=cost(16 * bins * halves * LANES, 8 * bins * halves * LANES),
        compiler_params=limit(12),
        name="interact",
    )(place, dia_plus * halves, dia_minus * halves, dia_coeff, *pieces)


def solution(mesh):
    in_specs = (
        P("spec", "dom"),
        P(None, None, "dom"),
        P(None, "dom"),
        P("dom", None, None),
        P("dom"),
        P(),
        P(),
        P(),
        P(),
    )
    out_specs = P(None, ("dom", "spec"))
    return jax.shard_map(
        on_device, mesh=mesh, in_specs=in_specs, out_specs=out_specs, check_vma=False
    )
```

```python
import functools
import math

import jax
import jax.numpy as jnp
from jax import lax
from jax.experimental import pallas as pl
from jax.experimental.pallas import tpu as pltpu
from jax.sharding import PartitionSpec as P


NDIR = 36
REACH = 2
STEPS = 2
BLOCKS = 2 * REACH
LANES = 128
GROUPS = 2


weight_plus = 1.25 ** (-4)
weight_minus = 0.75 ** (-4)
weight_both = 0.9375 ** (-4)

VM = pl.BlockSpec(memory_space=pltpu.VMEM)
SM = pl.BlockSpec(memory_space=pltpu.SMEM)


def offset_of(position):
    return position - REACH if position < REACH else position - REACH + 1


def passed_along(value, axis, steps):
    count = lax.axis_size(axis)
    return lax.ppermute(value, axis, [(source, (source + steps) % count) for source in range(count)])


def chunked(total, limit):
    return max(size for size in range(1, limit + 1) if total % size == 0)


def rows_to_block(sub, lanes, stage, block, start=0):
    for column in range(block.shape[1] // LANES):
        for part in range(block.shape[0] // lanes):
            tile = stage[pl.ds(column * LANES * sub + start + part, LANES, stride=sub), :].T
            block[part * lanes : (part + 1) * lanes, column * LANES : (column + 1) * LANES] = tile[:lanes]


def block_to_rows(sub, lanes, block, square, rows, first, start=0):
    for column in range(block.shape[1] // LANES):
        for part in range(block.shape[0] // lanes):
            slot = square.at[(column * sub + part) % square.shape[0]]
            slot[:lanes, :] = block[part * lanes : (part + 1) * lanes, column * LANES : (column + 1) * LANES]
            rows[pl.ds(first + column * LANES * sub + start + part, LANES, stride=sub), :] = slot[...].T


def pack_rows(parts, lanes, send, full, stages, outs):
    start, size = parts
    slots = outs[0].shape[1]
    unroll = chunked(slots, 32)
    for position in range(BLOCKS):
        stage = stages.at[position]

        @pl.loop(0, slots // unroll)
        def _(k):
            first = k * unroll
            listed = send.at[pl.ds((BLOCKS - 1 - position) * slots + first, unroll)]
            for u in range(unroll):
                stage[pl.ds((first + u) * size, size), :] = full[pl.ds(listed[u] + start, size), :]

    for position in range(BLOCKS):
        rows_to_block(size, lanes, stages.at[position], outs[position])


def enter_kernel(sub, lanes, send, spectrum, full, *rest):
    outs, square, stages = rest[:BLOCKS], rest[BLOCKS], rest[BLOCKS + 1]
    square[...] = jnp.zeros_like(square)
    block_to_rows(sub, lanes, spectrum, square, full, 0)
    pack_rows((0, sub), lanes, send, full, stages, outs)


def clear(items):
    rows = items[0].shape[0]
    step = chunked(rows, 64)
    zero = jnp.zeros((step, LANES), jnp.float32)

    @pl.loop(0, rows // step)
    def _(k):
        for item in items:
            item[pl.ds(pl.multiple_of(k * step, step), step), :] = zero


def slope_kernel(sub, shared, normals, step_weight, wave, coef, weight, lines):
    elements = normals.shape[2]
    parts = 1 if shared else sub
    plane = elements * parts
    lines[...] = jnp.zeros_like(lines)
    for component in range(2):
        for corner in range(2):
            row = component * 2 + corner
            lines[row : row + 1, :] = normals[component, corner : corner + 1, :]

    def spread(column):
        return jnp.broadcast_to(column, (8, LANES))

    @pl.loop(0, elements // LANES)
    def _(k):
        turned = lines[:, pl.ds(pl.multiple_of(k * LANES, LANES), LANES)].T
        for group in range(LANES // 8):
            at = slice(group * 8, group * 8 + 8)
            x0, x1, y0, y1 = (spread(turned[at, j : j + 1]) for j in range(4))
            base = (k * LANES + group * 8) * parts
            for part in range(parts):
                east, north = wave[part : part + 1, :], wave[sub + part : sub + part + 1, :]
                first = x0 * east + y0 * north
                second = x1 * east + y1 * north
                inward = jnp.minimum(first, 0.0) + jnp.minimum(second, 0.0) - jnp.maximum(first + second, 0.0)
                for which, value in enumerate((first, second, 1.0 / inward)):
                    first_row = which * plane + base
                    if parts == 1:
                        coef[pl.ds(pl.multiple_of(first_row, 8), 8), :] = value
                    else:
                        coef[pl.ds(first_row + part, 8, stride=parts), :] = value

    nodes = step_weight.shape[1]
    for block in range(nodes // LANES):
        turned = jnp.broadcast_to(step_weight[0:1, block * LANES : (block + 1) * LANES], (8, LANES)).T
        for group in range(LANES // 8):
            value = spread(turned[group * 8 : group * 8 + 8, 0:1])
            for part in range(sub):
                at = pl.ds((block * LANES + group * 8) * sub + part, 8, stride=sub)
                weight[at, :] = value * wave[2 * sub + part : 2 * sub + part + 1, :]


def total(sums, at):
    result = sums[0][at, :]
    for item in sums[1:]:
        result = result + item[at, :]
    return result


def sweep_kernel(sub, inner, groups, lanes, shared, own_rows, conn, coef, weight, *rest):
    ghosts, rest = rest[: BLOCKS * len(inner)], rest[BLOCKS * len(inner) + 1 :]
    full, rest = rest[0], rest[1:]
    returned, rest = rest[: BLOCKS * len(groups)], rest[BLOCKS * len(groups) :]
    square, stages, sums = rest[0], rest[1], rest[2:]
    clear(sums)
    ghost_rows = (full.shape[0] - own_rows) // BLOCKS
    elements = conn.shape[0] // 3
    parts = 1 if shared else sub
    square[...] = jnp.zeros_like(square)
    for which, (start, _) in enumerate(inner):
        for position in range(BLOCKS):
            block = ghosts[which * BLOCKS + position]
            block_to_rows(sub, lanes, block, square, full, own_rows + position * ghost_rows, start)

    share = elements // GROUPS
    unroll = chunked(share, 16)

    @pl.loop(0, share // unroll)
    def _(k):
        listed = [
            [conn.at[pl.ds(corner * elements + group * share + k * unroll, unroll)] for corner in range(3)]
            for group in range(GROUPS)
        ]
        for u in range(unroll):
            for group in range(GROUPS):
                element = group * share + k * unroll + u
                index = [item[u] for item in listed[group]]
                value = [full[pl.ds(row, sub), :] for row in index]
                first, second, inverse = (
                    jnp.broadcast_to(coef[pl.ds((j * elements + element) * parts, parts), :], (sub, LANES))
                    for j in range(3)
                )
                both = first + second
                inflow = jnp.minimum(first, 0.0) * value[0] + jnp.minimum(second, 0.0) * value[1]
                inflow = (inflow - jnp.maximum(both, 0.0) * value[2]) * inverse
                residual = (
                    jnp.maximum(first, 0.0) * (value[0] - inflow),
                    jnp.maximum(second, 0.0) * (value[1] - inflow),
                    jnp.minimum(both, 0.0) * (inflow - value[2]),
                )
                for corner in range(3):
                    item = sums[group * 3 + corner]
                    at = pl.ds(index[corner], sub)
                    item[at, :] = item[at, :] + residual[corner]

    step = chunked(ghost_rows, 64)
    for position in range(BLOCKS):
        stage = stages.at[position]

        @pl.loop(0, ghost_rows // step)
        def _(k):
            at = pl.multiple_of(k * step, step)
            stage[pl.ds(at, step), :] = total(sums, pl.ds(own_rows + position * ghost_rows + at, step))

    for which, (start, _) in enumerate(groups):
        for position in range(BLOCKS):
            rows_to_block(sub, lanes, stages.at[position], returned[which * BLOCKS + position], start)

    own_step = chunked(own_rows, 64)

    @pl.loop(0, own_rows // own_step)
    def _(k):
        at = pl.ds(pl.multiple_of(k * own_step, own_step), own_step)
        full[at, :] = full[at, :] - weight[at, :] * total(sums, at)


def add_returned(parts, lanes, send, weight, incoming, square, stages, full):
    start, size = parts
    slots = incoming[0].shape[1]
    square[...] = jnp.zeros_like(square)
    unroll = chunked(slots, 16)
    for position in range(BLOCKS):
        block_to_rows(size, lanes, incoming[position], square, stages.at[position], 0)
    for position in range(BLOCKS):
        stage = stages.at[position]

        @pl.loop(0, slots // unroll)
        def _(k):
            first = k * unroll
            listed = send.at[pl.ds((BLOCKS - 1 - position) * slots + first, unroll)]
            rows = [pl.ds(listed[u] + start, size) for u in range(unroll)]
            fresh = [
                full[row, :] - weight[row, :] * stage[pl.ds((first + u) * size, size), :]
                for u, row in enumerate(rows)
            ]
            for row, item in zip(rows, fresh):
                full[row, :] = item


def between_kernel(parts, lanes, send, weight, *rest):
    incoming, rest = rest[:BLOCKS], rest[BLOCKS + 1 :]
    full, outs, square, stages = rest[0], rest[1 : 1 + BLOCKS], rest[1 + BLOCKS], rest[2 + BLOCKS]
    add_returned(parts, lanes, send, weight, incoming, square, stages, full)
    pack_rows(parts, lanes, send, full, stages, outs)


def leave_kernel(sub, parts, lanes, halves, count, place, send, weight, *rest):
    incoming, rest = rest[:BLOCKS], rest[BLOCKS + 1 :]
    full, outs, square, stages = rest[0], rest[1 : 1 + count], rest[1 + count], rest[2 + count]
    add_returned(parts, lanes, send, weight, incoming, square, stages, full)
    start, size = parts
    for distance in range(count):
        target = lax.rem(place[0] + distance, count)
        for half in range(halves):
            first = (target * halves + half) * LANES * sub + start
            for part in range(size):
                tile = full[pl.ds(first + part, LANES, stride=sub), :].T
                outs[distance][pl.ds(part * lanes * halves + half, lanes, stride=halves), :] = tile[:lanes]


def interact_kernel(per_source, halves, count, starts, place, plus, minus, rate, *rest):
    pieces, rest = rest[: count * len(starts)], rest[count * len(starts) :]
    target, energy, kept, added, out, done = rest[0], rest[1], rest[2], rest[3:-2], rest[-2], rest[-1]
    clear(added)
    for which, start in enumerate(starts):
        for distance in range(count):
            piece = pieces[which * count + distance]
            first = lax.rem(place[0] + count - distance, count) * per_source + start
            if per_source % 8 == 0 and start % 8 == 0:
                first = pl.multiple_of(first, 8)
            energy[pl.ds(first, piece.shape[0]), :] = piece[...]
    bins = plus.shape[0]
    share = bins // GROUPS
    unroll = chunked(share, 12)

    @pl.loop(0, share // unroll)
    def _(k):
        for u in range(unroll):
            for group in range(GROUPS):
                index = group * share + k * unroll + u
                up, down = plus[index], minus[index]
                here = pl.ds(index * halves, halves)
                own = energy[here, :]
                upper = energy[pl.ds(up, halves), :]
                lower = energy[pl.ds(down, halves), :]
                term = rate[index] * (
                    own * own * (weight_plus * upper + weight_minus * lower)
                    - 2.0 * weight_both * own * upper * lower
                )
                kept[here, :] = own - 2.0 * term
                for item, row in zip(added[2 * group :], (up, down)):
                    item[pl.ds(row, halves), :] = item[pl.ds(row, halves), :] + term

    copies = done.shape[0]
    share = bins // copies
    step = chunked(share, 48)
    for which in range(copies):

        @pl.loop(which * share // step, (which + 1) * share // step)
        def _(k):
            for half in range(halves):
                at = pl.ds(k * step * halves + half, step, stride=halves)
                result = kept[at, :] + total(added, at)
                out[pl.ds(pl.multiple_of(k * step, step), step), half * LANES : (half + 1) * LANES] = result

        at = pl.ds(which * share, share)
        pltpu.make_async_copy(out.at[at], target.at[at], done.at[which]).start()
    for which in range(copies):
        at = pl.ds(which * share, share)
        pltpu.make_async_copy(out.at[at], target.at[at], done.at[which]).wait()


def shape_of(*dims):
    return jax.ShapeDtypeStruct(dims, jnp.float32)


def cost(flops, moved):
    return pl.CostEstimate(flops=flops, bytes_accessed=moved, transcendentals=0)


def limit(mebibytes):
    return pltpu.CompilerParams(vmem_limit_bytes=mebibytes << 20)


def on_device(
    spectrum, normals, conn, send_nodes, step_weight, group_speed, dia_plus, dia_minus, dia_coeff
):
    row_count, owned = spectrum.shape
    slots = send_nodes.shape[2]
    elements = conn.shape[1]
    bins = dia_plus.shape[0]
    spec_count = lax.axis_size("spec")
    sub = -(-row_count // LANES)
    while row_count % sub:
        sub += 1
    lanes = row_count // sub
    shared = lanes % NDIR == 0
    own_rows = owned * sub
    ghost_rows = slots * sub
    rows = own_rows + BLOCKS * ghost_rows
    halves = owned // (spec_count * LANES)

    send = (send_nodes[0] * sub).reshape(-1)
    nodes = (conn * sub).reshape(-1)
    place = lax.axis_index("spec").reshape(1)

    bin_of = (
        lax.axis_index("spec") * row_count
        + jnp.arange(sub, dtype=jnp.int32)[:, None] * lanes
        + jnp.arange(LANES, dtype=jnp.int32)[None, :]
    )
    angle = (bin_of % NDIR).astype(jnp.float32) * (2.0 * math.pi / NDIR)
    east, north = jnp.cos(angle), jnp.sin(angle)
    select = ((bin_of // NDIR)[:, :, None] == jnp.arange(group_speed.shape[0], dtype=jnp.int32)).astype(jnp.float32)
    speed = jnp.sum(select * group_speed, axis=2)
    wave = jnp.concatenate([east, north, speed])

    def blocks_of(groups):
        return [shape_of(size * lanes, slots) for _, size in groups for _ in range(BLOCKS)]

    whole = ((0, sub),)
    block_shapes = blocks_of(whole)
    full_shape = shape_of(rows, LANES)
    sums = [pltpu.VMEM((rows, LANES), jnp.float32)] * (3 * GROUPS)
    squares = pltpu.VMEM((4, LANES, LANES), jnp.float32)
    stages = pltpu.VMEM((BLOCKS, ghost_rows, LANES), jnp.float32)
    moved = 4 * LANES * own_rows

    full, *outs = pl.pallas_call(
        functools.partial(enter_kernel, sub, lanes),
        out_shape=[full_shape] + block_shapes,
        in_specs=[SM, VM],
        out_specs=[VM] * (1 + BLOCKS),
        scratch_shapes=[squares, stages],
        cost_estimate=cost(0, 2 * moved),
        compiler_params=limit(4),
        name="enter",
    )(send, spectrum)
    pitch = 3 if shared else 3 * sub
    coef, weight = pl.pallas_call(
        functools.partial(slope_kernel, sub, shared),
        out_shape=[shape_of(elements * pitch, LANES), shape_of(own_rows, LANES)],
        in_specs=[VM] * 3,
        out_specs=[VM] * 2,
        scratch_shapes=[pltpu.VMEM((LANES, elements), jnp.float32)],
        cost_estimate=cost(20 * elements * LANES, 4 * LANES * (elements * pitch + own_rows)),
        compiler_params=limit(4),
        name="slopes",
    )(normals, step_weight.reshape(1, owned), wave)

    groups = whole if sub == 1 else ((0, 1), (1, sub - 1))
    inner = whole
    for sweep_index in range(STEPS):
        ghosts = []
        for p, item in enumerate(outs):
            ghosts.append(passed_along(item, "dom", -offset_of(p % BLOCKS)))
        full, *returned = pl.pallas_call(
            functools.partial(sweep_kernel, sub, inner, groups, lanes, shared, own_rows),
            out_shape=[full_shape] + blocks_of(groups),
            in_specs=[SM] + [VM] * (3 + len(ghosts)),
            out_specs=[VM] * (1 + BLOCKS * len(groups)),
            input_output_aliases={3 + len(ghosts): 0},
            scratch_shapes=[squares, stages] + sums,
            cost_estimate=cost(elements * 24 * row_count, 4 * LANES * (3 * elements + 4 * rows)),
            compiler_params=limit(20),
            name="sweep",
        )(nodes, coef, weight, *ghosts, full)
        incoming = []
        for p, item in enumerate(returned):
            incoming.append(passed_along(item, "dom", offset_of(p % BLOCKS)))
        if sweep_index < STEPS - 1:
            outs, inner = [], groups
            for which, parts in enumerate(groups):
                full, *more = pl.pallas_call(
                    functools.partial(between_kernel, parts, lanes),
                    out_shape=[full_shape] + blocks_of((parts,)),
                    in_specs=[SM] + [VM] * (2 + BLOCKS),
                    out_specs=[VM] * (1 + BLOCKS),
                    input_output_aliases={2 + BLOCKS: 0},
                    scratch_shapes=[squares, stages],
                    cost_estimate=cost(2 * owned * parts[1] * LANES, 4 * moved * parts[1] // sub),
                    compiler_params=limit(4),
                )(send, weight, *incoming[which * BLOCKS : (which + 1) * BLOCKS], full)
                outs += more

    pieces = []
    for which, (start, size) in enumerate(groups):
        full, *blocks = pl.pallas_call(
            functools.partial(leave_kernel, sub, (start, size), lanes, halves, spec_count),
            out_shape=[full_shape] + [shape_of(size * lanes * halves, LANES)] * spec_count,
            in_specs=[SM] * 2 + [VM] * (2 + BLOCKS),
            out_specs=[VM] * (1 + spec_count),
            input_output_aliases={3 + BLOCKS: 0},
            scratch_shapes=[squares, stages],
            cost_estimate=cost(2 * owned * size * LANES, 3 * moved * size // sub),
            compiler_params=limit(4),
        )(place, send, weight, *incoming[which * BLOCKS : (which + 1) * BLOCKS], full)
        pieces += [blocks[0]] + [passed_along(blocks[d], "spec", d) for d in range(1, spec_count)]
    return pl.pallas_call(
        functools.partial(interact_kernel, row_count * halves, halves, spec_count, [s * lanes * halves for s, _ in groups]),
        out_shape=shape_of(bins, halves * LANES),
        in_specs=[SM] * 4 + [VM] * len(pieces),
        out_specs=pl.BlockSpec(memory_space=pl.ANY),
        scratch_shapes=[pltpu.VMEM((bins * halves, LANES), jnp.float32)] * (2 + 2 * GROUPS)
        + [pltpu.VMEM((bins, halves * LANES), jnp.float32), pltpu.SemaphoreType.DMA((chunked(bins // 48, 4),))],
        cost_estimate=cost(16 * bins * halves * LANES, 8 * bins * halves * LANES),
        compiler_params=limit(12),
        name="interact",
    )(place, dia_plus * halves, dia_minus * halves, dia_coeff, *pieces)


def solution(mesh):
    in_specs = (
        P("spec", "dom"),
        P(None, None, "dom"),
        P(None, "dom"),
        P("dom", None, None),
        P("dom"),
        P(),
        P(),
        P(),
        P(),
    )
    out_specs = P(None, ("dom", "spec"))
    return jax.shard_map(
        on_device, mesh=mesh, in_specs=in_specs, out_specs=out_specs, check_vma=False
    )
```

```python
import functools
import math

import jax
import jax.numpy as jnp
from jax import lax
from jax.experimental import pallas as pl
from jax.experimental.pallas import tpu as pltpu
from jax.sharding import PartitionSpec as P


NDIR = 36
REACH = 2
STEPS = 2
BLOCKS = 2 * REACH
LANES = 128
GROUPS = 2


weight_plus = 1.25 ** (-4)
weight_minus = 0.75 ** (-4)
weight_both = 0.9375 ** (-4)

VM = pl.BlockSpec(memory_space=pltpu.VMEM)
SM = pl.BlockSpec(memory_space=pltpu.SMEM)


def offset_of(position):
    return position - REACH if position < REACH else position - REACH + 1


def passed_along(value, axis, steps):
    count = lax.axis_size(axis)
    return lax.ppermute(value, axis, [(source, (source + steps) % count) for source in range(count)])


def chunked(total, limit):
    return max(size for size in range(1, limit + 1) if total % size == 0)


def rows_to_block(sub, lanes, stage, block, start=0):
    for column in range(block.shape[1] // LANES):
        for part in range(block.shape[0] // lanes):
            tile = stage[pl.ds(column * LANES * sub + start + part, LANES, stride=sub), :].T
            block[part * lanes : (part + 1) * lanes, column * LANES : (column + 1) * LANES] = tile[:lanes]


def block_to_rows(sub, lanes, block, square, rows, first, start=0):
    for column in range(block.shape[1] // LANES):
        for part in range(block.shape[0] // lanes):
            slot = square.at[(column * sub + part) % square.shape[0]]
            slot[:lanes, :] = block[part * lanes : (part + 1) * lanes, column * LANES : (column + 1) * LANES]
            rows[pl.ds(first + column * LANES * sub + start + part, LANES, stride=sub), :] = slot[...].T


def pack_rows(parts, lanes, send, full, stages, outs):
    start, size = parts
    slots = outs[0].shape[1]
    unroll = chunked(slots, 32)
    for position in range(BLOCKS):
        stage = stages.at[position]

        @pl.loop(0, slots // unroll)
        def _(k):
            first = k * unroll
            listed = send.at[pl.ds((BLOCKS - 1 - position) * slots + first, unroll)]
            for u in range(unroll):
                stage[pl.ds((first + u) * size, size), :] = full[pl.ds(listed[u] + start, size), :]

    for position in range(BLOCKS):
        rows_to_block(size, lanes, stages.at[position], outs[position])


def enter_kernel(sub, lanes, send, spectrum, full, *rest):
    outs, square, stages = rest[:BLOCKS], rest[BLOCKS], rest[BLOCKS + 1]
    square[...] = jnp.zeros_like(square)
    block_to_rows(sub, lanes, spectrum, square, full, 0)
    pack_rows((0, sub), lanes, send, full, stages, outs)


def clear(items):
    rows = items[0].shape[0]
    step = chunked(rows, 64)
    zero = jnp.zeros((step, LANES), jnp.float32)

    @pl.loop(0, rows // step)
    def _(k):
        for item in items:
            item[pl.ds(pl.multiple_of(k * step, step), step), :] = zero


def slope_kernel(sub, shared, normals, step_weight, wave, coef, weight, lines):
    elements = normals.shape[2]
    parts = 1 if shared else sub
    plane = elements * parts
    lines[...] = jnp.zeros_like(lines)
    for component in range(2):
        for corner in range(2):
            row = component * 2 + corner
            lines[row : row + 1, :] = normals[component, corner : corner + 1, :]

    def spread(column):
        return jnp.broadcast_to(column, (8, LANES))

    @pl.loop(0, elements // LANES)
    def _(k):
        turned = lines[:, pl.ds(pl.multiple_of(k * LANES, LANES), LANES)].T
        for group in range(LANES // 8):
            at = slice(group * 8, group * 8 + 8)
            x0, x1, y0, y1 = (spread(turned[at, j : j + 1]) for j in range(4))
            base = (k * LANES + group * 8) * parts
            for part in range(parts):
                east, north = wave[part : part + 1, :], wave[sub + part : sub + part + 1, :]
                first = x0 * east + y0 * north
                second = x1 * east + y1 * north
                inward = jnp.minimum(first, 0.0) + jnp.minimum(second, 0.0) - jnp.maximum(first + second, 0.0)
                for which, value in enumerate((first, second, 1.0 / inward)):
                    first_row = which * plane + base
                    if parts == 1:
                        coef[pl.ds(pl.multiple_of(first_row, 8), 8), :] = value
                    else:
                        coef[pl.ds(first_row + part, 8, stride=parts), :] = value

    nodes = step_weight.shape[1]
    for block in range(nodes // LANES):
        turned = jnp.broadcast_to(step_weight[0:1, block * LANES : (block + 1) * LANES], (8, LANES)).T
        for group in range(LANES // 8):
            value = spread(turned[group * 8 : group * 8 + 8, 0:1])
            for part in range(sub):
                at = pl.ds((block * LANES + group * 8) * sub + part, 8, stride=sub)
                weight[at, :] = value * wave[2 * sub + part : 2 * sub + part + 1, :]


def total(sums, at):
    result = sums[0][at, :]
    for item in sums[1:]:
        result = result + item[at, :]
    return result


def sweep_kernel(sub, inner, groups, lanes, shared, own_rows, conn, coef, weight, *rest):
    ghosts, rest = rest[: BLOCKS * len(inner)], rest[BLOCKS * len(inner) + 1 :]
    full, rest = rest[0], rest[1:]
    returned, rest = rest[: BLOCKS * len(groups)], rest[BLOCKS * len(groups) :]
    square, stages, sums = rest[0], rest[1], rest[2:]
    clear(sums)
    ghost_rows = (full.shape[0] - own_rows) // BLOCKS
    elements = conn.shape[0] // 3
    parts = 1 if shared else sub
    square[...] = jnp.zeros_like(square)
    for which, (start, _) in enumerate(inner):
        for position in range(BLOCKS):
            block = ghosts[which * BLOCKS + position]
            block_to_rows(sub, lanes, block, square, full, own_rows + position * ghost_rows, start)

    share = elements // GROUPS
    unroll = chunked(share, 32)

    @pl.loop(0, share // unroll)
    def _(k):
        listed = [
            [conn.at[pl.ds(corner * elements + group * share + k * unroll, unroll)] for corner in range(3)]
            for group in range(GROUPS)
        ]
        for u in range(unroll):
            for group in range(GROUPS):
                element = group * share + k * unroll + u
                index = [item[u] for item in listed[group]]
                value = [full[pl.ds(row, sub), :] for row in index]
                first, second, inverse = (
                    jnp.broadcast_to(coef[pl.ds((j * elements + element) * parts, parts), :], (sub, LANES))
                    for j in range(3)
                )
                both = first + second
                inflow = jnp.minimum(first, 0.0) * value[0] + jnp.minimum(second, 0.0) * value[1]
                inflow = (inflow - jnp.maximum(both, 0.0) * value[2]) * inverse
                residual = (
                    jnp.maximum(first, 0.0) * (value[0] - inflow),
                    jnp.maximum(second, 0.0) * (value[1] - inflow),
                    jnp.minimum(both, 0.0) * (inflow - value[2]),
                )
                for corner in range(3):
                    item = sums[group * 3 + corner]
                    at = pl.ds(index[corner], sub)
                    item[at, :] = item[at, :] + residual[corner]

    step = chunked(ghost_rows, 64)
    for position in range(BLOCKS):
        stage = stages.at[position]

        @pl.loop(0, ghost_rows // step)
        def _(k):
            at = pl.multiple_of(k * step, step)
            stage[pl.ds(at, step), :] = total(sums, pl.ds(own_rows + position * ghost_rows + at, step))

    for which, (start, _) in enumerate(groups):
        for position in range(BLOCKS):
            rows_to_block(sub, lanes, stages.at[position], returned[which * BLOCKS + position], start)

    own_step = chunked(own_rows, 64)

    @pl.loop(0, own_rows // own_step)
    def _(k):
        at = pl.ds(pl.multiple_of(k * own_step, own_step), own_step)
        full[at, :] = full[at, :] - weight[at, :] * total(sums, at)


def add_returned(parts, lanes, send, weight, incoming, square, stages, full):
    start, size = parts
    slots = incoming[0].shape[1]
    square[...] = jnp.zeros_like(square)
    unroll = chunked(slots, 16)
    for position in range(BLOCKS):
        block_to_rows(size, lanes, incoming[position], square, stages.at[position], 0)
    for position in range(BLOCKS):
        stage = stages.at[position]

        @pl.loop(0, slots // unroll)
        def _(k):
            first = k * unroll
            listed = send.at[pl.ds((BLOCKS - 1 - position) * slots + first, unroll)]
            rows = [pl.ds(listed[u] + start, size) for u in range(unroll)]
            fresh = [
                full[row, :] - weight[row, :] * stage[pl.ds((first + u) * size, size), :]
                for u, row in enumerate(rows)
            ]
            for row, item in zip(rows, fresh):
                full[row, :] = item


def between_kernel(parts, lanes, send, weight, *rest):
    incoming, rest = rest[:BLOCKS], rest[BLOCKS + 1 :]
    full, outs, square, stages = rest[0], rest[1 : 1 + BLOCKS], rest[1 + BLOCKS], rest[2 + BLOCKS]
    add_returned(parts, lanes, send, weight, incoming, square, stages, full)
    pack_rows(parts, lanes, send, full, stages, outs)


def leave_kernel(sub, parts, lanes, halves, count, send, weight, *rest):
    incoming, rest = rest[:BLOCKS], rest[BLOCKS + 1 :]
    full, outs, square, stages = rest[0], rest[1 : 1 + count], rest[1 + count], rest[2 + count]
    add_returned(parts, lanes, send, weight, incoming, square, stages, full)
    start, size = parts
    place = send[send.shape[0] - 1]
    for distance in range(count):
        target = lax.rem(place + distance, count)
        for half in range(halves):
            first = (target * halves + half) * LANES * sub + start
            for part in range(size):
                tile = full[pl.ds(first + part, LANES, stride=sub), :].T
                outs[distance][pl.ds(part * lanes * halves + half, lanes, stride=halves), :] = tile[:lanes]


def interact_kernel(per_source, halves, count, starts, partner, rate, *rest):
    pieces, rest = rest[: count * len(starts)], rest[count * len(starts) :]
    target, energy, kept, added, out, done = rest[0], rest[1], rest[2], rest[3:-2], rest[-2], rest[-1]
    bins = rate.shape[0]
    place = partner[2 * bins]
    clear(added)
    for which, start in enumerate(starts):
        for distance in range(count):
            piece = pieces[which * count + distance]
            first = lax.rem(place + count - distance, count) * per_source + start
            if per_source % 8 == 0 and start % 8 == 0:
                first = pl.multiple_of(first, 8)
            energy[pl.ds(first, piece.shape[0]), :] = piece[...]
    share = bins // GROUPS
    unroll = chunked(share, 18)

    @pl.loop(0, share // unroll)
    def _(k):
        for u in range(unroll):
            for group in range(GROUPS):
                index = group * share + k * unroll + u
                up, down = partner[index], partner[bins + index]
                here = pl.ds(index * halves, halves)
                own = energy[here, :]
                upper = energy[pl.ds(up, halves), :]
                lower = energy[pl.ds(down, halves), :]
                term = rate[index] * (
                    own * own * (weight_plus * upper + weight_minus * lower)
                    - 2.0 * weight_both * own * upper * lower
                )
                kept[here, :] = own - 2.0 * term
                for item, row in zip(added[2 * group :], (up, down)):
                    item[pl.ds(row, halves), :] = item[pl.ds(row, halves), :] + term

    copies = done.shape[0]
    share = bins // copies
    step = chunked(share, 48)
    for which in range(copies):

        @pl.loop(which * share // step, (which + 1) * share // step)
        def _(k):
            for half in range(halves):
                at = pl.ds(k * step * halves + half, step, stride=halves)
                result = kept[at, :] + total(added, at)
                out[pl.ds(pl.multiple_of(k * step, step), step), half * LANES : (half + 1) * LANES] = result

        at = pl.ds(which * share, share)
        pltpu.make_async_copy(out.at[at], target.at[at], done.at[which]).start()
    for which in range(copies):
        at = pl.ds(which * share, share)
        pltpu.make_async_copy(out.at[at], target.at[at], done.at[which]).wait()


def shape_of(*dims):
    return jax.ShapeDtypeStruct(dims, jnp.float32)


def cost(flops, moved):
    return pl.CostEstimate(flops=flops, bytes_accessed=moved, transcendentals=0)


def limit(mebibytes):
    return pltpu.CompilerParams(vmem_limit_bytes=mebibytes << 20)


def on_device(
    spectrum, normals, conn, send_nodes, step_weight, group_speed, dia_plus, dia_minus, dia_coeff
):
    row_count, owned = spectrum.shape
    slots = send_nodes.shape[2]
    elements = conn.shape[1]
    bins = dia_plus.shape[0]
    spec_count = lax.axis_size("spec")
    sub = -(-row_count // LANES)
    while row_count % sub:
        sub += 1
    lanes = row_count // sub
    shared = lanes % NDIR == 0
    own_rows = owned * sub
    ghost_rows = slots * sub
    rows = own_rows + BLOCKS * ghost_rows
    halves = owned // (spec_count * LANES)

    nodes = (conn * sub).reshape(-1)
    place = lax.axis_index("spec").reshape(1)
    send = (send_nodes[0] * sub).reshape(-1)
    listing = jnp.concatenate([send, place])

    bin_of = (
        lax.axis_index("spec") * row_count
        + jnp.arange(sub, dtype=jnp.int32)[:, None] * lanes
        + jnp.arange(LANES, dtype=jnp.int32)[None, :]
    )
    angle = (bin_of % NDIR).astype(jnp.float32) * (2.0 * math.pi / NDIR)
    east, north = jnp.cos(angle), jnp.sin(angle)
    select = ((bin_of // NDIR)[:, :, None] == jnp.arange(group_speed.shape[0], dtype=jnp.int32)).astype(jnp.float32)
    speed = jnp.sum(select * group_speed, axis=2)
    wave = jnp.concatenate([east, north, speed])

    def blocks_of(groups):
        return [shape_of(size * lanes, slots) for _, size in groups for _ in range(BLOCKS)]

    whole = ((0, sub),)
    block_shapes = blocks_of(whole)
    full_shape = shape_of(rows, LANES)
    sums = [pltpu.VMEM((rows, LANES), jnp.float32)] * (3 * GROUPS)
    squares = pltpu.VMEM((4, LANES, LANES), jnp.float32)
    stages = pltpu.VMEM((BLOCKS, ghost_rows, LANES), jnp.float32)
    moved = 4 * LANES * own_rows

    full, *outs = pl.pallas_call(
        functools.partial(enter_kernel, sub, lanes),
        out_shape=[full_shape] + block_shapes,
        in_specs=[SM, VM],
        out_specs=[VM] * (1 + BLOCKS),
        scratch_shapes=[squares, stages],
        cost_estimate=cost(0, 2 * moved),
        compiler_params=limit(4),
        name="enter",
    )(send, spectrum)
    pitch = 3 if shared else 3 * sub
    coef, weight = pl.pallas_call(
        functools.partial(slope_kernel, sub, shared),
        out_shape=[shape_of(elements * pitch, LANES), shape_of(own_rows, LANES)],
        in_specs=[VM] * 3,
        out_specs=[VM] * 2,
        scratch_shapes=[pltpu.VMEM((LANES, elements), jnp.float32)],
        cost_estimate=cost(20 * elements * LANES, 4 * LANES * (elements * pitch + own_rows)),
        compiler_params=limit(4),
        name="slopes",
    )(normals, step_weight.reshape(1, owned), wave)

    groups = whole if sub == 1 else ((0, 1), (1, sub - 1))
    inner = whole
    for sweep_index in range(STEPS):
        ghosts = []
        for p, item in enumerate(outs):
            ghosts.append(passed_along(item, "dom", -offset_of(p % BLOCKS)))
        full, *returned = pl.pallas_call(
            functools.partial(sweep_kernel, sub, inner, groups, lanes, shared, own_rows),
            out_shape=[full_shape] + blocks_of(groups),
            in_specs=[SM] + [VM] * (3 + len(ghosts)),
            out_specs=[VM] * (1 + BLOCKS * len(groups)),
            input_output_aliases={3 + len(ghosts): 0},
            scratch_shapes=[squares, stages] + sums,
            cost_estimate=cost(elements * 24 * row_count, 4 * LANES * (3 * elements + 4 * rows)),
            compiler_params=limit(20),
            name="sweep",
        )(nodes, coef, weight, *ghosts, full)
        incoming = []
        for p, item in enumerate(returned):
            incoming.append(passed_along(item, "dom", offset_of(p % BLOCKS)))
        if sweep_index < STEPS - 1:
            outs, inner = [], groups
            for which, parts in enumerate(groups):
                full, *more = pl.pallas_call(
                    functools.partial(between_kernel, parts, lanes),
                    out_shape=[full_shape] + blocks_of((parts,)),
                    in_specs=[SM] + [VM] * (2 + BLOCKS),
                    out_specs=[VM] * (1 + BLOCKS),
                    input_output_aliases={2 + BLOCKS: 0},
                    scratch_shapes=[squares, stages],
                    cost_estimate=cost(2 * owned * parts[1] * LANES, 4 * moved * parts[1] // sub),
                    compiler_params=limit(4),
                )(send, weight, *incoming[which * BLOCKS : (which + 1) * BLOCKS], full)
                outs += more

    pieces = []
    for which, (start, size) in enumerate(groups):
        full, *blocks = pl.pallas_call(
            functools.partial(leave_kernel, sub, (start, size), lanes, halves, spec_count),
            out_shape=[full_shape] + [shape_of(size * lanes * halves, LANES)] * spec_count,
            in_specs=[SM] + [VM] * (2 + BLOCKS),
            out_specs=[VM] * (1 + spec_count),
            input_output_aliases={2 + BLOCKS: 0},
            scratch_shapes=[squares, stages],
            cost_estimate=cost(2 * owned * size * LANES, 3 * moved * size // sub),
            compiler_params=limit(4),
        )(listing, weight, *incoming[which * BLOCKS : (which + 1) * BLOCKS], full)
        pieces += [blocks[0]] + [passed_along(blocks[d], "spec", d) for d in range(1, spec_count)]
    return pl.pallas_call(
        functools.partial(interact_kernel, row_count * halves, halves, spec_count, [s * lanes * halves for s, _ in groups]),
        out_shape=shape_of(bins, halves * LANES),
        in_specs=[SM] * 2 + [VM] * len(pieces),
        out_specs=pl.BlockSpec(memory_space=pl.ANY),
        scratch_shapes=[pltpu.VMEM((bins * halves, LANES), jnp.float32)] * (2 + 2 * GROUPS)
        + [pltpu.VMEM((bins, halves * LANES), jnp.float32), pltpu.SemaphoreType.DMA((chunked(bins // 48, 4),))],
        cost_estimate=cost(16 * bins * halves * LANES, 8 * bins * halves * LANES),
        compiler_params=limit(12),
        name="interact",
    )(jnp.concatenate([dia_plus * halves, dia_minus * halves, place]), dia_coeff, *pieces)


def solution(mesh):
    in_specs = (
        P("spec", "dom"),
        P(None, None, "dom"),
        P(None, "dom"),
        P("dom", None, None),
        P("dom"),
        P(),
        P(),
        P(),
        P(),
    )
    out_specs = P(None, ("dom", "spec"))
    return jax.shard_map(
        on_device, mesh=mesh, in_specs=in_specs, out_specs=out_specs, check_vma=False
    )
```

```python
import functools
import math

import jax
import jax.numpy as jnp
from jax import lax
from jax.experimental import pallas as pl
from jax.experimental.pallas import tpu as pltpu
from jax.sharding import PartitionSpec as P


NDIR = 36
REACH = 2
STEPS = 2
BLOCKS = 2 * REACH
LANES = 128
GROUPS = 2


weight_plus = 1.25 ** (-4)
weight_minus = 0.75 ** (-4)
weight_both = 0.9375 ** (-4)

VM = pl.BlockSpec(memory_space=pltpu.VMEM)
ANY = pl.BlockSpec(memory_space=pl.ANY)


def offset_of(position):
    return position - REACH if position < REACH else position - REACH + 1


def passed_along(value, axis, steps):
    count = lax.axis_size(axis)
    return lax.ppermute(value, axis, [(source, (source + steps) % count) for source in range(count)])


def chunked(total, limit):
    return max(size for size in range(1, limit + 1) if total % size == 0)


def listed_in(source, scratch, done):
    copy = pltpu.make_async_copy(source, scratch, done)
    copy.start()
    return copy


def list_scratch(length, dtype=jnp.int32):
    return [pltpu.SMEM((length,), dtype), pltpu.SemaphoreType.DMA(())]


def rows_to_block(sub, lanes, stage, block, start=0):
    for column in range(block.shape[1] // LANES):
        for part in range(block.shape[0] // lanes):
            tile = stage[pl.ds(column * LANES * sub + start + part, LANES, stride=sub), :].T
            block[part * lanes : (part + 1) * lanes, column * LANES : (column + 1) * LANES] = tile[:lanes]


def block_to_rows(sub, lanes, block, square, rows, first, start=0):
    for column in range(block.shape[1] // LANES):
        for part in range(block.shape[0] // lanes):
            slot = square.at[(column * sub + part) % square.shape[0]]
            slot[:lanes, :] = block[part * lanes : (part + 1) * lanes, column * LANES : (column + 1) * LANES]
            rows[pl.ds(first + column * LANES * sub + start + part, LANES, stride=sub), :] = slot[...].T


def pack_rows(parts, lanes, send, full, stages, outs):
    start, size = parts
    slots = outs[0].shape[1]
    unroll = chunked(slots, 32)
    for position in range(BLOCKS):
        stage = stages.at[position]

        @pl.loop(0, slots // unroll)
        def _(k):
            first = k * unroll
            listed = send.at[pl.ds((BLOCKS - 1 - position) * slots + first, unroll)]
            for u in range(unroll):
                stage[pl.ds((first + u) * size, size), :] = full[pl.ds(listed[u] + start, size), :]

    for position in range(BLOCKS):
        rows_to_block(size, lanes, stages.at[position], outs[position])


def enter_kernel(sub, lanes, source, spectrum, full, *rest):
    outs, (square, stages, send, done) = rest[:BLOCKS], rest[BLOCKS:]
    pending = listed_in(source, send, done)
    square[...] = jnp.zeros_like(square)
    block_to_rows(sub, lanes, spectrum, square, full, 0)
    pending.wait()
    pack_rows((0, sub), lanes, send, full, stages, outs)


def clear(items):
    rows = items[0].shape[0]
    step = chunked(rows, 64)
    zero = jnp.zeros((step, LANES), jnp.float32)

    @pl.loop(0, rows // step)
    def _(k):
        for item in items:
            item[pl.ds(pl.multiple_of(k * step, step), step), :] = zero


def slope_kernel(sub, shared, normals, step_weight, wave, coef, weight, lines):
    elements = normals.shape[2]
    parts = 1 if shared else sub
    plane = elements * parts
    lines[...] = jnp.zeros_like(lines)
    for component in range(2):
        for corner in range(2):
            row = component * 2 + corner
            lines[row : row + 1, :] = normals[component, corner : corner + 1, :]

    def spread(column):
        return jnp.broadcast_to(column, (8, LANES))

    @pl.loop(0, elements // LANES)
    def _(k):
        turned = lines[:, pl.ds(pl.multiple_of(k * LANES, LANES), LANES)].T
        for group in range(LANES // 8):
            at = slice(group * 8, group * 8 + 8)
            x0, x1, y0, y1 = (spread(turned[at, j : j + 1]) for j in range(4))
            base = (k * LANES + group * 8) * parts
            for part in range(parts):
                east, north = wave[part : part + 1, :], wave[sub + part : sub + part + 1, :]
                first = x0 * east + y0 * north
                second = x1 * east + y1 * north
                inward = jnp.minimum(first, 0.0) + jnp.minimum(second, 0.0) - jnp.maximum(first + second, 0.0)
                for which, value in enumerate((first, second, 1.0 / inward)):
                    first_row = which * plane + base
                    if parts == 1:
                        coef[pl.ds(pl.multiple_of(first_row, 8), 8), :] = value
                    else:
                        coef[pl.ds(first_row + part, 8, stride=parts), :] = value

    nodes = step_weight.shape[1]
    for block in range(nodes // LANES):
        turned = jnp.broadcast_to(step_weight[0:1, block * LANES : (block + 1) * LANES], (8, LANES)).T
        for group in range(LANES // 8):
            value = spread(turned[group * 8 : group * 8 + 8, 0:1])
            for part in range(sub):
                at = pl.ds((block * LANES + group * 8) * sub + part, 8, stride=sub)
                weight[at, :] = value * wave[2 * sub + part : 2 * sub + part + 1, :]


def total(sums, at):
    result = sums[0][at, :]
    for item in sums[1:]:
        result = result + item[at, :]
    return result


def sweep_kernel(sub, inner, groups, lanes, shared, own_rows, source, coef, weight, *rest):
    ghosts, rest = rest[: BLOCKS * len(inner)], rest[BLOCKS * len(inner) + 1 :]
    full, rest = rest[0], rest[1:]
    returned, rest = rest[: BLOCKS * len(groups)], rest[BLOCKS * len(groups) :]
    square, stages, conn, done, sums = rest[0], rest[1], rest[2], rest[3], rest[4:]
    pending = listed_in(source, conn, done)
    clear(sums)
    ghost_rows = (full.shape[0] - own_rows) // BLOCKS
    elements = conn.shape[0] // 3
    parts = 1 if shared else sub
    square[...] = jnp.zeros_like(square)
    for which, (start, _) in enumerate(inner):
        for position in range(BLOCKS):
            block = ghosts[which * BLOCKS + position]
            block_to_rows(sub, lanes, block, square, full, own_rows + position * ghost_rows, start)

    pending.wait()
    share = elements // GROUPS
    unroll = chunked(share, 32)

    @pl.loop(0, share // unroll)
    def _(k):
        listed = [
            [conn.at[pl.ds(corner * elements + group * share + k * unroll, unroll)] for corner in range(3)]
            for group in range(GROUPS)
        ]
        for u in range(unroll):
            for group in range(GROUPS):
                element = group * share + k * unroll + u
                index = [item[u] for item in listed[group]]
                value = [full[pl.ds(row, sub), :] for row in index]
                first, second, inverse = (
                    jnp.broadcast_to(coef[pl.ds((j * elements + element) * parts, parts), :], (sub, LANES))
                    for j in range(3)
                )
                both = first + second
                inflow = jnp.minimum(first, 0.0) * value[0] + jnp.minimum(second, 0.0) * value[1]
                inflow = (inflow - jnp.maximum(both, 0.0) * value[2]) * inverse
                residual = (
                    jnp.maximum(first, 0.0) * (value[0] - inflow),
                    jnp.maximum(second, 0.0) * (value[1] - inflow),
                    jnp.minimum(both, 0.0) * (inflow - value[2]),
                )
                for corner in range(3):
                    item = sums[group * 3 + corner]
                    at = pl.ds(index[corner], sub)
                    item[at, :] = item[at, :] + residual[corner]

    step = chunked(ghost_rows, 64)
    for position in range(BLOCKS):
        stage = stages.at[position]

        @pl.loop(0, ghost_rows // step)
        def _(k):
            at = pl.multiple_of(k * step, step)
            stage[pl.ds(at, step), :] = total(sums, pl.ds(own_rows + position * ghost_rows + at, step))

    for which, (start, _) in enumerate(groups):
        for position in range(BLOCKS):
            rows_to_block(sub, lanes, stages.at[position], returned[which * BLOCKS + position], start)

    own_step = chunked(own_rows, 64)

    @pl.loop(0, own_rows // own_step)
    def _(k):
        at = pl.ds(pl.multiple_of(k * own_step, own_step), own_step)
        full[at, :] = full[at, :] - weight[at, :] * total(sums, at)


def add_returned(parts, lanes, pending, send, weight, incoming, square, stages, full):
    start, size = parts
    slots = incoming[0].shape[1]
    square[...] = jnp.zeros_like(square)
    unroll = chunked(slots, 16)
    for position in range(BLOCKS):
        block_to_rows(size, lanes, incoming[position], square, stages.at[position], 0)
    pending.wait()
    for position in range(BLOCKS):
        stage = stages.at[position]

        @pl.loop(0, slots // unroll)
        def _(k):
            first = k * unroll
            listed = send.at[pl.ds((BLOCKS - 1 - position) * slots + first, unroll)]
            rows = [pl.ds(listed[u] + start, size) for u in range(unroll)]
            fresh = [
                full[row, :] - weight[row, :] * stage[pl.ds((first + u) * size, size), :]
                for u, row in enumerate(rows)
            ]
            for row, item in zip(rows, fresh):
                full[row, :] = item


def between_kernel(parts, lanes, source, weight, *rest):
    incoming, rest = rest[:BLOCKS], rest[BLOCKS + 1 :]
    full, outs, (square, stages, send, done) = rest[0], rest[1 : 1 + BLOCKS], rest[1 + BLOCKS :]
    pending = listed_in(source, send, done)
    add_returned(parts, lanes, pending, send, weight, incoming, square, stages, full)
    pack_rows(parts, lanes, send, full, stages, outs)


def leave_kernel(sub, parts, lanes, halves, count, source, weight, *rest):
    incoming, rest = rest[:BLOCKS], rest[BLOCKS + 1 :]
    full, outs, (square, stages, send, done) = rest[0], rest[1 : 1 + count], rest[1 + count :]
    pending = listed_in(source, send, done)
    add_returned(parts, lanes, pending, send, weight, incoming, square, stages, full)
    start, size = parts
    place = lax.axis_index("spec")
    for distance in range(count):
        target = lax.rem(place + distance, count)
        for half in range(halves):
            first = (target * halves + half) * LANES * sub + start
            for part in range(size):
                tile = full[pl.ds(first + part, LANES, stride=sub), :].T
                outs[distance][pl.ds(part * lanes * halves + half, lanes, stride=halves), :] = tile[:lanes]


def interact_kernel(per_source, halves, count, starts, partner_source, rate_source, *rest):
    pieces, rest = rest[: count * len(starts)], rest[count * len(starts) :]
    target, energy, kept, added = rest[0], rest[1], rest[2], rest[3:-6]
    out, done, partner, partner_done, rate, rate_done = rest[-6:]
    pending = listed_in(partner_source, partner, partner_done), listed_in(rate_source, rate, rate_done)
    bins = rate.shape[0]
    place = lax.axis_index("spec")
    clear(added)
    for which, start in enumerate(starts):
        for distance in range(count):
            piece = pieces[which * count + distance]
            first = lax.rem(place + count - distance, count) * per_source + start
            if per_source % 8 == 0 and start % 8 == 0:
                first = pl.multiple_of(first, 8)
            energy[pl.ds(first, piece.shape[0]), :] = piece[...]
    for item in pending:
        item.wait()
    share = bins // GROUPS
    unroll = chunked(share, 18)

    @pl.loop(0, share // unroll)
    def _(k):
        for u in range(unroll):
            for group in range(GROUPS):
                index = group * share + k * unroll + u
                up, down = partner[index], partner[bins + index]
                here = pl.ds(index * halves, halves)
                own = energy[here, :]
                upper = energy[pl.ds(up, halves), :]
                lower = energy[pl.ds(down, halves), :]
                term = rate[index] * (
                    own * own * (weight_plus * upper + weight_minus * lower)
                    - 2.0 * weight_both * own * upper * lower
                )
                kept[here, :] = own - 2.0 * term
                for item, row in zip(added[2 * group :], (up, down)):
                    item[pl.ds(row, halves), :] = item[pl.ds(row, halves), :] + term

    copies = done.shape[0]
    share = bins // copies
    step = chunked(share, 48)
    for which in range(copies):

        @pl.loop(which * share // step, (which + 1) * share // step)
        def _(k):
            for half in range(halves):
                at = pl.ds(k * step * halves + half, step, stride=halves)
                result = kept[at, :] + total(added, at)
                out[pl.ds(pl.multiple_of(k * step, step), step), half * LANES : (half + 1) * LANES] = result

        at = pl.ds(which * share, share)
        pltpu.make_async_copy(out.at[at], target.at[at], done.at[which]).start()
    for which in range(copies):
        at = pl.ds(which * share, share)
        pltpu.make_async_copy(out.at[at], target.at[at], done.at[which]).wait()


def shape_of(*dims):
    return jax.ShapeDtypeStruct(dims, jnp.float32)


def cost(flops, moved):
    return pl.CostEstimate(flops=flops, bytes_accessed=moved, transcendentals=0)


def limit(mebibytes):
    return pltpu.CompilerParams(vmem_limit_bytes=mebibytes << 20)


def on_device(
    spectrum, normals, conn, send_nodes, step_weight, group_speed, dia_plus, dia_minus, dia_coeff
):
    row_count, owned = spectrum.shape
    slots = send_nodes.shape[2]
    elements = conn.shape[1]
    bins = dia_plus.shape[0]
    spec_count = lax.axis_size("spec")
    sub = -(-row_count // LANES)
    while row_count % sub:
        sub += 1
    lanes = row_count // sub
    shared = lanes % NDIR == 0
    own_rows = owned * sub
    ghost_rows = slots * sub
    rows = own_rows + BLOCKS * ghost_rows
    halves = owned // (spec_count * LANES)

    nodes = (conn * sub).reshape(-1)
    send = (send_nodes[0] * sub).reshape(-1)

    bin_of = (
        lax.axis_index("spec") * row_count
        + jnp.arange(sub, dtype=jnp.int32)[:, None] * lanes
        + jnp.arange(LANES, dtype=jnp.int32)[None, :]
    )
    angle = (bin_of % NDIR).astype(jnp.float32) * (2.0 * math.pi / NDIR)
    east, north = jnp.cos(angle), jnp.sin(angle)
    select = ((bin_of // NDIR)[:, :, None] == jnp.arange(group_speed.shape[0], dtype=jnp.int32)).astype(jnp.float32)
    speed = jnp.sum(select * group_speed, axis=2)
    wave = jnp.concatenate([east, north, speed])

    def blocks_of(groups):
        return [shape_of(size * lanes, slots) for _, size in groups for _ in range(BLOCKS)]

    whole = ((0, sub),)
    block_shapes = blocks_of(whole)
    full_shape = shape_of(rows, LANES)
    sums = [pltpu.VMEM((rows, LANES), jnp.float32)] * (3 * GROUPS)
    squares = pltpu.VMEM((4, LANES, LANES), jnp.float32)
    stages = pltpu.VMEM((BLOCKS, ghost_rows, LANES), jnp.float32)
    moved = 4 * LANES * own_rows

    full, *outs = pl.pallas_call(
        functools.partial(enter_kernel, sub, lanes),
        out_shape=[full_shape] + block_shapes,
        in_specs=[ANY, VM],
        out_specs=[VM] * (1 + BLOCKS),
        scratch_shapes=[squares, stages] + list_scratch(BLOCKS * slots),
        cost_estimate=cost(0, 2 * moved),
        compiler_params=limit(4),
        name="enter",
    )(send, spectrum)
    pitch = 3 if shared else 3 * sub
    coef, weight = pl.pallas_call(
        functools.partial(slope_kernel, sub, shared),
        out_shape=[shape_of(elements * pitch, LANES), shape_of(own_rows, LANES)],
        in_specs=[VM] * 3,
        out_specs=[VM] * 2,
        scratch_shapes=[pltpu.VMEM((LANES, elements), jnp.float32)],
        cost_estimate=cost(20 * elements * LANES, 4 * LANES * (elements * pitch + own_rows)),
        compiler_params=limit(4),
        name="slopes",
    )(normals, step_weight.reshape(1, owned), wave)

    groups = whole if sub == 1 else ((0, 1), (1, sub - 1))
    inner = whole
    for sweep_index in range(STEPS):
        ghosts = []
        for p, item in enumerate(outs):
            ghosts.append(passed_along(item, "dom", -offset_of(p % BLOCKS)))
        full, *returned = pl.pallas_call(
            functools.partial(sweep_kernel, sub, inner, groups, lanes, shared, own_rows),
            out_shape=[full_shape] + blocks_of(groups),
            in_specs=[ANY] + [VM] * (3 + len(ghosts)),
            out_specs=[VM] * (1 + BLOCKS * len(groups)),
            input_output_aliases={3 + len(ghosts): 0},
            scratch_shapes=[squares, stages] + list_scratch(3 * elements) + sums,
            cost_estimate=cost(elements * 24 * row_count, 4 * LANES * (3 * elements + 4 * rows)),
            compiler_params=limit(20),
            name="sweep",
        )(nodes, coef, weight, *ghosts, full)
        incoming = []
        for p, item in enumerate(returned):
            incoming.append(passed_along(item, "dom", offset_of(p % BLOCKS)))
        if sweep_index < STEPS - 1:
            outs, inner = [], groups
            for which, parts in enumerate(groups):
                full, *more = pl.pallas_call(
                    functools.partial(between_kernel, parts, lanes),
                    out_shape=[full_shape] + blocks_of((parts,)),
                    in_specs=[ANY] + [VM] * (2 + BLOCKS),
                    out_specs=[VM] * (1 + BLOCKS),
                    input_output_aliases={2 + BLOCKS: 0},
                    scratch_shapes=[squares, stages] + list_scratch(BLOCKS * slots),
                    cost_estimate=cost(2 * owned * parts[1] * LANES, 4 * moved * parts[1] // sub),
                    compiler_params=limit(4),
                )(send, weight, *incoming[which * BLOCKS : (which + 1) * BLOCKS], full)
                outs += more

    pieces = []
    for which, (start, size) in enumerate(groups):
        full, *blocks = pl.pallas_call(
            functools.partial(leave_kernel, sub, (start, size), lanes, halves, spec_count),
            out_shape=[full_shape] + [shape_of(size * lanes * halves, LANES)] * spec_count,
            in_specs=[ANY] + [VM] * (2 + BLOCKS),
            out_specs=[VM] * (1 + spec_count),
            input_output_aliases={2 + BLOCKS: 0},
            scratch_shapes=[squares, stages] + list_scratch(BLOCKS * slots),
            cost_estimate=cost(2 * owned * size * LANES, 3 * moved * size // sub),
            compiler_params=limit(4),
        )(send, weight, *incoming[which * BLOCKS : (which + 1) * BLOCKS], full)
        pieces.append(blocks[0])
        for distance in range(1, spec_count):
            pieces.append(passed_along(blocks[distance], "spec", distance))
    return pl.pallas_call(
        functools.partial(interact_kernel, row_count * halves, halves, spec_count, [s * lanes * halves for s, _ in groups]),
        out_shape=shape_of(bins, halves * LANES),
        in_specs=[ANY] * 2 + [VM] * len(pieces),
        out_specs=pl.BlockSpec(memory_space=pl.ANY),
        scratch_shapes=[pltpu.VMEM((bins * halves, LANES), jnp.float32)] * (2 + 2 * GROUPS)
        + [pltpu.VMEM((bins, halves * LANES), jnp.float32), pltpu.SemaphoreType.DMA((chunked(bins // 48, 4),))]
        + list_scratch(2 * bins)
        + list_scratch(bins, jnp.float32),
        cost_estimate=cost(16 * bins * halves * LANES, 8 * bins * halves * LANES),
        compiler_params=limit(12),
        name="interact",
    )(jnp.concatenate([dia_plus, dia_minus]) * halves, dia_coeff, *pieces)


def solution(mesh):
    in_specs = (
        P("spec", "dom"),
        P(None, None, "dom"),
        P(None, "dom"),
        P("dom", None, None),
        P("dom"),
        P(),
        P(),
        P(),
        P(),
    )
    out_specs = P(None, ("dom", "spec"))
    return jax.shard_map(
        on_device, mesh=mesh, in_specs=in_specs, out_specs=out_specs, check_vma=False
    )
```

```python
import functools
import math

import jax
import jax.numpy as jnp
from jax import lax
from jax.experimental import pallas as pl
from jax.experimental.pallas import tpu as pltpu
from jax.sharding import PartitionSpec as P


NDIR = 36
REACH = 2
STEPS = 2
BLOCKS = 2 * REACH
LANES = 128
GROUPS = 2


weight_plus = 1.25 ** (-4)
weight_minus = 0.75 ** (-4)
weight_both = 0.9375 ** (-4)

VM = pl.BlockSpec(memory_space=pltpu.VMEM)
ANY = pl.BlockSpec(memory_space=pl.ANY)


def offset_of(position):
    return position - REACH if position < REACH else position - REACH + 1


def passed_along(value, axis, steps):
    count = lax.axis_size(axis)
    return lax.ppermute(value, axis, [(source, (source + steps) % count) for source in range(count)])


def chunked(total, limit):
    return max(size for size in range(1, limit + 1) if total % size == 0)


def listed_in(source, scratch, done):
    copy = pltpu.make_async_copy(source, scratch, done)
    copy.start()
    return copy


def list_scratch(length, dtype=jnp.int32):
    return [pltpu.SMEM((length,), dtype), pltpu.SemaphoreType.DMA(())]


def rows_to_block(sub, lanes, stage, block, start=0):
    for column in range(block.shape[1] // LANES):
        for part in range(block.shape[0] // lanes):
            tile = stage[pl.ds(column * LANES * sub + start + part, LANES, stride=sub), :].T
            block[part * lanes : (part + 1) * lanes, column * LANES : (column + 1) * LANES] = tile[:lanes]


def block_to_rows(sub, lanes, block, square, rows, first, start=0, factor=None):
    for column in range(block.shape[1] // LANES):
        for part in range(block.shape[0] // lanes):
            slot = square.at[(column * sub + part) % square.shape[0]]
            slot[:lanes, :] = block[part * lanes : (part + 1) * lanes, column * LANES : (column + 1) * LANES]
            tile = slot[...].T
            if factor is not None:
                tile = tile * factor(column, part)
            rows[pl.ds(first + column * LANES * sub + start + part, LANES, stride=sub), :] = tile


def pack_rows(parts, lanes, send, full, stages, outs):
    start, size = parts
    slots = outs[0].shape[1]
    unroll = chunked(slots, 32)
    for position in range(BLOCKS):
        stage = stages.at[position]

        @pl.loop(0, slots // unroll)
        def _(k):
            first = k * unroll
            listed = send.at[pl.ds((BLOCKS - 1 - position) * slots + first, unroll)]
            for u in range(unroll):
                stage[pl.ds((first + u) * size, size), :] = full[pl.ds(listed[u] + start, size), :]

    for position in range(BLOCKS):
        rows_to_block(size, lanes, stages.at[position], outs[position])


def enter_kernel(sub, lanes, source, spectrum, full, *rest):
    outs, (square, stages, send, done) = rest[:BLOCKS], rest[BLOCKS:]
    pending = listed_in(source, send, done)
    square[...] = jnp.zeros_like(square)
    block_to_rows(sub, lanes, spectrum, square, full, 0)
    pending.wait()
    pack_rows((0, sub), lanes, send, full, stages, outs)


def clear(items):
    rows = items[0].shape[0]
    step = chunked(rows, 64)
    zero = jnp.zeros((step, LANES), jnp.float32)

    @pl.loop(0, rows // step)
    def _(k):
        for item in items:
            item[pl.ds(pl.multiple_of(k * step, step), step), :] = zero


def slope_kernel(sub, shared, source, normals, step_weight, wave, coef, weight, listed_weight, lines, send, done):
    pending = listed_in(source, send, done)
    elements = normals.shape[2]
    parts = 1 if shared else sub
    plane = elements * parts
    lines[...] = jnp.zeros_like(lines)
    for component in range(2):
        for corner in range(2):
            row = component * 2 + corner
            lines[row : row + 1, :] = normals[component, corner : corner + 1, :]

    def spread(column):
        return jnp.broadcast_to(column, (8, LANES))

    @pl.loop(0, elements // LANES)
    def _(k):
        turned = lines[:, pl.ds(pl.multiple_of(k * LANES, LANES), LANES)].T
        for group in range(LANES // 8):
            at = slice(group * 8, group * 8 + 8)
            x0, x1, y0, y1 = (spread(turned[at, j : j + 1]) for j in range(4))
            base = (k * LANES + group * 8) * parts
            for part in range(parts):
                east, north = wave[part : part + 1, :], wave[sub + part : sub + part + 1, :]
                first = x0 * east + y0 * north
                second = x1 * east + y1 * north
                inward = jnp.minimum(first, 0.0) + jnp.minimum(second, 0.0) - jnp.maximum(first + second, 0.0)
                for which, value in enumerate((first, second, 1.0 / inward)):
                    first_row = which * plane + base
                    if parts == 1:
                        coef[pl.ds(pl.multiple_of(first_row, 8), 8), :] = value
                    else:
                        coef[pl.ds(first_row + part, 8, stride=parts), :] = value

    nodes = step_weight.shape[1]
    for block in range(nodes // LANES):
        turned = jnp.broadcast_to(step_weight[0:1, block * LANES : (block + 1) * LANES], (8, LANES)).T
        for group in range(LANES // 8):
            value = spread(turned[group * 8 : group * 8 + 8, 0:1])
            for part in range(sub):
                at = pl.ds((block * LANES + group * 8) * sub + part, 8, stride=sub)
                weight[at, :] = value * wave[2 * sub + part : 2 * sub + part + 1, :]

    pending.wait()
    unroll = chunked(send.shape[0], 32)

    @pl.loop(0, send.shape[0] // unroll)
    def _(k):
        listed = send.at[pl.ds(k * unroll, unroll)]
        for u in range(unroll):
            listed_weight[pl.ds((k * unroll + u) * sub, sub), :] = weight[pl.ds(listed[u], sub), :]


def total(sums, at):
    result = sums[0][at, :]
    for item in sums[1:]:
        result = result + item[at, :]
    return result


def sweep_kernel(sub, inner, groups, lanes, shared, own_rows, source, coef, weight, *rest):
    ghosts, rest = rest[: BLOCKS * len(inner)], rest[BLOCKS * len(inner) + 1 :]
    full, rest = rest[0], rest[1:]
    returned, rest = rest[: BLOCKS * len(groups)], rest[BLOCKS * len(groups) :]
    square, stages, conn, done, sums = rest[0], rest[1], rest[2], rest[3], rest[4:]
    pending = listed_in(source, conn, done)
    clear(sums)
    ghost_rows = (full.shape[0] - own_rows) // BLOCKS
    elements = conn.shape[0] // 3
    parts = 1 if shared else sub
    square[...] = jnp.zeros_like(square)
    for which, (start, _) in enumerate(inner):
        for position in range(BLOCKS):
            block = ghosts[which * BLOCKS + position]
            block_to_rows(sub, lanes, block, square, full, own_rows + position * ghost_rows, start)

    pending.wait()
    share = elements // GROUPS
    unroll = chunked(share, 32)

    @pl.loop(0, share // unroll)
    def _(k):
        listed = [
            [conn.at[pl.ds(corner * elements + group * share + k * unroll, unroll)] for corner in range(3)]
            for group in range(GROUPS)
        ]
        for u in range(unroll):
            for group in range(GROUPS):
                element = group * share + k * unroll + u
                index = [item[u] for item in listed[group]]
                value = [full[pl.ds(row, sub), :] for row in index]
                first, second, inverse = (
                    jnp.broadcast_to(coef[pl.ds((j * elements + element) * parts, parts), :], (sub, LANES))
                    for j in range(3)
                )
                both = first + second
                inflow = jnp.minimum(first, 0.0) * value[0] + jnp.minimum(second, 0.0) * value[1]
                inflow = (inflow - jnp.maximum(both, 0.0) * value[2]) * inverse
                residual = (
                    jnp.maximum(first, 0.0) * (value[0] - inflow),
                    jnp.maximum(second, 0.0) * (value[1] - inflow),
                    jnp.minimum(both, 0.0) * (inflow - value[2]),
                )
                for corner in range(3):
                    item = sums[group * 3 + corner]
                    at = pl.ds(index[corner], sub)
                    item[at, :] = item[at, :] + residual[corner]

    step = chunked(ghost_rows, 64)
    for position in range(BLOCKS):
        stage = stages.at[position]

        @pl.loop(0, ghost_rows // step)
        def _(k):
            at = pl.multiple_of(k * step, step)
            stage[pl.ds(at, step), :] = total(sums, pl.ds(own_rows + position * ghost_rows + at, step))

    for which, (start, _) in enumerate(groups):
        for position in range(BLOCKS):
            rows_to_block(sub, lanes, stages.at[position], returned[which * BLOCKS + position], start)

    own_step = chunked(own_rows, 64)

    @pl.loop(0, own_rows // own_step)
    def _(k):
        at = pl.ds(pl.multiple_of(k * own_step, own_step), own_step)
        full[at, :] = full[at, :] - weight[at, :] * total(sums, at)


def add_returned(sub, parts, lanes, pending, send, listed_weight, incoming, square, stages, full):
    start, size = parts
    slots = incoming[0].shape[1]
    square[...] = jnp.zeros_like(square)
    unroll = chunked(slots, 16)
    for position in range(BLOCKS):
        base = (BLOCKS - 1 - position) * slots * sub + start

        def factor(column, part):
            return listed_weight[pl.ds(base + column * LANES * sub + part, LANES, stride=sub), :]

        block_to_rows(size, lanes, incoming[position], square, stages.at[position], 0, 0, factor)
    pending.wait()
    for position in range(BLOCKS):
        stage = stages.at[position]

        @pl.loop(0, slots // unroll)
        def _(k):
            first = k * unroll
            listed = send.at[pl.ds((BLOCKS - 1 - position) * slots + first, unroll)]
            rows = [pl.ds(listed[u] + start, size) for u in range(unroll)]
            fresh = [full[row, :] - stage[pl.ds((first + u) * size, size), :] for u, row in enumerate(rows)]
            for row, item in zip(rows, fresh):
                full[row, :] = item


def between_kernel(sub, parts, lanes, source, listed_weight, *rest):
    incoming, rest = rest[:BLOCKS], rest[BLOCKS + 1 :]
    full, outs, (square, stages, send, done) = rest[0], rest[1 : 1 + BLOCKS], rest[1 + BLOCKS :]
    pending = listed_in(source, send, done)
    add_returned(sub, parts, lanes, pending, send, listed_weight, incoming, square, stages, full)
    pack_rows(parts, lanes, send, full, stages, outs)


def leave_kernel(sub, parts, lanes, halves, count, source, listed_weight, *rest):
    incoming, rest = rest[:BLOCKS], rest[BLOCKS + 1 :]
    full, outs, (square, stages, send, done) = rest[0], rest[1 : 1 + count], rest[1 + count :]
    pending = listed_in(source, send, done)
    add_returned(sub, parts, lanes, pending, send, listed_weight, incoming, square, stages, full)
    start, size = parts
    place = lax.axis_index("spec")
    for distance in range(count):
        target = lax.rem(place + distance, count)
        for half in range(halves):
            first = (target * halves + half) * LANES * sub + start
            for part in range(size):
                tile = full[pl.ds(first + part, LANES, stride=sub), :].T
                outs[distance][pl.ds(part * lanes * halves + half, lanes, stride=halves), :] = tile[:lanes]


def interact_kernel(per_source, halves, count, starts, partner_source, rate_source, *rest):
    pieces, rest = rest[: count * len(starts)], rest[count * len(starts) :]
    target, energy, kept, added = rest[0], rest[1], rest[2], rest[3:-6]
    out, done, partner, partner_done, rate, rate_done = rest[-6:]
    pending = listed_in(partner_source, partner, partner_done), listed_in(rate_source, rate, rate_done)
    bins = rate.shape[0]
    place = lax.axis_index("spec")
    clear(added)
    for which, start in enumerate(starts):
        for distance in range(count):
            piece = pieces[which * count + distance]
            first = lax.rem(place + count - distance, count) * per_source + start
            if per_source % 8 == 0 and start % 8 == 0:
                first = pl.multiple_of(first, 8)
            energy[pl.ds(first, piece.shape[0]), :] = piece[...]
    for item in pending:
        item.wait()
    share = bins // GROUPS
    unroll = chunked(share, 18)

    @pl.loop(0, share // unroll)
    def _(k):
        for u in range(unroll):
            for group in range(GROUPS):
                index = group * share + k * unroll + u
                up, down = partner[index], partner[bins + index]
                here = pl.ds(index * halves, halves)
                own = energy[here, :]
                upper = energy[pl.ds(up, halves), :]
                lower = energy[pl.ds(down, halves), :]
                term = rate[index] * (
                    own * own * (weight_plus * upper + weight_minus * lower)
                    - 2.0 * weight_both * own * upper * lower
                )
                kept[here, :] = own - 2.0 * term
                for item, row in zip(added[2 * group :], (up, down)):
                    item[pl.ds(row, halves), :] = item[pl.ds(row, halves), :] + term

    copies = done.shape[0]
    share = bins // copies
    step = chunked(share, 48)
    for which in range(copies):

        @pl.loop(which * share // step, (which + 1) * share // step)
        def _(k):
            for half in range(halves):
                at = pl.ds(k * step * halves + half, step, stride=halves)
                result = kept[at, :] + total(added, at)
                out[pl.ds(pl.multiple_of(k * step, step), step), half * LANES : (half + 1) * LANES] = result

        at = pl.ds(which * share, share)
        pltpu.make_async_copy(out.at[at], target.at[at], done.at[which]).start()
    for which in range(copies):
        at = pl.ds(which * share, share)
        pltpu.make_async_copy(out.at[at], target.at[at], done.at[which]).wait()


def shape_of(*dims):
    return jax.ShapeDtypeStruct(dims, jnp.float32)


def cost(flops, moved):
    return pl.CostEstimate(flops=flops, bytes_accessed=moved, transcendentals=0)


def limit(mebibytes):
    return pltpu.CompilerParams(vmem_limit_bytes=mebibytes << 20)


def on_device(
    spectrum, normals, conn, send_nodes, step_weight, group_speed, dia_plus, dia_minus, dia_coeff
):
    row_count, owned = spectrum.shape
    slots = send_nodes.shape[2]
    elements = conn.shape[1]
    bins = dia_plus.shape[0]
    spec_count = lax.axis_size("spec")
    sub = -(-row_count // LANES)
    while row_count % sub:
        sub += 1
    lanes = row_count // sub
    shared = lanes % NDIR == 0
    own_rows = owned * sub
    ghost_rows = slots * sub
    rows = own_rows + BLOCKS * ghost_rows
    halves = owned // (spec_count * LANES)

    nodes = (conn * sub).reshape(-1)
    send = (send_nodes[0] * sub).reshape(-1)

    bin_of = (
        lax.axis_index("spec") * row_count
        + jnp.arange(sub, dtype=jnp.int32)[:, None] * lanes
        + jnp.arange(LANES, dtype=jnp.int32)[None, :]
    )
    angle = (bin_of % NDIR).astype(jnp.float32) * (2.0 * math.pi / NDIR)
    east, north = jnp.cos(angle), jnp.sin(angle)
    select = ((bin_of // NDIR)[:, :, None] == jnp.arange(group_speed.shape[0], dtype=jnp.int32)).astype(jnp.float32)
    speed = jnp.sum(select * group_speed, axis=2)
    wave = jnp.concatenate([east, north, speed])

    def blocks_of(groups):
        return [shape_of(size * lanes, slots) for _, size in groups for _ in range(BLOCKS)]

    whole = ((0, sub),)
    block_shapes = blocks_of(whole)
    full_shape = shape_of(rows, LANES)
    sums = [pltpu.VMEM((rows, LANES), jnp.float32)] * (3 * GROUPS)
    squares = pltpu.VMEM((4, LANES, LANES), jnp.float32)
    stages = pltpu.VMEM((BLOCKS, ghost_rows, LANES), jnp.float32)
    moved = 4 * LANES * own_rows

    full, *outs = pl.pallas_call(
        functools.partial(enter_kernel, sub, lanes),
        out_shape=[full_shape] + block_shapes,
        in_specs=[ANY, VM],
        out_specs=[VM] * (1 + BLOCKS),
        scratch_shapes=[squares, stages] + list_scratch(BLOCKS * slots),
        cost_estimate=cost(0, 2 * moved),
        compiler_params=limit(4),
        name="enter",
    )(send, spectrum)
    pitch = 3 if shared else 3 * sub
    coef, weight, listed_weight = pl.pallas_call(
        functools.partial(slope_kernel, sub, shared),
        out_shape=[shape_of(elements * pitch, LANES), shape_of(own_rows, LANES), shape_of(BLOCKS * ghost_rows, LANES)],
        in_specs=[ANY] + [VM] * 3,
        out_specs=[VM] * 3,
        scratch_shapes=[pltpu.VMEM((LANES, elements), jnp.float32)] + list_scratch(BLOCKS * slots),
        cost_estimate=cost(20 * elements * LANES, 4 * LANES * (elements * pitch + own_rows)),
        compiler_params=limit(4),
        name="slopes",
    )(send, normals, step_weight.reshape(1, owned), wave)

    groups = whole if sub == 1 else ((0, 1), (1, sub - 1))
    inner = whole
    for sweep_index in range(STEPS):
        ghosts = []
        for p, item in enumerate(outs):
            ghosts.append(passed_along(item, "dom", -offset_of(p % BLOCKS)))
        full, *returned = pl.pallas_call(
            functools.partial(sweep_kernel, sub, inner, groups, lanes, shared, own_rows),
            out_shape=[full_shape] + blocks_of(groups),
            in_specs=[ANY] + [VM] * (3 + len(ghosts)),
            out_specs=[VM] * (1 + BLOCKS * len(groups)),
            input_output_aliases={3 + len(ghosts): 0},
            scratch_shapes=[squares, stages] + list_scratch(3 * elements) + sums,
            cost_estimate=cost(elements * 24 * row_count, 4 * LANES * (3 * elements + 4 * rows)),
            compiler_params=limit(20),
            name="sweep",
        )(nodes, coef, weight, *ghosts, full)
        incoming = []
        for p, item in enumerate(returned):
            incoming.append(passed_along(item, "dom", offset_of(p % BLOCKS)))
        if sweep_index < STEPS - 1:
            outs, inner = [], groups
            for which, parts in enumerate(groups):
                full, *more = pl.pallas_call(
                    functools.partial(between_kernel, sub, parts, lanes),
                    out_shape=[full_shape] + blocks_of((parts,)),
                    in_specs=[ANY] + [VM] * (2 + BLOCKS),
                    out_specs=[VM] * (1 + BLOCKS),
                    input_output_aliases={2 + BLOCKS: 0},
                    scratch_shapes=[squares, stages] + list_scratch(BLOCKS * slots),
                    cost_estimate=cost(2 * owned * parts[1] * LANES, 4 * moved * parts[1] // sub),
                    compiler_params=limit(4),
                )(send, listed_weight, *incoming[which * BLOCKS : (which + 1) * BLOCKS], full)
                outs += more

    pieces = []
    for which, (start, size) in enumerate(groups):
        full, *blocks = pl.pallas_call(
            functools.partial(leave_kernel, sub, (start, size), lanes, halves, spec_count),
            out_shape=[full_shape] + [shape_of(size * lanes * halves, LANES)] * spec_count,
            in_specs=[ANY] + [VM] * (2 + BLOCKS),
            out_specs=[VM] * (1 + spec_count),
            input_output_aliases={2 + BLOCKS: 0},
            scratch_shapes=[squares, stages] + list_scratch(BLOCKS * slots),
            cost_estimate=cost(2 * owned * size * LANES, 3 * moved * size // sub),
            compiler_params=limit(4),
        )(send, listed_weight, *incoming[which * BLOCKS : (which + 1) * BLOCKS], full)
        pieces.append(blocks[0])
        for distance in range(1, spec_count):
            pieces.append(passed_along(blocks[distance], "spec", distance))
    return pl.pallas_call(
        functools.partial(interact_kernel, row_count * halves, halves, spec_count, [s * lanes * halves for s, _ in groups]),
        out_shape=shape_of(bins, halves * LANES),
        in_specs=[ANY] * 2 + [VM] * len(pieces),
        out_specs=pl.BlockSpec(memory_space=pl.ANY),
        scratch_shapes=[pltpu.VMEM((bins * halves, LANES), jnp.float32)] * (2 + 2 * GROUPS)
        + [pltpu.VMEM((bins, halves * LANES), jnp.float32), pltpu.SemaphoreType.DMA((chunked(bins // 48, 4),))]
        + list_scratch(2 * bins)
        + list_scratch(bins, jnp.float32),
        cost_estimate=cost(16 * bins * halves * LANES, 8 * bins * halves * LANES),
        compiler_params=limit(12),
        name="interact",
    )(jnp.concatenate([dia_plus, dia_minus]) * halves, dia_coeff, *pieces)


def solution(mesh):
    in_specs = (
        P("spec", "dom"),
        P(None, None, "dom"),
        P(None, "dom"),
        P("dom", None, None),
        P("dom"),
        P(),
        P(),
        P(),
        P(),
    )
    out_specs = P(None, ("dom", "spec"))
    return jax.shard_map(
        on_device, mesh=mesh, in_specs=in_specs, out_specs=out_specs, check_vma=False
    )
```

```python
import functools
import math

import jax
import jax.numpy as jnp
from jax import lax
from jax.experimental import pallas as pl
from jax.experimental.pallas import tpu as pltpu
from jax.sharding import PartitionSpec as P


NDIR = 36
REACH = 2
STEPS = 2
BLOCKS = 2 * REACH
LANES = 128
GROUPS = 2


weight_plus = 1.25 ** (-4)
weight_minus = 0.75 ** (-4)
weight_both = 0.9375 ** (-4)

VM = pl.BlockSpec(memory_space=pltpu.VMEM)
ANY = pl.BlockSpec(memory_space=pl.ANY)


def offset_of(position):
    return position - REACH if position < REACH else position - REACH + 1


def passed_along(value, axis, steps):
    count = lax.axis_size(axis)
    return lax.ppermute(value, axis, [(source, (source + steps) % count) for source in range(count)])


def chunked(total, limit):
    return max(size for size in range(1, limit + 1) if total % size == 0)


def listed_in(source, scratch, done):
    copy = pltpu.make_async_copy(source, scratch, done)
    copy.start()
    return copy


def list_scratch(length, dtype=jnp.int32):
    return [pltpu.SMEM((length,), dtype), pltpu.SemaphoreType.DMA(())]


def rows_to_block(sub, lanes, stage, block, start=0):
    for column in range(block.shape[1] // LANES):
        for part in range(block.shape[0] // lanes):
            tile = stage[pl.ds(column * LANES * sub + start + part, LANES, stride=sub), :].T
            block[part * lanes : (part + 1) * lanes, column * LANES : (column + 1) * LANES] = tile[:lanes]


def block_to_rows(sub, lanes, block, square, rows, first, start=0, factor=None):
    for column in range(block.shape[1] // LANES):
        for part in range(block.shape[0] // lanes):
            slot = square.at[(column * sub + part) % square.shape[0]]
            slot[:lanes, :] = block[part * lanes : (part + 1) * lanes, column * LANES : (column + 1) * LANES]
            tile = slot[...].T
            if factor is not None:
                tile = tile * factor(column, part)
            rows[pl.ds(first + column * LANES * sub + start + part, LANES, stride=sub), :] = tile


def pack_rows(parts, lanes, send, full, stages, outs):
    start, size = parts
    slots = outs[0].shape[1]
    unroll = chunked(slots, 32)
    for position in range(BLOCKS):
        stage = stages.at[position]

        @pl.loop(0, slots // unroll)
        def _(k):
            first = k * unroll
            listed = send.at[pl.ds((BLOCKS - 1 - position) * slots + first, unroll)]
            for u in range(unroll):
                stage[pl.ds((first + u) * size, size), :] = full[pl.ds(listed[u] + start, size), :]

    for position in range(BLOCKS):
        rows_to_block(size, lanes, stages.at[position], outs[position])


def enter_kernel(sub, lanes, source, spectrum, full, *rest):
    outs, (square, stages, send, done) = rest[:BLOCKS], rest[BLOCKS:]
    pending = listed_in(source, send, done)
    square[...] = jnp.zeros_like(square)
    block_to_rows(sub, lanes, spectrum, square, full, 0)
    pending.wait()
    pack_rows((0, sub), lanes, send, full, stages, outs)


def clear(items):
    rows = items[0].shape[0]
    step = chunked(rows, 64)
    zero = jnp.zeros((step, LANES), jnp.float32)

    @pl.loop(0, rows // step)
    def _(k):
        for item in items:
            item[pl.ds(pl.multiple_of(k * step, step), step), :] = zero


def slope_kernel(sub, shared, source, normals, step_weight, wave, coef, weight, listed_weight, lines, send, done):
    pending = listed_in(source, send, done)
    elements = normals.shape[2]
    parts = 1 if shared else sub
    plane = elements * parts
    lines[...] = jnp.zeros_like(lines)
    for component in range(2):
        for corner in range(2):
            row = component * 2 + corner
            lines[row : row + 1, :] = normals[component, corner : corner + 1, :]

    def spread(column):
        return jnp.broadcast_to(column, (8, LANES))

    @pl.loop(0, elements // LANES)
    def _(k):
        turned = lines[:, pl.ds(pl.multiple_of(k * LANES, LANES), LANES)].T
        for group in range(LANES // 8):
            at = slice(group * 8, group * 8 + 8)
            x0, x1, y0, y1 = (spread(turned[at, j : j + 1]) for j in range(4))
            base = (k * LANES + group * 8) * parts
            for part in range(parts):
                east, north = wave[part : part + 1, :], wave[sub + part : sub + part + 1, :]
                first = x0 * east + y0 * north
                second = x1 * east + y1 * north
                inward = jnp.minimum(first, 0.0) + jnp.minimum(second, 0.0) - jnp.maximum(first + second, 0.0)
                for which, value in enumerate((first, second, 1.0 / inward)):
                    first_row = which * plane + base
                    if parts == 1:
                        coef[pl.ds(pl.multiple_of(first_row, 8), 8), :] = value
                    else:
                        coef[pl.ds(first_row + part, 8, stride=parts), :] = value

    nodes = step_weight.shape[1]
    for block in range(nodes // LANES):
        turned = jnp.broadcast_to(step_weight[0:1, block * LANES : (block + 1) * LANES], (8, LANES)).T
        for group in range(LANES // 8):
            value = spread(turned[group * 8 : group * 8 + 8, 0:1])
            for part in range(sub):
                at = pl.ds((block * LANES + group * 8) * sub + part, 8, stride=sub)
                weight[at, :] = value * wave[2 * sub + part : 2 * sub + part + 1, :]

    pending.wait()
    unroll = chunked(send.shape[0], 32)

    @pl.loop(0, send.shape[0] // unroll)
    def _(k):
        listed = send.at[pl.ds(k * unroll, unroll)]
        for u in range(unroll):
            listed_weight[pl.ds((k * unroll + u) * sub, sub), :] = weight[pl.ds(listed[u], sub), :]


def total(sums, at):
    result = sums[0][at, :]
    for item in sums[1:]:
        result = result + item[at, :]
    return result


def sweep_kernel(sub, inner, groups, lanes, shared, own_rows, source, coef, weight, *rest):
    ghosts, rest = rest[: BLOCKS * len(inner)], rest[BLOCKS * len(inner) + 1 :]
    full, rest = rest[0], rest[1:]
    returned, rest = rest[: BLOCKS * len(groups)], rest[BLOCKS * len(groups) :]
    square, stages, conn, done, sums = rest[0], rest[1], rest[2], rest[3], rest[4:]
    pending = listed_in(source, conn, done)
    clear(sums)
    ghost_rows = (full.shape[0] - own_rows) // BLOCKS
    elements = conn.shape[0] // 3
    parts = 1 if shared else sub
    square[...] = jnp.zeros_like(square)
    for which, (start, _) in enumerate(inner):
        for position in range(BLOCKS):
            block = ghosts[which * BLOCKS + position]
            block_to_rows(sub, lanes, block, square, full, own_rows + position * ghost_rows, start)

    pending.wait()
    share = elements // GROUPS
    unroll = chunked(share, 32)

    @pl.loop(0, share // unroll)
    def _(k):
        listed = [
            [conn.at[pl.ds(corner * elements + group * share + k * unroll, unroll)] for corner in range(3)]
            for group in range(GROUPS)
        ]
        for u in range(unroll):
            for group in range(GROUPS):
                element = group * share + k * unroll + u
                index = [item[u] for item in listed[group]]
                value = [full[pl.ds(row, sub), :] for row in index]
                first, second, inverse = (
                    jnp.broadcast_to(coef[pl.ds((j * elements + element) * parts, parts), :], (sub, LANES))
                    for j in range(3)
                )
                both = first + second
                inflow = jnp.minimum(first, 0.0) * value[0] + jnp.minimum(second, 0.0) * value[1]
                inflow = (inflow - jnp.maximum(both, 0.0) * value[2]) * inverse
                residual = (
                    jnp.maximum(first, 0.0) * (value[0] - inflow),
                    jnp.maximum(second, 0.0) * (value[1] - inflow),
                    jnp.minimum(both, 0.0) * (inflow - value[2]),
                )
                for corner in range(3):
                    item = sums[group * 3 + corner]
                    at = pl.ds(index[corner], sub)
                    item[at, :] = item[at, :] + residual[corner]

    step = chunked(ghost_rows, 128)
    for position in range(BLOCKS):
        stage = stages.at[position]

        @pl.loop(0, ghost_rows // step)
        def _(k):
            at = pl.multiple_of(k * step, step)
            stage[pl.ds(at, step), :] = total(sums, pl.ds(own_rows + position * ghost_rows + at, step))

    for which, (start, _) in enumerate(groups):
        for position in range(BLOCKS):
            rows_to_block(sub, lanes, stages.at[position], returned[which * BLOCKS + position], start)

    own_step = chunked(own_rows, 128)

    @pl.loop(0, own_rows // own_step)
    def _(k):
        at = pl.ds(pl.multiple_of(k * own_step, own_step), own_step)
        full[at, :] = full[at, :] - weight[at, :] * total(sums, at)


def add_returned(sub, parts, lanes, pending, send, listed_weight, incoming, square, stages, full):
    start, size = parts
    slots = incoming[0].shape[1]
    square[...] = jnp.zeros_like(square)
    unroll = chunked(slots, 16)
    for position in range(BLOCKS):
        base = (BLOCKS - 1 - position) * slots * sub + start

        def factor(column, part):
            return listed_weight[pl.ds(base + column * LANES * sub + part, LANES, stride=sub), :]

        block_to_rows(size, lanes, incoming[position], square, stages.at[position], 0, 0, factor)
    pending.wait()
    for position in range(BLOCKS):
        stage = stages.at[position]

        @pl.loop(0, slots // unroll)
        def _(k):
            first = k * unroll
            listed = send.at[pl.ds((BLOCKS - 1 - position) * slots + first, unroll)]
            rows = [pl.ds(listed[u] + start, size) for u in range(unroll)]
            fresh = [full[row, :] - stage[pl.ds((first + u) * size, size), :] for u, row in enumerate(rows)]
            for row, item in zip(rows, fresh):
                full[row, :] = item


def between_kernel(sub, parts, lanes, source, listed_weight, *rest):
    incoming, rest = rest[:BLOCKS], rest[BLOCKS + 1 :]
    full, outs, (square, stages, send, done) = rest[0], rest[1 : 1 + BLOCKS], rest[1 + BLOCKS :]
    pending = listed_in(source, send, done)
    add_returned(sub, parts, lanes, pending, send, listed_weight, incoming, square, stages, full)
    pack_rows(parts, lanes, send, full, stages, outs)


def leave_kernel(sub, parts, lanes, halves, count, source, listed_weight, *rest):
    incoming, rest = rest[:BLOCKS], rest[BLOCKS + 1 :]
    full, outs, (square, stages, send, done) = rest[0], rest[1 : 1 + count], rest[1 + count :]
    pending = listed_in(source, send, done)
    add_returned(sub, parts, lanes, pending, send, listed_weight, incoming, square, stages, full)
    start, size = parts
    place = lax.axis_index("spec")
    for distance in range(count):
        target = lax.rem(place + distance, count)
        for half in range(halves):
            first = (target * halves + half) * LANES * sub + start
            for part in range(size):
                tile = full[pl.ds(first + part, LANES, stride=sub), :].T
                outs[distance][pl.ds(part * lanes * halves + half, lanes, stride=halves), :] = tile[:lanes]


def interact_kernel(per_source, halves, count, starts, partner_source, rate_source, *rest):
    pieces, rest = rest[: count * len(starts)], rest[count * len(starts) :]
    target, energy, kept, added = rest[0], rest[1], rest[2], rest[3:-6]
    out, done, partner, partner_done, rate, rate_done = rest[-6:]
    pending = listed_in(partner_source, partner, partner_done), listed_in(rate_source, rate, rate_done)
    bins = rate.shape[0]
    place = lax.axis_index("spec")
    clear(added)
    for which, start in enumerate(starts):
        for distance in range(count):
            piece = pieces[which * count + distance]
            first = lax.rem(place + count - distance, count) * per_source + start
            if per_source % 8 == 0 and start % 8 == 0:
                first = pl.multiple_of(first, 8)
            energy[pl.ds(first, piece.shape[0]), :] = piece[...]
    for item in pending:
        item.wait()
    share = bins // GROUPS
    unroll = chunked(share, 18)

    @pl.loop(0, share // unroll)
    def _(k):
        for u in range(unroll):
            for group in range(GROUPS):
                index = group * share + k * unroll + u
                up, down = partner[index], partner[bins + index]
                here = pl.ds(index * halves, halves)
                own = energy[here, :]
                upper = energy[pl.ds(up, halves), :]
                lower = energy[pl.ds(down, halves), :]
                term = rate[index] * (
                    own * own * (weight_plus * upper + weight_minus * lower)
                    - 2.0 * weight_both * own * upper * lower
                )
                kept[here, :] = own - 2.0 * term
                for item, row in zip(added[2 * group :], (up, down)):
                    item[pl.ds(row, halves), :] = item[pl.ds(row, halves), :] + term

    copies = done.shape[0]
    share = bins // copies
    step = chunked(share, 144)
    for which in range(copies):

        @pl.loop(which * share // step, (which + 1) * share // step)
        def _(k):
            for half in range(halves):
                at = pl.ds(k * step * halves + half, step, stride=halves)
                result = kept[at, :] + total(added, at)
                out[pl.ds(pl.multiple_of(k * step, step), step), half * LANES : (half + 1) * LANES] = result

        at = pl.ds(which * share, share)
        pltpu.make_async_copy(out.at[at], target.at[at], done.at[which]).start()
    for which in range(copies):
        at = pl.ds(which * share, share)
        pltpu.make_async_copy(out.at[at], target.at[at], done.at[which]).wait()


def shape_of(*dims):
    return jax.ShapeDtypeStruct(dims, jnp.float32)


def cost(flops, moved):
    return pl.CostEstimate(flops=flops, bytes_accessed=moved, transcendentals=0)


def limit(mebibytes):
    return pltpu.CompilerParams(vmem_limit_bytes=mebibytes << 20)


def on_device(
    spectrum, normals, conn, send_nodes, step_weight, group_speed, dia_plus, dia_minus, dia_coeff
):
    row_count, owned = spectrum.shape
    slots = send_nodes.shape[2]
    elements = conn.shape[1]
    bins = dia_plus.shape[0]
    spec_count = lax.axis_size("spec")
    sub = -(-row_count // LANES)
    while row_count % sub:
        sub += 1
    lanes = row_count // sub
    shared = lanes % NDIR == 0
    own_rows = owned * sub
    ghost_rows = slots * sub
    rows = own_rows + BLOCKS * ghost_rows
    halves = owned // (spec_count * LANES)

    nodes = (conn * sub).reshape(-1)
    send = (send_nodes[0] * sub).reshape(-1)

    bin_of = (
        lax.axis_index("spec") * row_count
        + jnp.arange(sub, dtype=jnp.int32)[:, None] * lanes
        + jnp.arange(LANES, dtype=jnp.int32)[None, :]
    )
    angle = (bin_of % NDIR).astype(jnp.float32) * (2.0 * math.pi / NDIR)
    east, north = jnp.cos(angle), jnp.sin(angle)
    select = ((bin_of // NDIR)[:, :, None] == jnp.arange(group_speed.shape[0], dtype=jnp.int32)).astype(jnp.float32)
    speed = jnp.sum(select * group_speed, axis=2)
    wave = jnp.concatenate([east, north, speed])

    def blocks_of(groups):
        return [shape_of(size * lanes, slots) for _, size in groups for _ in range(BLOCKS)]

    whole = ((0, sub),)
    block_shapes = blocks_of(whole)
    full_shape = shape_of(rows, LANES)
    sums = [pltpu.VMEM((rows, LANES), jnp.float32)] * (3 * GROUPS)
    squares = pltpu.VMEM((4, LANES, LANES), jnp.float32)
    stages = pltpu.VMEM((BLOCKS, ghost_rows, LANES), jnp.float32)
    moved = 4 * LANES * own_rows

    full, *outs = pl.pallas_call(
        functools.partial(enter_kernel, sub, lanes),
        out_shape=[full_shape] + block_shapes,
        in_specs=[ANY, VM],
        out_specs=[VM] * (1 + BLOCKS),
        scratch_shapes=[squares, stages] + list_scratch(BLOCKS * slots),
        cost_estimate=cost(0, 2 * moved),
        compiler_params=limit(4),
        name="enter",
    )(send, spectrum)
    pitch = 3 if shared else 3 * sub
    coef, weight, listed_weight = pl.pallas_call(
        functools.partial(slope_kernel, sub, shared),
        out_shape=[shape_of(elements * pitch, LANES), shape_of(own_rows, LANES), shape_of(BLOCKS * ghost_rows, LANES)],
        in_specs=[ANY] + [VM] * 3,
        out_specs=[VM] * 3,
        scratch_shapes=[pltpu.VMEM((LANES, elements), jnp.float32)] + list_scratch(BLOCKS * slots),
        cost_estimate=cost(20 * elements * LANES, 4 * LANES * (elements * pitch + own_rows)),
        compiler_params=limit(4),
        name="slopes",
    )(send, normals, step_weight.reshape(1, owned), wave)

    groups = whole if sub == 1 else ((0, 1), (1, sub - 1))
    inner = whole
    for sweep_index in range(STEPS):
        ghosts = []
        for p, item in enumerate(outs):
            ghosts.append(passed_along(item, "dom", -offset_of(p % BLOCKS)))
        full, *returned = pl.pallas_call(
            functools.partial(sweep_kernel, sub, inner, groups, lanes, shared, own_rows),
            out_shape=[full_shape] + blocks_of(groups),
            in_specs=[ANY] + [VM] * (3 + len(ghosts)),
            out_specs=[VM] * (1 + BLOCKS * len(groups)),
            input_output_aliases={3 + len(ghosts): 0},
            scratch_shapes=[squares, stages] + list_scratch(3 * elements) + sums,
            cost_estimate=cost(elements * 24 * row_count, 4 * LANES * (3 * elements + 4 * rows)),
            compiler_params=limit(20),
            name="sweep",
        )(nodes, coef, weight, *ghosts, full)
        incoming = []
        for p, item in enumerate(returned):
            incoming.append(passed_along(item, "dom", offset_of(p % BLOCKS)))
        if sweep_index < STEPS - 1:
            outs, inner = [], groups
            for which, parts in enumerate(groups):
                full, *more = pl.pallas_call(
                    functools.partial(between_kernel, sub, parts, lanes),
                    out_shape=[full_shape] + blocks_of((parts,)),
                    in_specs=[ANY] + [VM] * (2 + BLOCKS),
                    out_specs=[VM] * (1 + BLOCKS),
                    input_output_aliases={2 + BLOCKS: 0},
                    scratch_shapes=[squares, stages] + list_scratch(BLOCKS * slots),
                    cost_estimate=cost(2 * owned * parts[1] * LANES, 4 * moved * parts[1] // sub),
                    compiler_params=limit(4),
                )(send, listed_weight, *incoming[which * BLOCKS : (which + 1) * BLOCKS], full)
                outs += more

    pieces = []
    for which, (start, size) in enumerate(groups):
        full, *blocks = pl.pallas_call(
            functools.partial(leave_kernel, sub, (start, size), lanes, halves, spec_count),
            out_shape=[full_shape] + [shape_of(size * lanes * halves, LANES)] * spec_count,
            in_specs=[ANY] + [VM] * (2 + BLOCKS),
            out_specs=[VM] * (1 + spec_count),
            input_output_aliases={2 + BLOCKS: 0},
            scratch_shapes=[squares, stages] + list_scratch(BLOCKS * slots),
            cost_estimate=cost(2 * owned * size * LANES, 3 * moved * size // sub),
            compiler_params=limit(4),
        )(send, listed_weight, *incoming[which * BLOCKS : (which + 1) * BLOCKS], full)
        pieces.append(blocks[0])
        for distance in range(1, spec_count):
            pieces.append(passed_along(blocks[distance], "spec", distance))
    return pl.pallas_call(
        functools.partial(interact_kernel, row_count * halves, halves, spec_count, [s * lanes * halves for s, _ in groups]),
        out_shape=shape_of(bins, halves * LANES),
        in_specs=[ANY] * 2 + [VM] * len(pieces),
        out_specs=pl.BlockSpec(memory_space=pl.ANY),
        scratch_shapes=[pltpu.VMEM((bins * halves, LANES), jnp.float32)] * (2 + 2 * GROUPS)
        + [pltpu.VMEM((bins, halves * LANES), jnp.float32), pltpu.SemaphoreType.DMA((chunked(bins // 48, 4),))]
        + list_scratch(2 * bins)
        + list_scratch(bins, jnp.float32),
        cost_estimate=cost(16 * bins * halves * LANES, 8 * bins * halves * LANES),
        compiler_params=limit(12),
        name="interact",
    )(jnp.concatenate([dia_plus, dia_minus]) * halves, dia_coeff, *pieces)


def solution(mesh):
    in_specs = (
        P("spec", "dom"),
        P(None, None, "dom"),
        P(None, "dom"),
        P("dom", None, None),
        P("dom"),
        P(),
        P(),
        P(),
        P(),
    )
    out_specs = P(None, ("dom", "spec"))
    return jax.shard_map(
        on_device, mesh=mesh, in_specs=in_specs, out_specs=out_specs, check_vma=False
    )
```
